256 devices in a mesh: gx: 8 (over x_lo, y), gy: 16 (over z, core), gz: 2 (over x_hi).
Axes of the slice: x: 4 (x_hi: 2, x_lo: 2; x = x_hi * 2 + x_lo), y: 4, z: 8, core: 2. Of those that a mesh axis runs over, the one named last changes fastest.
Arguments:
- velocity: float32 [3, 256, 256, 256], P(None, 'gx', 'gy', 'gz'), may hold values from -6 to 6
- adjoint_seed: float32 [3, 256, 256, 256], P(None, 'gx', 'gy', 'gz'), may hold values from -6 to 6
- susceptibility: float32 [256, 256, 256], P('gx', 'gy', 'gz'), may hold values from 0.5 to 4
- remanence: float32 [256, 256, 256], P('gx', 'gy', 'gz'), may hold values from 0.2 to 1.5
- region_bounds: int32 [2, 3], replicated, may hold values from 0 to 128, as said below
- step_id: int32 [1], replicated, may hold values from 0 to 999
Outputs:
- next_velocity: float32 [3, 256, 256, 256], P(None, 'gx', 'gy', 'gz')
- velocity_adjoint: float32 [3, 256, 256, 256], P(None, 'gx', 'gy', 'gz')
- design_gradient: float32 [256, 256, 256], P('gx', 'gy', 'gz')
The draws below stay inside these ranges and needn't reach their ends.
Inputs may be any that keep to these rules, and one draw needn't show every extreme that they name: Along every dimension the design region is nonempty and lies in the lower half of the box: region_bounds[0, d] < region_bounds[1, d] <= half the cells along d.
All inputs are finite; a program needn't handle non-finite values.
Results may differ from the reference program's by a relative error of at most 0.000096.
Values sent between devices are 32-bit elements; how exact they have to be, the bound alone decides.
A program may use at most 128 MiB of HBM per device.

```python
import math
import jax
import jax.numpy as jnp

NX = 256
NY = 256
NZ = 256


def draw_region_bounds(key, part):
    first_key, second_key = jax.random.split(jax.random.fold_in(key, 11))
    lengths = jnp.array([NX, NY, NZ], dtype=jnp.int32)
    lower = jax.random.randint(first_key, (3,), 0, lengths // 8 + 1)
    upper = jax.random.randint(second_key, (3,), 3 * lengths // 8, lengths // 2 + 1)
    lower = lower.at[0].set(0)
    upper = upper.at[0].set(NX // 2)
    return jnp.stack([lower, upper]).astype(jnp.int32)


def levels(stream_key, extent, pieces, low, high):
    def one(position, shards_of):
        heights = jax.random.uniform(jax.random.fold_in(jax.random.fold_in(stream_key, 6), position), (shards_of,), jnp.float32, low / len(pieces), high / len(pieces))
        return jnp.repeat(jnp.exp(heights), extent[position] // shards_of).reshape((-1,) + (1,) * (len(extent) - position - 1))

    level = one(*pieces[0])
    for cut in pieces[1:]:
        level = level * one(*cut)
    return level


def noise(stream_key, extent, scale, bound, pieces=(), held_as=jnp.bfloat16):
    loudness = levels(stream_key, extent, pieces, -0.22, 0.18) if pieces else 1.0
    values = jax.random.normal(stream_key, extent, jnp.float32) * scale * loudness
    return jnp.minimum(jnp.maximum(values, -bound), bound).astype(held_as)


def setup_inputs(seed: int = 0) -> dict:
    key_list = jax.random.split(jax.random.key(seed), 7)
    velocity = noise(key_list[0], (3, NX, NY, NZ), 1.0, 6.0, ((1, 8), (2, 16), (3, 2)), jnp.float32)
    adjoint_seed = noise(key_list[1], (3, NX, NY, NZ), 1.0, 6.0, ((1, 8), (2, 16), (3, 2)), jnp.float32)
    susceptibility = jnp.clip(jnp.exp(math.log(4.0) - 2.0794415 * jax.random.uniform(key_list[2], (NX, NY, NZ), jnp.float32) ** levels(key_list[2], (NX, NY, NZ), ((0, 8), (1, 16), (2, 2)), -0.2, 0.2)), 0.5, 4.0)
    remanence = jnp.clip(0.2 + 1.3 * jax.random.uniform(key_list[3], (NX, NY, NZ), jnp.float32) ** levels(key_list[3], (NX, NY, NZ), ((0, 8), (1, 16), (2, 2)), -0.2, 0.2), 0.2, 1.5)
    region_bounds = draw_region_bounds(jax.random.fold_in(key_list[6], 71), 0)
    step_id = jax.random.randint(key_list[5], (1,), 0, 1000).astype(jnp.int32)
    return dict(velocity=velocity, adjoint_seed=adjoint_seed, susceptibility=susceptibility, remanence=remanence, region_bounds=region_bounds, step_id=step_id)


time_step = 0.5
viscosity = 0.2
field_period = 24
full_turn = 6.283185307179586


def folded_wave(length):
    cell_index = jnp.arange(length, dtype=jnp.int32)
    folded = jnp.where(cell_index < length // 2, cell_index, cell_index - length)
    return folded, full_turn * folded.astype(jnp.float32) / length


def kernel_set():
    fold_first, wave_first = folded_wave(NX)
    fold_second, wave_second = folded_wave(NY)
    fold_third, wave_third = folded_wave(NZ)
    fold_first, wave_first = fold_first[:, None, None], wave_first[:, None, None]
    fold_second, wave_second = fold_second[None, :, None], wave_second[None, :, None]
    fold_third, wave_third = fold_third[None, None, :], wave_third[None, None, :]
    anchor = (fold_first == 0) & (fold_second == 0) & (fold_third == 0)
    square = wave_first * wave_first + wave_second * wave_second + wave_third * wave_third
    safe_square = jnp.where(anchor, 1.0, square)
    return [jnp.where(anchor, 0.0, -(component_wave * wave_third) / safe_square) for component_wave in (wave_first, wave_second, wave_third)]


def region_mask_of(region_bounds):
    masks = []
    for axis_number, length in enumerate((NX, NY, NZ)):
        positions = jnp.arange(length, dtype=jnp.int32)
        masks.append((positions >= region_bounds[0, axis_number]) & (positions < region_bounds[1, axis_number]))
    joined = masks[0][:, None, None] & masks[1][None, :, None] & masks[2][None, None, :]
    return joined.astype(jnp.float32)


def central_slope(padded, axis_number):
    if axis_number == 0:
        return (padded[..., 2:, 1:-1, 1:-1] - padded[..., :-2, 1:-1, 1:-1]) * 0.5
    if axis_number == 1:
        return (padded[..., 1:-1, 2:, 1:-1] - padded[..., 1:-1, :-2, 1:-1]) * 0.5
    return (padded[..., 1:-1, 1:-1, 2:] - padded[..., 1:-1, 1:-1, :-2]) * 0.5


def laplace(padded):
    beside = padded[..., 2:, 1:-1, 1:-1] + padded[..., :-2, 1:-1, 1:-1]
    beside = beside + padded[..., 1:-1, 2:, 1:-1] + padded[..., 1:-1, :-2, 1:-1]
    beside = beside + padded[..., 1:-1, 1:-1, 2:] + padded[..., 1:-1, 1:-1, :-2]
    return beside - 6.0 * padded[..., 1:-1, 1:-1, 1:-1]


def pad_cells(field):
    widths = [(0, 0)] * (field.ndim - 3) + [(1, 1), (1, 1), (1, 1)]
    return jnp.pad(field, widths)


def reference(velocity, adjoint_seed, susceptibility, remanence, region_bounds, step_id):
    region_mask = region_mask_of(region_bounds)
    magnet = remanence * region_mask
    kernels = kernel_set()
    spectrum = jnp.fft.fftn(magnet)
    demag_field = jnp.stack([jnp.real(jnp.fft.ifftn(kernel * spectrum)) for kernel in kernels])
    phase_angle = full_turn * (step_id[0] % field_period).astype(jnp.float32) / field_period
    applied = jnp.stack([jnp.cos(phase_angle), jnp.sin(phase_angle), jnp.zeros((), jnp.float32)])
    total_field = demag_field + applied[:, None, None, None]
    energy = 0.5 * jnp.sum(total_field * total_field, axis=0)
    padded_energy = pad_cells(energy)
    padded_velocity = pad_cells(velocity)
    padded_seed = pad_cells(adjoint_seed)
    padded_suscept = pad_cells(susceptibility)
    advect = jnp.stack([velocity[0] * central_slope(padded_velocity[comp], 0) + velocity[1] * central_slope(padded_velocity[comp], 1) + velocity[2] * central_slope(padded_velocity[comp], 2) for comp in range(3)])
    pushed = jnp.stack([susceptibility * central_slope(padded_energy, axis_number) for axis_number in range(3)])
    next_velocity = velocity + time_step * (viscosity * laplace(padded_velocity) - advect + pushed)
    flux_terms = padded_suscept[None] * padded_seed
    source = central_slope(flux_terms[0], 0) + central_slope(flux_terms[1], 1) + central_slope(flux_terms[2], 2)
    source = -time_step * source
    field_adjoint = source[None] * total_field
    combined = kernels[0] * jnp.fft.fftn(field_adjoint[0]) + kernels[1] * jnp.fft.fftn(field_adjoint[1]) + kernels[2] * jnp.fft.fftn(field_adjoint[2])
    magnet_adjoint = jnp.real(jnp.fft.ifftn(combined))
    design_gradient = region_mask * magnet_adjoint
    shear_terms = jnp.stack([adjoint_seed[0] * central_slope(padded_velocity[0], comp) + adjoint_seed[1] * central_slope(padded_velocity[1], comp) + adjoint_seed[2] * central_slope(padded_velocity[2], comp) for comp in range(3)])
    carried = jnp.stack([central_slope(padded_velocity[0] * padded_seed[comp], 0) + central_slope(padded_velocity[1] * padded_seed[comp], 1) + central_slope(padded_velocity[2] * padded_seed[comp], 2) for comp in range(3)])
    velocity_adjoint = adjoint_seed + time_step * (viscosity * laplace(padded_seed) - shear_terms + carried)
    return next_velocity, velocity_adjoint, design_gradient
```

```python
import jax
import jax.numpy as jnp
import numpy as np
from jax import lax
from jax.experimental import pallas as pl
from jax.experimental.pallas import tpu as pltpu
from jax.sharding import PartitionSpec as P

time_step = 0.5
viscosity = 0.2
field_period = 24
full_turn = 6.283185307179586

bf16 = jnp.bfloat16
f32 = jnp.float32
MESH = pl.DeviceIdType.MESH


def pieces(matrix):
    matrix = np.asarray(matrix, np.float32)
    high = matrix.astype(jnp.bfloat16)
    low = (matrix - high.astype(np.float32)).astype(jnp.bfloat16)
    return np.concatenate([high, high, low], axis=-1)


def cut(value, axis):
    high = value.astype(bf16)
    low = (value - high.astype(f32)).astype(bf16)
    return jnp.concatenate([high, low, high], axis=axis)


def mul(matrix, value):
    return jnp.dot(matrix, cut(value, 0), preferred_element_type=f32)


def make_tables():
    turn = 2.0 * np.pi / 256
    eye8, eye16 = np.eye(8), np.eye(16)
    k3 = 1 + 8 * np.arange(16)[:, None] + np.arange(8)[None, :]
    z = np.arange(128)
    phase = turn * k3[:, :, None] * z
    forward_z = np.stack([np.cos(phase), -np.sin(phase)], 1).reshape(256, 128)
    weight = np.where(k3 == 128, 1.0, 2.0)[:, :, None] / 256.0**3
    inverse_z = []
    for part in range(2):
        phase = turn * k3[:, :, None] * (z + 128 * part)
        both = np.stack([np.cos(phase) * weight, -np.sin(phase) * weight], 1)
        inverse_z.append(both.reshape(256, 128).T)
    q, t, ka = np.arange(8), np.arange(2), np.arange(16)
    theta = turn * 16 * (2 * q[:, None, None] + t[None, :, None]) * ka
    c, s = np.cos(theta), np.sin(theta)
    turned = np.stack([np.stack([c, s]), np.stack([-s, c])])
    sign = np.stack([np.ones(8), (-1.0) ** (1 + np.arange(8))])
    forward_x = np.einsum("abqtk,gj,ji->takiqgbj", turned, sign, eye8)
    forward_x = forward_x.reshape(2, 256, 256)
    lower = np.einsum("abqtk,ji->akitqbj", turned[:, :, :4], eye8).reshape(256, 128)
    back = np.stack([np.stack([c, -s]), np.stack([s, c])])
    inverse_x = np.einsum("abqtk,ij->tqaibkj", back, eye8).reshape(256, 256)
    lower_back = np.einsum("abqtk,ij->tqaibkj", back[:, :, :4], eye8).reshape(128, 256)
    b = np.arange(16)
    phi = turn * ka[:, None] * b
    twiddle = np.stack([np.cos(phi), np.sin(phi)])[:, :, None, :, None]
    twiddle = np.broadcast_to(twiddle, (2, 16, 8, 16, 16)).reshape(2, 128, 256)
    angle = turn * 16 * b[:, None] * b
    kron = [np.kron(np.cos(angle), eye16), np.kron(np.sin(angle), eye16)]
    k = np.arange(256)
    angle = turn * (k[:, None] * k % 256)
    second = np.stack([np.cos(angle), np.sin(angle)])
    return dict(
        forward_z=pieces(forward_z),
        inverse_z=pieces(np.stack(inverse_z)),
        forward_x=pieces(forward_x),
        lower_x=pieces(lower),
        inverse_x=pieces(inverse_x),
        lower_back=pieces(lower_back),
        twiddle=twiddle.astype(np.float32),
        kron=pieces(np.stack(kron)),
        second=pieces(second),
        second_lower=pieces(second[:, :, :128]),
    )


def rotated(pair, value, direction):
    value = cut(value, 0)
    first = jnp.dot(pair[0], value, preferred_element_type=f32)
    second = jnp.dot(pair[1], value, preferred_element_type=f32)
    real = first[:, :128] - direction * second[:, 128:]
    imag = first[:, 128:] + direction * second[:, :128]
    return real, imag


def depth_waves(block, forward_z):
    return lax.dot_general(
        forward_z, cut(block, 1), (((1,), (1,)), ((), ())), preferred_element_type=f32
    )


def first_forward(mixed, twiddle, kron):
    real, imag = mixed[:128], mixed[128:]
    c, s = twiddle[0], twiddle[1]
    turned = jnp.concatenate([real * c + imag * s, imag * c - real * s], axis=0)
    return rotated(kron, turned.T, -1.0)


def first_inverse(value, twiddle, kron, inverse_x):
    real, imag = rotated(kron, value, 1.0)
    turned = jnp.concatenate([real, imag], axis=1).T
    real, imag = turned[:128], turned[128:]
    c, s = twiddle[0], twiddle[1]
    turned = jnp.concatenate([real * c - imag * s, imag * c + real * s], axis=0)
    return mul(inverse_x, turned)


def signed_wave(index):
    folded = jnp.where(index < 128, index, index - 256)
    return jnp.where(index == 128, 0, folded).astype(f32) * (full_turn / 256)


def factor_of(index, third):
    half = full_turn / 2
    return jnp.where(third == 128, jnp.where(index == 128, half, 0.0), signed_wave(index))


def spectral_factors(place, gy):
    row = lax.broadcasted_iota(jnp.int32, (256, 128), 0)
    lane = lax.broadcasted_iota(jnp.int32, (256, 128), 1)
    third = 1 + 8 * place + lane % 8
    first = lane // 8 + 16 * gy
    third_wave = third.astype(f32) * (full_turn / 256)
    fold = lambda i: jnp.where(i < 128, i, i - 256).astype(f32) * (full_turn / 256)
    first_wave, second_wave = fold(first), fold(row)
    square = first_wave * first_wave + second_wave * second_wave + third_wave * third_wave
    return -third_wave / square, factor_of(row, third)


def mixing_factors(place):
    row = lax.broadcasted_iota(jnp.int32, (256, 128), 0)
    lane = lax.broadcasted_iota(jnp.int32, (256, 128), 1)
    third = 1 + 8 * place + lane % 8
    return factor_of(lane // 8 + 16 * (row // 16), third), third.astype(f32) * (full_turn / 256)


def twice(value):
    return jnp.concatenate([value, value], axis=1)


class Place:
    def __init__(self):
        self.gx, self.gy, self.gz = (lax.axis_index(a) for a in ("gx", "gy", "gz"))
        self.wave = self.gx * 2 + self.gz

    def by_wave(self, wave):
        return (wave // 2, self.gy, wave % 2)

    def by_second(self, second):
        return (self.gx, second, self.gz)

    def greet(self):
        barrier = pltpu.get_barrier_semaphore()

        def signal(step, carry):
            for target in (
                self.by_wave((self.wave + step) % 16),
                self.by_second((self.gy + step) % 16),
            ):
                pl.semaphore_signal(barrier, inc=1, device_id=target, device_id_type=MESH)
            return carry

        lax.fori_loop(1, 16, signal, 0)
        pl.semaphore_wait(barrier, 30)


class Exchange:
    def __init__(self, me, device, src, dst, send_sem, recv_sem, wanted=None):
        self.me, self.device, self.src, self.dst = me, device, src, dst
        self.send_sem, self.recv_sem, self.wanted = send_sem, recv_sem, wanted

    def each(self, act):
        def body(step, carry):
            peer = (self.me + step) % 16
            copy = pltpu.make_async_remote_copy(
                src_ref=self.src(peer),
                dst_ref=self.dst,
                send_sem=self.send_sem(peer),
                recv_sem=self.recv_sem,
                device_id=self.device(peer),
                device_id_type=MESH,
            )
            if self.wanted is None:
                act(copy)
            else:
                pl.when(self.wanted(peer))(lambda: act(copy))
            return carry

        lax.fori_loop(1, 16, body, 0)

    def start(self):
        self.each(lambda copy: copy.start())
        own = pltpu.make_async_copy(self.src(self.me), self.dst, self.recv_sem)
        if self.wanted is None:
            own.start()
        else:
            pl.when(self.wanted(self.me))(lambda: own.start())

    def finish(self):
        self.each(lambda copy: copy.wait_send())


def arrived(count, block, sem, skip=None):
    def wait(step, carry):
        pltpu.make_async_copy(block(step), block(step), sem(step)).wait()
        return carry

    lax.fori_loop(0, count, wait, 0)


def field_kernel(
    magnet_in, bounds, forward_z, lower_x, twiddle, kron, second_lower, second, inverse_x, inverse_z,
    field_out,
    z_out, z_in, k_out, k_in, y_out, y_in, x_out, x_in,
    z_sent, z_got, k_sent, k_got, y_sent, y_got, x_sent, x_got,
):
    at = Place()
    at.greet()
    has_magnet = (at.gx < 4) & (at.gy < 8) & (at.gz == 0)
    has_rows = at.gy < 8

    depths = Exchange(
        at.wave, at.by_wave, lambda p: z_out.at[p], z_in.at[at.gx % 4],
        lambda p: z_sent.at[p], z_got.at[at.gx % 4],
    )
    firsts = Exchange(
        at.gy, at.by_second, lambda p: k_out.at[p], k_in.at[at.gy % 8],
        lambda p: k_sent.at[p], k_got.at[at.gy % 8],
    )
    seconds = [
        Exchange(
            at.gy, at.by_second, lambda p, f=f: y_out.at[f, p], y_in.at[f, at.gy],
            lambda p, f=f: y_sent.at[f, p], y_got.at[f, at.gy],
        )
        for f in range(2)
    ]
    lasts = [
        Exchange(
            at.wave, at.by_wave, lambda p, f=f: x_out.at[f, p // 2], x_in.at[f, at.wave],
            lambda p, f=f: x_sent.at[f, p], x_got.at[f, at.wave],
        )
        for f in range(3)
    ]

    @pl.when(has_magnet)
    def _():
        magnet = magnet_in[...] * region(at, bounds)
        z_out[...] = depth_waves(magnet, forward_z[...]).reshape(16, 16, 512)
        depths.start()

    @pl.when(has_rows)
    def _():
        arrived(4, lambda i: z_in.at[i], lambda i: z_got.at[i])
        block = z_in[...].reshape(64, 512)
        block = jnp.concatenate([block[:, :256], block[:, 256:]], axis=0)
        real, imag = first_forward(mul(lower_x[...], block), twiddle[...], kron[...])
        k_out[...] = jnp.concatenate([real, imag], axis=1).reshape(16, 16, 256)
        firsts.start()

    potential, second_factor = spectral_factors(at.wave, at.gy)
    arrived(8, lambda i: k_in.at[i], lambda i: k_got.at[i])
    real, imag = rotated(second_lower[...], k_in[...].reshape(128, 256), -1.0)
    value = jnp.concatenate([real * potential, imag * potential], axis=1)
    for f in range(2):
        if f == 1:
            value = value * twice(second_factor)
        real, imag = rotated(second[...], value, 1.0)
        y_out[f] = jnp.concatenate([real, imag], axis=1).reshape(16, 16, 256)
        seconds[f].start()

    first_factor, third_factor = mixing_factors(at.wave)

    def send_first(f, value):
        value = first_inverse(value, twiddle[...], kron[...], inverse_x[...])
        x_out[f, :, :, :256] = value[:128].reshape(8, 16, 256)
        x_out[f, :, :, 256:] = value[128:].reshape(8, 16, 256)
        lasts[f].start()

    arrived(16, lambda i: y_in.at[0, i], lambda i: y_got.at[0, i])
    value = y_in[0].reshape(256, 256)
    send_first(0, value * twice(first_factor))
    send_first(2, value * twice(third_factor))
    arrived(16, lambda i: y_in.at[1, i], lambda i: y_got.at[1, i])
    send_first(1, y_in[1].reshape(256, 256))

    for f in (0, 2, 1):
        arrived(16, lambda i, f=f: x_in.at[f, i], lambda i, f=f: x_got.at[f, i])
        field_out[f] = mul(inverse_z[at.gz], x_in[f].reshape(256, 512)).T

    pl.when(has_magnet)(lambda: depths.finish())
    pl.when(has_rows)(lambda: firsts.finish())
    for each in seconds + lasts:
        each.finish()


def region(at, bounds):
    row = lax.broadcasted_iota(jnp.int32, (512, 128), 0)
    third = lax.broadcasted_iota(jnp.int32, (512, 128), 1) + at.gz * 128
    first, second = row // 16 + at.gx * 32, row % 16 + at.gy * 16
    inside = (first >= bounds[0, 0]) & (first < bounds[1, 0])
    inside = inside & (second >= bounds[0, 1]) & (second < bounds[1, 1])
    inside = inside & (third >= bounds[0, 2]) & (third < bounds[1, 2])
    return jnp.where(inside, 1.0, 0.0)


def gradient_kernel(
    adjoint_in, bounds, forward_z, forward_x, twiddle, kron, second, lower_back, inverse_z,
    gradient_out,
    z_out, z_in, k_out, k_in, y_out, y_in, x_out, x_in,
    z_sent, z_got, k_sent, k_got, y_sent, y_got, x_sent, x_got,
):
    at = Place()
    at.greet()
    keeps = (at.gx < 4) & (at.gy < 8) & (at.gz == 0)
    has_rows = at.gy < 8

    depths = [
        Exchange(
            at.wave, at.by_wave, lambda p, f=f: z_out.at[f, p], z_in.at[f, at.wave],
            lambda p, f=f: z_sent.at[f, p], z_got.at[f, at.wave],
        )
        for f in range(3)
    ]
    firsts = [
        Exchange(
            at.gy, at.by_second, lambda p, f=f: k_out.at[f, p], k_in.at[f, at.gy],
            lambda p, f=f: k_sent.at[f, p], k_got.at[f, at.gy],
        )
        for f in range(2)
    ]
    seconds = Exchange(
        at.gy, at.by_second, lambda p: y_out.at[p % 8], y_in.at[at.gy],
        lambda p: y_sent.at[p], y_got.at[at.gy], lambda p: p < 8,
    )
    lasts = Exchange(
        at.wave, at.by_wave, lambda p: x_out.at[p // 2 % 4], x_in.at[at.wave],
        lambda p: x_sent.at[p], x_got.at[at.wave], lambda p: (p < 8) & (p % 2 == 0),
    )

    for f in (1, 0, 2):
        z_out[f] = depth_waves(adjoint_in[f], forward_z[...]).reshape(16, 16, 512)
        depths[f].start()

    def first_of(f):
        arrived(16, lambda i: z_in.at[f, i], lambda i: z_got.at[f, i])
        block = z_in[f].reshape(256, 512)
        mixed = mul(forward_x[0], block[:, :256]) + mul(forward_x[1], block[:, 256:])
        real, imag = first_forward(mixed, twiddle[...], kron[...])
        return jnp.concatenate([real, imag], axis=1)

    first_factor, third_factor = mixing_factors(at.wave)
    k_out[1] = first_of(1).reshape(16, 16, 256)
    firsts[1].start()
    value = first_of(0) * twice(first_factor)
    value = value + first_of(2) * twice(third_factor)
    k_out[0] = value.reshape(16, 16, 256)
    firsts[0].start()

    potential, second_factor = spectral_factors(at.wave, at.gy)

    def second_of(f):
        arrived(16, lambda i: k_in.at[f, i], lambda i: k_got.at[f, i])
        real, imag = rotated(second[...], k_in[f].reshape(256, 256), -1.0)
        return jnp.concatenate([real, imag], axis=1)

    value = second_of(1) * twice(second_factor)
    value = (value + second_of(0)) * twice(potential)
    real, imag = rotated(second[:, :128], value, 1.0)
    y_out[...] = jnp.concatenate([real, imag], axis=1).reshape(8, 16, 256)
    seconds.start()

    @pl.when(has_rows)
    def _():
        arrived(16, lambda i: y_in.at[i], lambda i: y_got.at[i])
        value = y_in[...].reshape(256, 256)
        value = first_inverse(value, twiddle[...], kron[...], lower_back[...])
        x_out[:, :, :256] = value[:64].reshape(4, 16, 256)
        x_out[:, :, 256:] = value[64:].reshape(4, 16, 256)
        lasts.start()

    gradient_out[...] = jnp.zeros((512, 128), f32)

    @pl.when(keeps)
    def _():
        arrived(16, lambda i: x_in.at[i], lambda i: x_got.at[i])
        value = mul(inverse_z[0], x_in[...].reshape(256, 512)).T
        gradient_out[...] = value * region(at, bounds)

    for each in depths + firsts + [seconds]:
        each.finish()
    pl.when(has_rows)(lambda: lasts.finish())


VMEM = pl.BlockSpec(memory_space=pltpu.VMEM)
SMEM = pl.BlockSpec(memory_space=pltpu.SMEM)


def spectral_call(kernel, out, operands, shapes, sems, number):
    return pl.pallas_call(
        kernel,
        out_shape=jax.ShapeDtypeStruct(out, f32),
        in_specs=[SMEM if i == 1 else VMEM for i in range(len(operands))],
        out_specs=VMEM,
        scratch_shapes=[pltpu.VMEM(s, f32) for s in shapes]
        + [pltpu.SemaphoreType.DMA(s) for s in sems],
        compiler_params=pltpu.CompilerParams(
            collective_id=number, has_side_effects=True, vmem_limit_bytes=56 << 20
        ),
    )(*operands)


def demag_field_of(remanence, bounds, tables):
    names = ["forward_z", "lower_x", "twiddle", "kron", "second_lower", "second", "inverse_x", "inverse_z"]
    operands = [remanence.reshape(512, 128), bounds] + [tables[n] for n in names]
    shapes = [(16, 16, 512), (4, 16, 512), (16, 16, 256), (8, 16, 256)]
    shapes += [(2, 16, 16, 256), (2, 16, 16, 256), (3, 8, 16, 512), (3, 16, 16, 512)]
    sems = [(16,), (4,), (16,), (8,), (2, 16), (2, 16), (3, 16), (3, 16)]
    field = spectral_call(field_kernel, (3, 512, 128), operands, shapes, sems, 0)
    return field.reshape(3, 32, 16, 128)


def design_gradient_of(adjoint, bounds, tables):
    names = ["forward_z", "forward_x", "twiddle", "kron", "second", "lower_back", "inverse_z"]
    operands = [adjoint.reshape(3, 512, 128), bounds] + [tables[n] for n in names]
    shapes = [(3, 16, 16, 512), (3, 16, 16, 512), (2, 16, 16, 256), (2, 16, 16, 256)]
    shapes += [(8, 16, 256), (16, 16, 256), (4, 16, 512), (16, 16, 512)]
    sems = [(3, 16), (3, 16), (2, 16), (2, 16), (16,), (16,), (16,), (16,)]
    gradient = spectral_call(gradient_kernel, (512, 128), operands, shapes, sems, 1)
    return gradient.reshape(32, 16, 128)


def padded_2(array, sides, width):
    edges = {}
    for axis, dim in sides:
        peers, length = (lax.axis_size(axis), array.shape[dim])
        up = [(i, (i + 1) % peers) for i in range(peers - 1)]
        last = lax.slice_in_dim(array, length - width, length, axis=dim)
        first = lax.slice_in_dim(array, 0, width, axis=dim)
        edges[dim] = (
            lax.ppermute(last, axis, up),
            lax.ppermute(first, axis, [(b, a) for a, b in up]),
        )
    done = []
    for _, dim in sides:
        low, high = edges[dim]
        around = [(width, width) if d in done else (0, 0) for d in range(array.ndim)]
        array = jnp.concatenate([jnp.pad(low, around), array, jnp.pad(high, around)], axis=dim)
        done.append(dim)
    return array


def padded_3(block, sides, width):
    for axis, dim in sides:
        count = lax.axis_size(axis)
        forward = [(i, i + 1) for i in range(count - 1)]
        backward = [(target, source) for source, target in forward]
        low = lax.ppermute(
            lax.slice_in_dim(block, block.shape[dim] - width, None, axis=dim), axis, forward
        )
        high = lax.ppermute(lax.slice_in_dim(block, 0, width, axis=dim), axis, backward)
        block = jnp.concatenate([low, block, high], axis=dim)
    return block


def central_slope(padded, axis_number):
    if axis_number == 0:
        return (padded[..., 2:, 1:-1, 1:-1] - padded[..., :-2, 1:-1, 1:-1]) * 0.5
    if axis_number == 1:
        return (padded[..., 1:-1, 2:, 1:-1] - padded[..., 1:-1, :-2, 1:-1]) * 0.5
    return (padded[..., 1:-1, 1:-1, 2:] - padded[..., 1:-1, 1:-1, :-2]) * 0.5


def laplace(padded):
    beside = padded[..., 2:, 1:-1, 1:-1] + padded[..., :-2, 1:-1, 1:-1]
    beside = beside + padded[..., 1:-1, 2:, 1:-1] + padded[..., 1:-1, :-2, 1:-1]
    beside = beside + padded[..., 1:-1, 1:-1, 2:] + padded[..., 1:-1, 1:-1, :-2]
    return beside - 6.0 * padded[..., 1:-1, 1:-1, 1:-1]


def on_device(velocity, adjoint_seed, susceptibility, remanence, region_bounds, step_id):
    tables = make_tables()
    stacked = jnp.concatenate([velocity, adjoint_seed, susceptibility[None]], axis=0)
    padded_all = padded_2(stacked, (("gx", 1), ("gy", 2), ("gz", 3)), 1)
    demag_field = demag_field_of(remanence, region_bounds, tables)
    phase_angle = full_turn * (step_id[0] % field_period).astype(jnp.float32) / field_period
    applied = jnp.stack([jnp.cos(phase_angle), jnp.sin(phase_angle), jnp.zeros((), jnp.float32)])
    total_field = demag_field + applied[:, None, None, None]
    energy = 0.5 * jnp.sum(total_field * total_field, axis=0)
    padded_energy = padded_3(energy, (("gx", 0), ("gy", 1), ("gz", 2)), 1)
    padded_velocity = padded_all[0:3]
    padded_seed = padded_all[3:6]
    padded_suscept = padded_all[6]
    advect = jnp.stack(
        [
            velocity[0] * central_slope(padded_velocity[comp], 0)
            + velocity[1] * central_slope(padded_velocity[comp], 1)
            + velocity[2] * central_slope(padded_velocity[comp], 2)
            for comp in range(3)
        ]
    )
    pushed = jnp.stack(
        [susceptibility * central_slope(padded_energy, axis_number) for axis_number in range(3)]
    )
    next_velocity = velocity + time_step * (viscosity * laplace(padded_velocity) - advect + pushed)
    flux_terms = padded_suscept[None] * padded_seed
    source = (
        central_slope(flux_terms[0], 0)
        + central_slope(flux_terms[1], 1)
        + central_slope(flux_terms[2], 2)
    )
    source = -time_step * source
    field_adjoint = source[None] * total_field
    design_gradient = design_gradient_of(field_adjoint, region_bounds, tables)
    shear_terms = jnp.stack(
        [
            adjoint_seed[0] * central_slope(padded_velocity[0], comp)
            + adjoint_seed[1] * central_slope(padded_velocity[1], comp)
            + adjoint_seed[2] * central_slope(padded_velocity[2], comp)
            for comp in range(3)
        ]
    )
    carried = jnp.stack(
        [
            central_slope(padded_velocity[0] * padded_seed[comp], 0)
            + central_slope(padded_velocity[1] * padded_seed[comp], 1)
            + central_slope(padded_velocity[2] * padded_seed[comp], 2)
            for comp in range(3)
        ]
    )
    velocity_adjoint = adjoint_seed + time_step * (
        viscosity * laplace(padded_seed) - shear_terms + carried
    )
    return (next_velocity, velocity_adjoint, design_gradient)


def solution(mesh):
    return jax.shard_map(
        on_device,
        mesh=mesh,
        in_specs=(
            P(None, "gx", "gy", "gz"),
            P(None, "gx", "gy", "gz"),
            P("gx", "gy", "gz"),
            P("gx", "gy", "gz"),
            P(),
            P(),
        ),
        out_specs=(P(None, "gx", "gy", "gz"), P(None, "gx", "gy", "gz"), P("gx", "gy", "gz")),
        check_vma=False,
    )
```

```python
import jax
import jax.numpy as jnp
import numpy as np
from jax import lax
from jax.experimental import pallas as pl
from jax.experimental.pallas import tpu as pltpu
from jax.sharding import PartitionSpec as P

time_step = 0.5
viscosity = 0.2
field_period = 24
full_turn = 6.283185307179586

bf16 = jnp.bfloat16
f32 = jnp.float32
MESH = pl.DeviceIdType.MESH


def pieces(matrix):
    matrix = np.asarray(matrix, np.float32)
    high = matrix.astype(jnp.bfloat16)
    low = (matrix - high.astype(np.float32)).astype(jnp.bfloat16)
    return np.concatenate([high, high, low], axis=-1)


def cut(value, axis):
    high = value.astype(bf16)
    low = (value - high.astype(f32)).astype(bf16)
    return jnp.concatenate([high, low, high], axis=axis)


def mul(matrix, value):
    return jnp.dot(matrix, cut(value, 0), preferred_element_type=f32)


def make_tables():
    turn = 2.0 * np.pi / 256
    eye8, eye16 = np.eye(8), np.eye(16)
    k3 = 1 + 8 * np.arange(16)[:, None] + np.arange(8)[None, :]
    z = np.arange(128)
    phase = turn * k3[:, :, None] * z
    forward_z = np.stack([np.cos(phase), -np.sin(phase)], 1).reshape(256, 128)
    weight = np.where(k3 == 128, 1.0, 2.0)[:, :, None] / 256.0**3
    inverse_z = []
    for part in range(2):
        phase = turn * k3[:, :, None] * (z + 128 * part)
        both = np.stack([np.cos(phase) * weight, -np.sin(phase) * weight], 1)
        inverse_z.append(both.reshape(256, 128).T)
    q, t, ka = np.arange(8), np.arange(2), np.arange(16)
    theta = turn * 16 * (2 * q[:, None, None] + t[None, :, None]) * ka
    c, s = np.cos(theta), np.sin(theta)
    turned = np.stack([np.stack([c, s]), np.stack([-s, c])])
    sign = np.stack([np.ones(8), (-1.0) ** (1 + np.arange(8))])
    forward_x = np.einsum("abqtk,gj,ji->takiqgbj", turned, sign, eye8)
    forward_x = forward_x.reshape(2, 256, 256)
    lower = np.einsum("abqtk,ji->akitqbj", turned[:, :, :4], eye8).reshape(256, 128)
    back = np.stack([np.stack([c, -s]), np.stack([s, c])])
    inverse_x = np.einsum("abqtk,ij->tqaibkj", back, eye8).reshape(256, 256)
    lower_back = np.einsum("abqtk,ij->tqaibkj", back[:, :, :4], eye8).reshape(128, 256)
    b = np.arange(16)
    phi = turn * ka[:, None] * b
    twiddle = np.stack([np.cos(phi), np.sin(phi)])[:, :, None, :, None]
    twiddle = np.broadcast_to(twiddle, (2, 16, 8, 16, 16)).reshape(2, 128, 256)
    angle = turn * 16 * b[:, None] * b
    kron = [np.kron(np.cos(angle), eye16), np.kron(np.sin(angle), eye16)]
    k = np.arange(256)
    angle = turn * (k[:, None] * k % 256)
    second = np.stack([np.cos(angle), np.sin(angle)])
    return dict(
        forward_z=pieces(forward_z),
        inverse_z=pieces(np.stack(inverse_z)),
        forward_x=pieces(forward_x),
        lower_x=pieces(lower),
        inverse_x=pieces(inverse_x),
        lower_back=pieces(lower_back),
        twiddle=twiddle.astype(np.float32),
        kron=pieces(np.stack(kron)),
        second=pieces(second),
        second_lower=pieces(second[:, :, :128]),
    )


def rotated(pair, value, direction):
    value = cut(value, 0)
    first = jnp.dot(pair[0], value, preferred_element_type=f32)
    second = jnp.dot(pair[1], value, preferred_element_type=f32)
    real = first[:, :128] - direction * second[:, 128:]
    imag = first[:, 128:] + direction * second[:, :128]
    return real, imag


def depth_waves(block, forward_z):
    return lax.dot_general(
        forward_z, cut(block, 1), (((1,), (1,)), ((), ())), preferred_element_type=f32
    )


def first_forward(mixed, twiddle, kron):
    real, imag = mixed[:128], mixed[128:]
    c, s = twiddle[0], twiddle[1]
    turned = jnp.concatenate([real * c + imag * s, imag * c - real * s], axis=0)
    return rotated(kron, turned.T, -1.0)


def first_inverse(value, twiddle, kron, inverse_x):
    real, imag = rotated(kron, value, 1.0)
    turned = jnp.concatenate([real, imag], axis=1).T
    real, imag = turned[:128], turned[128:]
    c, s = twiddle[0], twiddle[1]
    turned = jnp.concatenate([real * c - imag * s, imag * c + real * s], axis=0)
    return mul(inverse_x, turned)


def signed_wave(index):
    folded = jnp.where(index < 128, index, index - 256)
    return jnp.where(index == 128, 0, folded).astype(f32) * (full_turn / 256)


def factor_of(index, third):
    half = full_turn / 2
    return jnp.where(third == 128, jnp.where(index == 128, half, 0.0), signed_wave(index))


def spectral_factors(place, gy):
    row = lax.broadcasted_iota(jnp.int32, (256, 128), 0)
    lane = lax.broadcasted_iota(jnp.int32, (256, 128), 1)
    third = 1 + 8 * place + lane % 8
    first = lane // 8 + 16 * gy
    third_wave = third.astype(f32) * (full_turn / 256)
    fold = lambda i: jnp.where(i < 128, i, i - 256).astype(f32) * (full_turn / 256)
    first_wave, second_wave = fold(first), fold(row)
    square = first_wave * first_wave + second_wave * second_wave + third_wave * third_wave
    return -third_wave / square, factor_of(row, third)


def mixing_factors(place):
    row = lax.broadcasted_iota(jnp.int32, (256, 128), 0)
    lane = lax.broadcasted_iota(jnp.int32, (256, 128), 1)
    third = 1 + 8 * place + lane % 8
    return factor_of(lane // 8 + 16 * (row // 16), third), third.astype(f32) * (full_turn / 256)


def twice(value):
    return jnp.concatenate([value, value], axis=1)


class Place:
    def __init__(self):
        self.gx, self.gy, self.gz = (lax.axis_index(a) for a in ("gx", "gy", "gz"))
        self.wave = self.gx * 2 + self.gz

    def by_wave(self, wave):
        return (wave // 2, self.gy, wave % 2)

    def by_second(self, second):
        return (self.gx, second, self.gz)

    def greet(self):
        barrier = pltpu.get_barrier_semaphore()

        def signal(step, carry):
            for target in (
                self.by_wave((self.wave + step) % 16),
                self.by_second((self.gy + step) % 16),
            ):
                pl.semaphore_signal(barrier, inc=1, device_id=target, device_id_type=MESH)
            return carry

        lax.fori_loop(1, 16, signal, 0)
        pl.semaphore_wait(barrier, 30)


class Exchange:
    def __init__(self, me, device, src, dst, send_sem, recv_sem, wanted=None):
        self.me, self.device, self.src, self.dst = me, device, src, dst
        self.send_sem, self.recv_sem, self.wanted = send_sem, recv_sem, wanted

    def each(self, act):
        def body(step, carry):
            peer = (self.me + step) % 16
            copy = pltpu.make_async_remote_copy(
                src_ref=self.src(peer),
                dst_ref=self.dst,
                send_sem=self.send_sem(peer),
                recv_sem=self.recv_sem,
                device_id=self.device(peer),
                device_id_type=MESH,
            )
            if self.wanted is None:
                act(copy)
            else:
                pl.when(self.wanted(peer))(lambda: act(copy))
            return carry

        lax.fori_loop(1, 16, body, 0)

    def start(self):
        self.each(lambda copy: copy.start())
        own = pltpu.make_async_copy(self.src(self.me), self.dst, self.recv_sem)
        if self.wanted is None:
            own.start()
        else:
            pl.when(self.wanted(self.me))(lambda: own.start())

    def finish(self):
        self.each(lambda copy: copy.wait_send())


def arrived(count, block, sem, skip=None):
    def wait(step, carry):
        pltpu.make_async_copy(block(step), block(step), sem(step)).wait()
        return carry

    lax.fori_loop(0, count, wait, 0)


def region(at, bounds):
    row = lax.broadcasted_iota(jnp.int32, (512, 128), 0)
    third = lax.broadcasted_iota(jnp.int32, (512, 128), 1) + at.gz * 128
    first, second = row // 16 + at.gx * 32, row % 16 + at.gy * 16
    inside = (first >= bounds[0, 0]) & (first < bounds[1, 0])
    inside = inside & (second >= bounds[0, 1]) & (second < bounds[1, 1])
    inside = inside & (third >= bounds[0, 2]) & (third < bounds[1, 2])
    return jnp.where(inside, 1.0, 0.0)


class Halo:
    def __init__(self, at, block, second_out, second_in, third_out, third_in, sent, got):
        self.at, self.block = at, block
        self.second_out, self.second_in = second_out, second_in
        self.third_out, self.third_in = third_out, third_in
        gx, gy, gz = at.gx, at.gy, at.gz
        self.copies = []
        for number, (src, dst, there, here, target) in enumerate(
            (
                (block.at[:, 32], block.at[:, 0], gx < 7, gx > 0, ((gx + 1) % 8, gy, gz)),
                (block.at[:, 1], block.at[:, 33], gx > 0, gx < 7, ((gx + 7) % 8, gy, gz)),
                (second_out.at[1], second_in.at[0], gy < 15, gy > 0, (gx, (gy + 1) % 16, gz)),
                (second_out.at[0], second_in.at[1], gy > 0, gy < 15, (gx, (gy + 15) % 16, gz)),
                (third_out, third_in, None, None, (gx, gy, 1 - gz)),
            )
        ):
            copy = pltpu.make_async_remote_copy(
                src_ref=src,
                dst_ref=dst,
                send_sem=sent.at[number],
                recv_sem=got.at[number],
                device_id=target,
                device_id_type=MESH,
            )
            self.copies.append((copy, there, here, dst))

    def start(self):
        block = self.block
        for face, row in ((0, 0), (1, 15)):
            self.second_out[face] = block[:, 1:33, row, :]
        for f in range(block.shape[0]):
            cells = block[f, 1:33].reshape(512, 128).T
            row = jnp.where(self.at.gz == 0, cells[127:128], cells[0:1])
            self.third_out[f : f + 1] = row
        for copy, there, here, dst in self.copies:
            if there is None:
                copy.start()
            else:
                pl.when(there)(lambda copy=copy: copy.start())

    def arrive(self, wide):
        for copy, there, here, dst in self.copies:
            if here is None:
                copy.wait_recv()
            else:
                pl.when(here)(lambda copy=copy: copy.wait_recv())

                @pl.when(jnp.logical_not(here))
                def _(dst=dst):
                    dst[...] = jnp.zeros(dst.shape, f32)

        for f in range(self.block.shape[0]):
            row = jnp.broadcast_to(self.third_in[f : f + 1], (128, 512))
            wide[f] = row.T.reshape(32, 16, 128)

    def finish(self):
        for copy, there, here, dst in self.copies:
            if there is None:
                copy.wait_send()
            else:
                pl.when(there)(lambda copy=copy: copy.wait_send())


def neighbours(at, halo, wide, f, i):
    block = halo.block
    here = block[f, i + 1]
    row = lax.broadcasted_iota(jnp.int32, (16, 128), 0)
    lane = lax.broadcasted_iota(jnp.int32, (16, 128), 1)
    below = halo.second_in[0, f, pl.ds(i, 1)]
    above = halo.second_in[1, f, pl.ds(i, 1)]
    side = wide[f, i]
    second = (
        jnp.where(row == 0, below, pltpu.roll(here, 1, 0)),
        jnp.where(row == 15, above, pltpu.roll(here, 15, 0)),
    )
    third = (
        jnp.where(lane == 0, jnp.where(at.gz == 1, side, 0.0), pltpu.roll(here, 1, 1)),
        jnp.where(lane == 127, jnp.where(at.gz == 0, side, 0.0), pltpu.roll(here, 127, 1)),
    )
    return here, ((block[f, i], block[f, i + 2]), second, third)


def laplace(here, around):
    total = -6.0 * here
    for low, high in around:
        total = total + (low + high)
    return total


def slope(pair):
    return (pair[1] - pair[0]) * 0.5


def cell_rows(at, halo, wide, next_out, adjoint_out, source):
    def body(i, carry):
        cells = [neighbours(at, halo, wide, f, i) for f in range(7)]
        velocity, seed = cells[:3], cells[3:6]
        suscept = cells[6]
        total = 0.0
        for d in range(3):
            pair = [suscept[1][d][e] * seed[d][1][d][e] for e in range(2)]
            total = total + slope(pair)
        source[i] = -time_step * total
        for k in range(3):
            here, around = velocity[k]
            advect = sum(velocity[j][0] * slope(around[j]) for j in range(3))
            next_out[k, i] = here + time_step * (viscosity * laplace(here, around) - advect)
            here, around = seed[k]
            shear = sum(seed[j][0] * slope(velocity[j][1][k]) for j in range(3))
            carried = sum(
                slope([velocity[j][1][j][e] * around[j][e] for e in range(2)]) for j in range(3)
            )
            adjoint_out[k, i] = here + time_step * (
                viscosity * laplace(here, around) - shear + carried
            )
        return carry

    lax.fori_loop(0, 32, body, 0)


def energy_rows(at, halo, wide, suscept, next_out):
    def body(i, carry):
        _, around = neighbours(at, halo, wide, 0, i)
        scaled = time_step * suscept[i]
        for k in range(3):
            next_out[k, i] = next_out[k, i] + scaled * slope(around[k])
        return carry

    lax.fori_loop(0, 32, body, 0)


ORDER = (0, 2, 1)


def kernel(
    velocity, adjoint_seed, suscept, remanence, bounds, step,
    forward_z, inverse_z, forward_x, lower_x, inverse_x, lower_back, twiddle, kron, second,
    second_lower,
    next_out, adjoint_out, gradient_out,
    z_out, z_in, k_out, k_in, y_out, y_in, x_out, x_in,
    zb_out, zb_in, kb_out, kb_in, yb_out, yb_in, xb_out, xb_in,
    cells, cells_y_out, cells_y_in, cells_z_out, cells_z_in, cells_wide,
    energy, energy_y_out, energy_y_in, energy_z_out, energy_z_in, energy_wide, source,
    z_sent, z_got, k_sent, k_got, y_sent, y_got, x_sent, x_got,
    zb_sent, zb_got, kb_sent, kb_got, yb_sent, yb_got, xb_sent, xb_got,
    cells_sent, cells_got, energy_sent, energy_got,
):
    at = Place()
    at.greet()
    in_lower = (at.gx < 4) & (at.gy < 8) & (at.gz == 0)
    has_rows = at.gy < 8

    depths = Exchange(
        at.wave, at.by_wave, lambda p: z_out.at[p], z_in.at[at.gx % 4],
        lambda p: z_sent.at[p], z_got.at[at.gx % 4],
    )
    firsts = Exchange(
        at.gy, at.by_second, lambda p: k_out.at[p], k_in.at[at.gy % 8],
        lambda p: k_sent.at[p], k_got.at[at.gy % 8],
    )
    seconds = [
        Exchange(
            at.gy, at.by_second, lambda p, f=f: y_out.at[f, p], y_in.at[f, at.gy],
            lambda p, f=f: y_sent.at[f, p], y_got.at[f, at.gy],
        )
        for f in range(2)
    ]
    lasts = [
        Exchange(
            at.wave, at.by_wave, lambda p, f=f: x_out.at[f, p // 2], x_in.at[f, at.wave],
            lambda p, f=f: x_sent.at[f, p], x_got.at[f, at.wave],
        )
        for f in range(3)
    ]
    depths_back = [
        Exchange(
            at.wave, at.by_wave, lambda p, f=f: zb_out.at[f, p], zb_in.at[f, at.wave],
            lambda p, f=f: zb_sent.at[f, p], zb_got.at[f, at.wave],
        )
        for f in range(3)
    ]
    firsts_back = [
        Exchange(
            at.gy, at.by_second, lambda p, f=f: kb_out.at[f, p], kb_in.at[f, at.gy],
            lambda p, f=f: kb_sent.at[f, p], kb_got.at[f, at.gy],
        )
        for f in range(2)
    ]
    seconds_back = Exchange(
        at.gy, at.by_second, lambda p: yb_out.at[p % 8], yb_in.at[at.gy],
        lambda p: yb_sent.at[p], yb_got.at[at.gy], lambda p: p < 8,
    )
    lasts_back = Exchange(
        at.wave, at.by_wave, lambda p: xb_out.at[p // 2 % 4], xb_in.at[at.wave],
        lambda p: xb_sent.at[p], xb_got.at[at.wave], lambda p: (p < 8) & (p % 2 == 0),
    )
    cell_halo = Halo(
        at, cells, cells_y_out, cells_y_in, cells_z_out, cells_z_in, cells_sent, cells_got
    )
    energy_halo = Halo(
        at, energy, energy_y_out, energy_y_in, energy_z_out, energy_z_in, energy_sent, energy_got
    )

    @pl.when(in_lower)
    def _():
        magnet = remanence[...].reshape(512, 128) * region(at, bounds)
        z_out[...] = depth_waves(magnet, forward_z[...]).reshape(16, 16, 512)
        depths.start()

    cells[0:3, 1:33] = velocity[...]
    cells[3:6, 1:33] = adjoint_seed[...]
    cells[6, 1:33] = suscept[...]
    cell_halo.start()

    @pl.when(has_rows)
    def _():
        arrived(4, lambda i: z_in.at[i], lambda i: z_got.at[i])
        block = z_in[...].reshape(64, 512)
        block = jnp.concatenate([block[:, :256], block[:, 256:]], axis=0)
        real, imag = first_forward(mul(lower_x[...], block), twiddle[...], kron[...])
        k_out[...] = jnp.concatenate([real, imag], axis=1).reshape(16, 16, 256)
        firsts.start()

    cell_halo.arrive(cells_wide)
    cell_rows(at, cell_halo, cells_wide, next_out, adjoint_out, source)

    potential, second_factor = spectral_factors(at.wave, at.gy)
    arrived(8, lambda i: k_in.at[i], lambda i: k_got.at[i])
    real, imag = rotated(second_lower[...], k_in[...].reshape(128, 256), -1.0)
    value = jnp.concatenate([real * potential, imag * potential], axis=1)
    for f in range(2):
        if f == 1:
            value = value * twice(second_factor)
        real, imag = rotated(second[...], value, 1.0)
        y_out[f] = jnp.concatenate([real, imag], axis=1).reshape(16, 16, 256)
        seconds[f].start()

    first_factor, third_factor = mixing_factors(at.wave)

    def send_first(f, value):
        value = first_inverse(value, twiddle[...], kron[...], inverse_x[...])
        x_out[f, :, :, :256] = value[:128].reshape(8, 16, 256)
        x_out[f, :, :, 256:] = value[128:].reshape(8, 16, 256)
        lasts[f].start()

    arrived(16, lambda i: y_in.at[0, i], lambda i: y_got.at[0, i])
    value = y_in[0].reshape(256, 256)
    send_first(0, value * twice(first_factor))
    send_first(2, value * twice(third_factor))
    arrived(16, lambda i: y_in.at[1, i], lambda i: y_got.at[1, i])
    send_first(1, y_in[1].reshape(256, 256))

    turned = jnp.full((8, 128), step[0] % field_period, jnp.int32).astype(f32)
    turned = full_turn * turned / field_period
    applied = (jnp.cos(turned)[:1], jnp.sin(turned)[:1], None)
    square = jnp.zeros((512, 128), f32)
    weight = source[...].reshape(512, 128)
    for f in ORDER:
        arrived(16, lambda i, f=f: x_in.at[f, i], lambda i, f=f: x_got.at[f, i])
        field = mul(inverse_z[at.gz], x_in[f].reshape(256, 512)).T
        if applied[f] is not None:
            field = field + applied[f]
        square = square + field * field
        zb_out[f] = depth_waves(weight * field, forward_z[...]).reshape(16, 16, 512)
        depths_back[f].start()
    energy[0, 1:33] = (0.5 * square).reshape(32, 16, 128)
    energy_halo.start()

    def first_of(f):
        arrived(16, lambda i: zb_in.at[f, i], lambda i: zb_got.at[f, i])
        block = zb_in[f].reshape(256, 512)
        mixed = mul(forward_x[0], block[:, :256]) + mul(forward_x[1], block[:, 256:])
        real, imag = first_forward(mixed, twiddle[...], kron[...])
        return jnp.concatenate([real, imag], axis=1)

    value = first_of(0) * twice(first_factor)
    value = value + first_of(2) * twice(third_factor)
    kb_out[0] = value.reshape(16, 16, 256)
    firsts_back[0].start()
    kb_out[1] = first_of(1).reshape(16, 16, 256)
    firsts_back[1].start()

    energy_halo.arrive(energy_wide)
    energy_rows(at, energy_halo, energy_wide, suscept, next_out)

    def second_of(f):
        arrived(16, lambda i: kb_in.at[f, i], lambda i: kb_got.at[f, i])
        real, imag = rotated(second[...], kb_in[f].reshape(256, 256), -1.0)
        return jnp.concatenate([real, imag], axis=1)

    value = second_of(0)
    value = (value + second_of(1) * twice(second_factor)) * twice(potential)
    real, imag = rotated(second[:, :128], value, 1.0)
    yb_out[...] = jnp.concatenate([real, imag], axis=1).reshape(8, 16, 256)
    seconds_back.start()

    @pl.when(has_rows)
    def _():
        arrived(16, lambda i: yb_in.at[i], lambda i: yb_got.at[i])
        value = yb_in[...].reshape(256, 256)
        value = first_inverse(value, twiddle[...], kron[...], lower_back[...])
        xb_out[:, :, :256] = value[:64].reshape(4, 16, 256)
        xb_out[:, :, 256:] = value[64:].reshape(4, 16, 256)
        lasts_back.start()

    gradient_out[...] = jnp.zeros((32, 16, 128), f32)

    @pl.when(in_lower)
    def _():
        arrived(16, lambda i: xb_in.at[i], lambda i: xb_got.at[i])
        value = mul(inverse_z[0], xb_in[...].reshape(256, 512)).T
        gradient_out[...] = (value * region(at, bounds)).reshape(32, 16, 128)

    pl.when(in_lower)(lambda: depths.finish())
    pl.when(has_rows)(lambda: firsts.finish())
    for each in seconds + lasts + depths_back + firsts_back + [seconds_back]:
        each.finish()
    pl.when(has_rows)(lambda: lasts_back.finish())
    cell_halo.finish()
    energy_halo.finish()


TABLES = (
    "forward_z", "inverse_z", "forward_x", "lower_x", "inverse_x", "lower_back", "twiddle",
    "kron", "second", "second_lower",
)


def on_device(velocity, adjoint_seed, susceptibility, remanence, region_bounds, step_id):
    tables = make_tables()
    shapes = [(16, 16, 512), (4, 16, 512), (16, 16, 256), (8, 16, 256)]
    shapes += [(2, 16, 16, 256), (2, 16, 16, 256), (3, 8, 16, 512), (3, 16, 16, 512)]
    shapes += [(3, 16, 16, 512), (3, 16, 16, 512), (2, 16, 16, 256), (2, 16, 16, 256)]
    shapes += [(8, 16, 256), (16, 16, 256), (4, 16, 512), (16, 16, 512)]
    for n in (7, 1):
        shapes += [(n, 34, 16, 128), (2, n, 32, 128), (2, n, 32, 128), (8, 512), (8, 512)]
        shapes += [(n, 32, 16, 128)]
    shapes += [(32, 16, 128)]
    sems = [(16,), (4,), (16,), (8,), (2, 16), (2, 16), (3, 16), (3, 16)]
    sems += [(3, 16), (3, 16), (2, 16), (2, 16), (16,), (16,), (16,), (16,)]
    sems += [(5,)] * 4
    vmem = pl.BlockSpec(memory_space=pltpu.VMEM)
    smem = pl.BlockSpec(memory_space=pltpu.SMEM)
    return pl.pallas_call(
        kernel,
        out_shape=(
            jax.ShapeDtypeStruct((3, 32, 16, 128), f32),
            jax.ShapeDtypeStruct((3, 32, 16, 128), f32),
            jax.ShapeDtypeStruct((32, 16, 128), f32),
        ),
        in_specs=[vmem] * 4 + [smem] * 2 + [vmem] * len(TABLES),
        out_specs=(vmem, vmem, vmem),
        scratch_shapes=[pltpu.VMEM(s, f32) for s in shapes]
        + [pltpu.SemaphoreType.DMA(s) for s in sems],
        compiler_params=pltpu.CompilerParams(
            collective_id=0, has_side_effects=True, vmem_limit_bytes=60 << 20
        ),
    )(
        velocity, adjoint_seed, susceptibility, remanence, region_bounds, step_id,
        *[tables[n] for n in TABLES],
    )


def solution(mesh):
    return jax.shard_map(
        on_device,
        mesh=mesh,
        in_specs=(
            P(None, "gx", "gy", "gz"),
            P(None, "gx", "gy", "gz"),
            P("gx", "gy", "gz"),
            P("gx", "gy", "gz"),
            P(),
            P(),
        ),
        out_specs=(P(None, "gx", "gy", "gz"), P(None, "gx", "gy", "gz"), P("gx", "gy", "gz")),
        check_vma=False,
    )
```

```python
import jax
import jax.numpy as jnp
import numpy as np
from jax import lax
from jax.experimental import pallas as pl
from jax.experimental.pallas import tpu as pltpu
from jax.sharding import PartitionSpec as P

time_step = 0.5
viscosity = 0.2
field_period = 24
full_turn = 6.283185307179586

bf16 = jnp.bfloat16
f32 = jnp.float32
MESH = pl.DeviceIdType.MESH


def pieces(matrix):
    matrix = np.asarray(matrix, np.float32)
    high = matrix.astype(jnp.bfloat16)
    low = (matrix - high.astype(np.float32)).astype(jnp.bfloat16)
    return np.stack([high, low])


def cut(value):
    high = value.astype(bf16)
    return high, (value - high.astype(f32)).astype(bf16)


def product(matrix, value, dims=(((1,), (0,)), ((), ()))):
    dot = lambda a, b: lax.dot_general(a, b, dims, preferred_element_type=f32)
    return dot(matrix[0], value[0]) + dot(matrix[0], value[1]) + dot(matrix[1], value[0])


def mul(matrix, value):
    return product(matrix, cut(value))


def make_tables():
    turn = 2.0 * np.pi / 256
    eye8, eye16 = np.eye(8), np.eye(16)
    k3 = 1 + 8 * np.arange(16)[:, None] + np.arange(8)[None, :]
    z = np.arange(128)
    phase = turn * k3[:, :, None] * z
    forward_z = np.stack([np.cos(phase), -np.sin(phase)], 1).reshape(256, 128)
    weight = np.where(k3 == 128, 1.0, 2.0)[:, :, None] / 256.0**3
    inverse_z = []
    for part in range(2):
        phase = turn * k3[:, :, None] * (z + 128 * part)
        both = np.stack([np.cos(phase) * weight, -np.sin(phase) * weight], 1)
        inverse_z.append(both.reshape(256, 128).T)
    q, t, ka = np.arange(8), np.arange(2), np.arange(16)
    theta = turn * 16 * (2 * q[:, None, None] + t[None, :, None]) * ka
    c, s = np.cos(theta), np.sin(theta)
    turned = np.stack([np.stack([c, s]), np.stack([-s, c])])
    sign = np.stack([np.ones(8), (-1.0) ** (1 + np.arange(8))])
    forward_x = np.einsum("abqtk,gj,ji->takiqgbj", turned, sign, eye8)
    forward_x = forward_x.reshape(2, 256, 256)
    lower = np.einsum("abqtk,ji->akitqbj", turned[:, :, :4], eye8).reshape(256, 128)
    back = np.stack([np.stack([c, -s]), np.stack([s, c])])
    inverse_x = np.einsum("abqtk,ij->tqaibkj", back, eye8).reshape(256, 256)
    b = np.arange(16)
    phi = turn * ka[:, None] * b
    twiddle = np.stack([np.cos(phi), np.sin(phi)])[:, :, None, :, None]
    twiddle = np.broadcast_to(twiddle, (2, 16, 8, 16, 16)).reshape(2, 128, 256)
    angle = turn * 16 * b[:, None] * b
    kron = [np.kron(np.cos(angle), eye16), np.kron(np.sin(angle), eye16)]
    k = np.arange(256)
    angle = turn * (k[:, None] * k % 256)
    second = np.stack([np.cos(angle), np.sin(angle)])
    return dict(
        forward_z=pieces(forward_z),
        inverse_z=np.stack([pieces(m) for m in inverse_z]),
        forward_x=np.stack([pieces(m) for m in forward_x]),
        lower_x=pieces(lower),
        inverse_x=pieces(inverse_x),
        twiddle=twiddle.astype(np.float32),
        kron=np.stack([pieces(m) for m in kron]),
        second=np.stack([pieces(m) for m in second]),
    )


def rotated(cosine, sine, value, direction):
    value = cut(value)
    first, second = product(cosine, value), product(sine, value)
    real = first[:, :128] - direction * second[:, 128:]
    imag = first[:, 128:] + direction * second[:, :128]
    return real, imag


def depth_waves(block, forward_z):
    return product(forward_z, cut(block), (((1,), (1,)), ((), ())))


def first_forward(mixed, twiddle, kron):
    real, imag = mixed[:128], mixed[128:]
    c, s = twiddle[0], twiddle[1]
    turned = jnp.concatenate([real * c + imag * s, imag * c - real * s], axis=0)
    return rotated(*kron, turned.T, -1.0)


def first_inverse(value, twiddle, kron, inverse_x):
    real, imag = rotated(*kron, value, 1.0)
    turned = jnp.concatenate([real, imag], axis=1).T
    real, imag = turned[:128], turned[128:]
    c, s = twiddle[0], twiddle[1]
    turned = jnp.concatenate([real * c - imag * s, imag * c + real * s], axis=0)
    return mul(inverse_x, turned)


def signed_wave(index):
    folded = jnp.where(index < 128, index, index - 256)
    return jnp.where(index == 128, 0, folded).astype(f32) * (full_turn / 256)


def factor_of(index, third):
    half = full_turn / 2
    return jnp.where(third == 128, jnp.where(index == 128, half, 0.0), signed_wave(index))


def spectral_factors(place, gy):
    row = lax.broadcasted_iota(jnp.int32, (256, 128), 0)
    lane = lax.broadcasted_iota(jnp.int32, (256, 128), 1)
    third = 1 + 8 * place + lane % 8
    first = lane // 8 + 16 * gy
    third_wave = third.astype(f32) * (full_turn / 256)
    fold = lambda i: jnp.where(i < 128, i, i - 256).astype(f32) * (full_turn / 256)
    first_wave, second_wave = fold(first), fold(row)
    square = first_wave * first_wave + second_wave * second_wave + third_wave * third_wave
    return -third_wave / square, factor_of(row, third)


def mixing_factors(place):
    row = lax.broadcasted_iota(jnp.int32, (256, 128), 0)
    lane = lax.broadcasted_iota(jnp.int32, (256, 128), 1)
    third = 1 + 8 * place + lane % 8
    return factor_of(lane // 8 + 16 * (row // 16), third), third.astype(f32) * (full_turn / 256)


def twice(value):
    return jnp.concatenate([value, value], axis=1)


UNROLL = 5


class Place:
    def __init__(self):
        self.gx, self.gy, self.gz = (lax.axis_index(a) for a in ("gx", "gy", "gz"))
        self.wave = self.gx * 2 + self.gz

    def by_wave(self, wave):
        return (wave // 2, self.gy, wave % 2)

    def by_second(self, second):
        return (self.gx, second, self.gz)

    def announce(self):
        barrier = pltpu.get_barrier_semaphore()

        def signal(step, carry):
            for target in (
                self.by_wave((self.wave + step) % 16),
                self.by_second((self.gy + step) % 16),
            ):
                pl.semaphore_signal(barrier, inc=1, device_id=target, device_id_type=MESH)
            return carry

        lax.fori_loop(1, 16, signal, 0, unroll=UNROLL)

    def meet(self):
        pl.semaphore_wait(pltpu.get_barrier_semaphore(), 30)


class Exchange:
    def __init__(self, me, device, src, dst, send_sem, recv_sem, wanted=None):
        self.me, self.device, self.src, self.dst = me, device, src, dst
        self.send_sem, self.recv_sem, self.wanted = send_sem, recv_sem, wanted

    def each(self, act):
        def body(step, carry):
            peer = (self.me + step) % 16
            if self.wanted is None:
                act(peer)
            else:
                pl.when(self.wanted(peer))(lambda: act(peer))
            return carry

        lax.fori_loop(1, 16, body, 0, unroll=UNROLL)

    def copy(self, peer):
        return pltpu.make_async_remote_copy(
            src_ref=self.src(peer),
            dst_ref=self.dst,
            send_sem=self.send_sem(peer),
            recv_sem=self.recv_sem,
            device_id=self.device(peer),
            device_id_type=MESH,
        )

    def start(self, after=None):
        def act(peer):
            if after is not None:
                after.copy(peer).wait_send()
            self.copy(peer).start()

        own = pltpu.make_async_copy(self.src(self.me), self.dst, self.recv_sem)
        if self.wanted is None:
            own.start()
        else:
            pl.when(self.wanted(self.me))(lambda: own.start())
        self.each(act)

    def finish(self):
        self.each(lambda peer: self.copy(peer).wait_send())


def arrived(buffer, sem):
    pltpu.make_async_copy(buffer, buffer, sem).wait()


def region(at, bounds):
    row = lax.broadcasted_iota(jnp.int32, (512, 128), 0)
    third = lax.broadcasted_iota(jnp.int32, (512, 128), 1) + at.gz * 128
    first, second = row // 16 + at.gx * 32, row % 16 + at.gy * 16
    inside = (first >= bounds[0, 0]) & (first < bounds[1, 0])
    inside = inside & (second >= bounds[0, 1]) & (second < bounds[1, 1])
    inside = inside & (third >= bounds[0, 2]) & (third < bounds[1, 2])
    return jnp.where(inside, 1.0, 0.0)


def parts(ref):
    return ref.at[0], ref.at[1]


def lower(ref, axis):
    if axis == 0:
        return ref[0, :, :128], ref[1, :, :128]
    return ref[0, :, :, :128], ref[1, :, :, :128]


def lower_rows(ref):
    return jnp.concatenate([ref[:, 0:64], ref[:, 128:192]], axis=1)


class Halo:
    def __init__(self, at, block, second_out, second_in, third_out, third_in, sent, got):
        self.at, self.block = at, block
        self.second_out, self.second_in = second_out, second_in
        self.third_out, self.third_in = third_out, third_in
        gx, gy, gz = at.gx, at.gy, at.gz
        self.copies = []
        for number, (src, dst, there, here, target) in enumerate(
            (
                (block.at[:, 32], block.at[:, 0], gx < 7, gx > 0, ((gx + 1) % 8, gy, gz)),
                (block.at[:, 1], block.at[:, 33], gx > 0, gx < 7, ((gx + 7) % 8, gy, gz)),
                (second_out.at[1], second_in.at[0], gy < 15, gy > 0, (gx, (gy + 1) % 16, gz)),
                (second_out.at[0], second_in.at[1], gy > 0, gy < 15, (gx, (gy + 15) % 16, gz)),
                (third_out, third_in, None, None, (gx, gy, 1 - gz)),
            )
        ):
            copy = pltpu.make_async_remote_copy(
                src_ref=src,
                dst_ref=dst,
                send_sem=sent.at[number],
                recv_sem=got.at[number],
                device_id=target,
                device_id_type=MESH,
            )
            self.copies.append((copy, there, here, dst))

    def start(self):
        block = self.block
        for face, row in ((0, 0), (1, 15)):
            self.second_out[face] = block[:, 1:33, row, :]
        for f in range(block.shape[0]):
            cells = block[f, 1:33].reshape(512, 128).T
            row = jnp.where(self.at.gz == 0, cells[127:128], cells[0:1])
            self.third_out[f : f + 1] = row
        for copy, there, here, dst in self.copies:
            if there is None:
                copy.start()
            else:
                pl.when(there)(lambda copy=copy: copy.start())

    def arrive(self, wide):
        for copy, there, here, dst in self.copies:
            if here is None:
                copy.wait_recv()
            else:
                pl.when(here)(lambda copy=copy: copy.wait_recv())

                @pl.when(jnp.logical_not(here))
                def _(dst=dst):
                    dst[...] = jnp.zeros(dst.shape, f32)

        for f in range(self.block.shape[0]):
            row = jnp.broadcast_to(self.third_in[f : f + 1], (128, 512))
            wide[f] = row.T.reshape(32, 16, 128)

    def finish(self):
        for copy, there, here, dst in self.copies:
            if there is None:
                copy.wait_send()
            else:
                pl.when(there)(lambda copy=copy: copy.wait_send())


def neighbours(at, halo, wide, f, i):
    block = halo.block
    here = block[f, i + 1]
    row = lax.broadcasted_iota(jnp.int32, (16, 128), 0)
    lane = lax.broadcasted_iota(jnp.int32, (16, 128), 1)
    below = halo.second_in[0, f, pl.ds(i, 1)]
    above = halo.second_in[1, f, pl.ds(i, 1)]
    side = wide[f, i]
    second = (
        jnp.where(row == 0, below, pltpu.roll(here, 1, 0)),
        jnp.where(row == 15, above, pltpu.roll(here, 15, 0)),
    )
    third = (
        jnp.where(lane == 0, jnp.where(at.gz == 1, side, 0.0), pltpu.roll(here, 1, 1)),
        jnp.where(lane == 127, jnp.where(at.gz == 0, side, 0.0), pltpu.roll(here, 127, 1)),
    )
    return here, ((block[f, i], block[f, i + 2]), second, third)


def laplace(here, around):
    total = -6.0 * here
    for low, high in around:
        total = total + (low + high)
    return total


def slope(pair):
    return (pair[1] - pair[0]) * 0.5


def cell_rows(at, halo, wide, next_out, adjoint_out, source):
    def body(i, carry):
        cells = [neighbours(at, halo, wide, f, i) for f in range(7)]
        velocity, seed = cells[:3], cells[3:6]
        suscept = cells[6]
        total = 0.0
        for d in range(3):
            pair = [suscept[1][d][e] * seed[d][1][d][e] for e in range(2)]
            total = total + slope(pair)
        source[i] = -time_step * total
        for k in range(3):
            here, around = velocity[k]
            advect = sum(velocity[j][0] * slope(around[j]) for j in range(3))
            next_out[k, i] = here + time_step * (viscosity * laplace(here, around) - advect)
            here, around = seed[k]
            shear = sum(seed[j][0] * slope(velocity[j][1][k]) for j in range(3))
            carried = sum(
                slope([velocity[j][1][j][e] * around[j][e] for e in range(2)]) for j in range(3)
            )
            adjoint_out[k, i] = here + time_step * (
                viscosity * laplace(here, around) - shear + carried
            )
        return carry

    lax.fori_loop(0, 32, body, 0)


def energy_rows(at, halo, wide, suscept, next_out):
    def body(i, carry):
        _, around = neighbours(at, halo, wide, 0, i)
        scaled = time_step * suscept[i]
        for k in range(3):
            next_out[k, i] = next_out[k, i] + scaled * slope(around[k])
        return carry

    lax.fori_loop(0, 32, body, 0)


ORDER = (0, 2, 1)


def kernel(
    velocity, adjoint_seed, suscept, remanence, bounds, step,
    forward_z, inverse_z, forward_x, lower_x, inverse_x, twiddle, kron, second,
    next_out, adjoint_out, gradient_out,
    z_out, z_in, k_out, k_in, y_out, y_in, x_out, x_in,
    zb_out, zb_in, kb_out, kb_in, yb_out, yb_in, xb_out, xb_in,
    cells, cells_y_out, cells_y_in, cells_z_out, cells_z_in, cells_wide,
    energy, energy_y_out, energy_y_in, energy_z_out, energy_z_in, energy_wide, source,
    z_sent, z_got, k_sent, k_got, y_sent, y_got, x_sent, x_got,
    zb_sent, zb_got, kb_sent, kb_got, yb_sent, yb_got, xb_sent, xb_got,
    cells_sent, cells_got, energy_sent, energy_got,
):
    at = Place()
    at.announce()
    in_lower = (at.gx < 4) & (at.gy < 8) & (at.gz == 0)
    has_rows = at.gy < 8

    depths = Exchange(
        at.wave, at.by_wave, lambda p: z_out.at[p], z_in.at[at.gx % 4],
        lambda p: z_sent.at[p], z_got,
    )
    firsts = Exchange(
        at.gy, at.by_second, lambda p: k_out.at[p], k_in.at[at.gy % 8],
        lambda p: k_sent.at[p], k_got,
    )
    seconds = [
        Exchange(
            at.gy, at.by_second, lambda p, f=f: y_out.at[f, p], y_in.at[f, at.gy],
            lambda p, f=f: y_sent.at[f, p], y_got.at[f],
        )
        for f in range(2)
    ]
    lasts = [
        Exchange(
            at.wave, at.by_wave, lambda p, f=f: x_out.at[f, p // 2], x_in.at[f, at.wave],
            lambda p, f=f: x_sent.at[f, p], x_got.at[f],
        )
        for f in range(3)
    ]
    depths_back = [
        Exchange(
            at.wave, at.by_wave, lambda p, f=f: zb_out.at[f, p], zb_in.at[f, at.wave],
            lambda p, f=f: zb_sent.at[f, p], zb_got.at[f],
        )
        for f in range(3)
    ]
    firsts_back = [
        Exchange(
            at.gy, at.by_second, lambda p, f=f: kb_out.at[f, p], kb_in.at[f, at.gy],
            lambda p, f=f: kb_sent.at[f, p], kb_got.at[f],
        )
        for f in range(2)
    ]
    seconds_back = Exchange(
        at.gy, at.by_second, lambda p: yb_out.at[p % 8], yb_in.at[at.gy],
        lambda p: yb_sent.at[p], yb_got, lambda p: p < 8,
    )
    lasts_back = Exchange(
        at.wave, at.by_wave, lambda p: xb_out.at[p // 2 % 4], xb_in.at[at.wave],
        lambda p: xb_sent.at[p], xb_got, lambda p: (p < 8) & (p % 2 == 0),
    )
    cell_halo = Halo(
        at, cells, cells_y_out, cells_y_in, cells_z_out, cells_z_in, cells_sent, cells_got
    )
    energy_halo = Halo(
        at, energy, energy_y_out, energy_y_in, energy_z_out, energy_z_in, energy_sent, energy_got
    )

    @pl.when(in_lower)
    def _():
        magnet = remanence[...].reshape(512, 128) * region(at, bounds)
        z_out[...] = depth_waves(magnet, forward_z).reshape(16, 16, 512)

    at.meet()
    pl.when(in_lower)(lambda: depths.start())

    cells[0:3, 1:33] = velocity[...]
    cells[3:6, 1:33] = adjoint_seed[...]
    cells[6, 1:33] = suscept[...]
    cell_halo.start()

    @pl.when(has_rows)
    def _():
        arrived(z_in, z_got)
        block = z_in[...].reshape(64, 512)
        block = jnp.concatenate([block[:, :256], block[:, 256:]], axis=0)
        real, imag = first_forward(mul(lower_x, block), twiddle, parts(kron))
        k_out[...] = jnp.concatenate([real, imag], axis=1).reshape(16, 16, 256)
        firsts.start()

    cell_halo.arrive(cells_wide)
    cell_rows(at, cell_halo, cells_wide, next_out, adjoint_out, source)

    potential, second_factor = spectral_factors(at.wave, at.gy)
    arrived(k_in, k_got)
    real, imag = rotated(*lower(second, 1), k_in[...].reshape(128, 256), -1.0)
    value = jnp.concatenate([real * potential, imag * potential], axis=1)
    for f in range(2):
        if f == 1:
            value = value * twice(second_factor)
        real, imag = rotated(*parts(second), value, 1.0)
        y_out[f] = jnp.concatenate([real, imag], axis=1).reshape(16, 16, 256)
        seconds[f].start(seconds[0] if f == 1 else None)

    first_factor, third_factor = mixing_factors(at.wave)

    def send_first(f, value, after=None):
        value = first_inverse(value, twiddle, parts(kron), inverse_x)
        x_out[f, :, :, :256] = value[:128].reshape(8, 16, 256)
        x_out[f, :, :, 256:] = value[128:].reshape(8, 16, 256)
        lasts[f].start(after)

    arrived(y_in.at[0], y_got.at[0])
    value = y_in[0].reshape(256, 256)
    send_first(0, value * twice(first_factor))
    send_first(2, value * twice(third_factor), lasts[0])
    arrived(y_in.at[1], y_got.at[1])
    send_first(1, y_in[1].reshape(256, 256), lasts[2])

    turned = jnp.full((8, 128), step[0] % field_period, jnp.int32).astype(f32)
    turned = full_turn * turned / field_period
    applied = (jnp.cos(turned)[:1], jnp.sin(turned)[:1], None)
    square = jnp.zeros((512, 128), f32)
    weight = source[...].reshape(512, 128)
    before = None
    for f in ORDER:
        arrived(x_in.at[f], x_got.at[f])
        field = mul(inverse_z.at[at.gz], x_in[f].reshape(256, 512)).T
        if applied[f] is not None:
            field = field + applied[f]
        square = square + field * field
        zb_out[f] = depth_waves(weight * field, forward_z).reshape(16, 16, 512)
        depths_back[f].start(before)
        before = depths_back[f]
    energy[0, 1:33] = (0.5 * square).reshape(32, 16, 128)
    energy_halo.start()

    def first_of(f):
        arrived(zb_in.at[f], zb_got.at[f])
        block = zb_in[f].reshape(256, 512)
        mixed = mul(forward_x.at[0], block[:, :256]) + mul(forward_x.at[1], block[:, 256:])
        real, imag = first_forward(mixed, twiddle, parts(kron))
        return jnp.concatenate([real, imag], axis=1)

    value = first_of(0) * twice(first_factor)
    value = value + first_of(2) * twice(third_factor)
    kb_out[0] = value.reshape(16, 16, 256)
    firsts_back[0].start()
    kb_out[1] = first_of(1).reshape(16, 16, 256)
    firsts_back[1].start(firsts_back[0])

    energy_halo.arrive(energy_wide)
    energy_rows(at, energy_halo, energy_wide, suscept, next_out)
    pl.when(in_lower)(lambda: depths.finish())
    pl.when(has_rows)(lambda: firsts.finish())
    for each in (seconds[1], lasts[1], depths_back[1], cell_halo, energy_halo):
        each.finish()

    def second_of(f):
        arrived(kb_in.at[f], kb_got.at[f])
        real, imag = rotated(*parts(second), kb_in[f].reshape(256, 256), -1.0)
        return jnp.concatenate([real, imag], axis=1)

    value = second_of(0)
    value = (value + second_of(1) * twice(second_factor)) * twice(potential)
    real, imag = rotated(*lower(second, 0), value, 1.0)
    yb_out[...] = jnp.concatenate([real, imag], axis=1).reshape(8, 16, 256)
    seconds_back.start()
    firsts_back[1].finish()
    gradient_out[...] = jnp.zeros((32, 16, 128), f32)

    @pl.when(has_rows)
    def _():
        arrived(yb_in, yb_got)
        value = yb_in[...].reshape(256, 256)
        value = first_inverse(value, twiddle, parts(kron), lower_rows(inverse_x))
        xb_out[:, :, :256] = value[:64].reshape(4, 16, 256)
        xb_out[:, :, 256:] = value[64:].reshape(4, 16, 256)
        lasts_back.start()

    @pl.when(in_lower)
    def _():
        arrived(xb_in, xb_got)
        value = mul(inverse_z.at[0], xb_in[...].reshape(256, 512)).T
        gradient_out[...] = (value * region(at, bounds)).reshape(32, 16, 128)

    seconds_back.finish()
    pl.when(has_rows)(lambda: lasts_back.finish())


TABLES = (
    "forward_z", "inverse_z", "forward_x", "lower_x", "inverse_x", "twiddle",
    "kron", "second",
)


def on_device(velocity, adjoint_seed, susceptibility, remanence, region_bounds, step_id):
    tables = make_tables()
    shapes = [(16, 16, 512), (4, 16, 512), (16, 16, 256), (8, 16, 256)]
    shapes += [(2, 16, 16, 256), (2, 16, 16, 256), (3, 8, 16, 512), (3, 16, 16, 512)]
    shapes += [(3, 16, 16, 512), (3, 16, 16, 512), (2, 16, 16, 256), (2, 16, 16, 256)]
    shapes += [(8, 16, 256), (16, 16, 256), (4, 16, 512), (16, 16, 512)]
    for n in (7, 1):
        shapes += [(n, 34, 16, 128), (2, n, 32, 128), (2, n, 32, 128), (8, 512), (8, 512)]
        shapes += [(n, 32, 16, 128)]
    shapes += [(32, 16, 128)]
    sems = [(16,), (), (16,), (), (2, 16), (2,), (3, 16), (3,)]
    sems += [(3, 16), (3,), (2, 16), (2,), (16,), (), (16,), ()]
    sems += [(5,)] * 4
    vmem = pl.BlockSpec(memory_space=pltpu.VMEM)
    smem = pl.BlockSpec(memory_space=pltpu.SMEM)
    return pl.pallas_call(
        kernel,
        out_shape=(
            jax.ShapeDtypeStruct((3, 32, 16, 128), f32),
            jax.ShapeDtypeStruct((3, 32, 16, 128), f32),
            jax.ShapeDtypeStruct((32, 16, 128), f32),
        ),
        in_specs=[vmem] * 4 + [smem] * 2 + [vmem] * len(TABLES),
        out_specs=(vmem, vmem, vmem),
        scratch_shapes=[pltpu.VMEM(s, f32) for s in shapes]
        + [pltpu.SemaphoreType.DMA(s) for s in sems],
        compiler_params=pltpu.CompilerParams(
            collective_id=0, has_side_effects=True, vmem_limit_bytes=24 << 20
        ),
    )(
        velocity, adjoint_seed, susceptibility, remanence, region_bounds, step_id,
        *[tables[n] for n in TABLES],
    )


def solution(mesh):
    return jax.shard_map(
        on_device,
        mesh=mesh,
        in_specs=(
            P(None, "gx", "gy", "gz"),
            P(None, "gx", "gy", "gz"),
            P("gx", "gy", "gz"),
            P("gx", "gy", "gz"),
            P(),
            P(),
        ),
        out_specs=(P(None, "gx", "gy", "gz"), P(None, "gx", "gy", "gz"), P("gx", "gy", "gz")),
        check_vma=False,
    )
```

```python
import jax
import jax.numpy as jnp
import numpy as np
from jax import lax
from jax.experimental import pallas as pl
from jax.experimental.pallas import tpu as pltpu
from jax.sharding import PartitionSpec as P

time_step = 0.5
viscosity = 0.2
field_period = 24
full_turn = 6.283185307179586

bf16 = jnp.bfloat16
f32 = jnp.float32
MESH = pl.DeviceIdType.MESH


def pieces(matrix):
    matrix = np.asarray(matrix, np.float32)
    high = matrix.astype(jnp.bfloat16)
    low = (matrix - high.astype(np.float32)).astype(jnp.bfloat16)
    return np.stack([high, low])


def cut(value):
    high = value.astype(bf16)
    return high, (value - high.astype(f32)).astype(bf16)


def product(matrix, value, dims=(((1,), (0,)), ((), ()))):
    dot = lambda a, b: lax.dot_general(a, b, dims, preferred_element_type=f32)
    return dot(matrix[0], value[0]) + dot(matrix[0], value[1]) + dot(matrix[1], value[0])


def mul(matrix, value):
    return product(matrix, cut(value))


def make_tables():
    turn = 2.0 * np.pi / 256
    eye8, eye16 = np.eye(8), np.eye(16)
    k3 = 1 + 8 * np.arange(16)[:, None] + np.arange(8)[None, :]
    z = np.arange(128)
    phase = turn * k3[:, :, None] * z
    forward_z = np.stack([np.cos(phase), -np.sin(phase)], 1).reshape(256, 128)
    weight = np.where(k3 == 128, 1.0, 2.0)[:, :, None] / 256.0**3
    inverse_z = []
    for part in range(2):
        phase = turn * k3[:, :, None] * (z + 128 * part)
        both = np.stack([np.cos(phase) * weight, -np.sin(phase) * weight], 1)
        inverse_z.append(both.reshape(256, 128).T)
    q, t, ka = np.arange(8), np.arange(2), np.arange(16)
    theta = turn * 16 * (2 * q[:, None, None] + t[None, :, None]) * ka
    c, s = np.cos(theta), np.sin(theta)
    turned = np.stack([np.stack([c, s]), np.stack([-s, c])])
    sign = np.stack([np.ones(8), (-1.0) ** (1 + np.arange(8))])
    forward_x = np.einsum("abqtk,gj,ji->takiqgbj", turned, sign, eye8)
    forward_x = forward_x.reshape(2, 256, 256)
    lower = np.einsum("abqtk,ji->akitqbj", turned[:, :, :4], eye8).reshape(256, 128)
    back = np.stack([np.stack([c, -s]), np.stack([s, c])])
    inverse_x = np.einsum("abqtk,ij->tqaibkj", back, eye8).reshape(256, 256)
    b = np.arange(16)
    phi = turn * ka[:, None] * b
    twiddle = np.stack([np.cos(phi), np.sin(phi)])[:, :, None, :, None]
    twiddle = np.broadcast_to(twiddle, (2, 16, 8, 16, 16)).reshape(2, 128, 256)
    angle = turn * 16 * b[:, None] * b
    kron = [np.kron(np.cos(angle), eye16), np.kron(np.sin(angle), eye16)]
    k = np.arange(256)
    angle = turn * (k[:, None] * k % 256)
    second = np.stack([np.cos(angle), np.sin(angle)])
    return dict(
        forward_z=pieces(forward_z),
        inverse_z=np.stack([pieces(m) for m in inverse_z]),
        forward_x=np.stack([pieces(m) for m in forward_x]),
        lower_x=pieces(lower),
        inverse_x=pieces(inverse_x),
        twiddle=twiddle.astype(np.float32),
        kron=np.stack([pieces(m) for m in kron]),
        second=np.stack([pieces(m) for m in second]),
    )


def rotated(cosine, sine, value, direction):
    value = cut(value)
    first, second = product(cosine, value), product(sine, value)
    real = first[:, :128] - direction * second[:, 128:]
    imag = first[:, 128:] + direction * second[:, :128]
    return real, imag


def depth_waves(block, forward_z):
    return product(forward_z, cut(block), (((1,), (1,)), ((), ())))


def first_forward(mixed, twiddle, kron):
    real, imag = mixed[:128], mixed[128:]
    c, s = twiddle[0], twiddle[1]
    turned = jnp.concatenate([real * c + imag * s, imag * c - real * s], axis=0)
    return rotated(*kron, turned.T, -1.0)


def first_inverse(value, twiddle, kron, inverse_x):
    real, imag = rotated(*kron, value, 1.0)
    turned = jnp.concatenate([real, imag], axis=1).T
    real, imag = turned[:128], turned[128:]
    c, s = twiddle[0], twiddle[1]
    turned = jnp.concatenate([real * c - imag * s, imag * c + real * s], axis=0)
    return mul(inverse_x, turned)


def signed_wave(index):
    folded = jnp.where(index < 128, index, index - 256)
    return jnp.where(index == 128, 0, folded).astype(f32) * (full_turn / 256)


def factor_of(index, third):
    half = full_turn / 2
    return jnp.where(third == 128, jnp.where(index == 128, half, 0.0), signed_wave(index))


def spectral_factors(place, gy):
    row = lax.broadcasted_iota(jnp.int32, (256, 128), 0)
    lane = lax.broadcasted_iota(jnp.int32, (256, 128), 1)
    third = 1 + 8 * place + lane % 8
    first = lane // 8 + 16 * gy
    third_wave = third.astype(f32) * (full_turn / 256)
    fold = lambda i: jnp.where(i < 128, i, i - 256).astype(f32) * (full_turn / 256)
    first_wave, second_wave = fold(first), fold(row)
    square = first_wave * first_wave + second_wave * second_wave + third_wave * third_wave
    return -third_wave / square, factor_of(row, third)


def mixing_factors(place):
    row = lax.broadcasted_iota(jnp.int32, (256, 128), 0)
    lane = lax.broadcasted_iota(jnp.int32, (256, 128), 1)
    third = 1 + 8 * place + lane % 8
    return factor_of(lane // 8 + 16 * (row // 16), third), third.astype(f32) * (full_turn / 256)


def twice(value):
    return jnp.concatenate([value, value], axis=1)


UNROLL = 5


class Place:
    def __init__(self):
        self.gx, self.gy, self.gz = (lax.axis_index(a) for a in ("gx", "gy", "gz"))
        self.wave = self.gx * 2 + self.gz

    def by_wave(self, wave):
        return (wave // 2, self.gy, wave % 2)

    def by_second(self, second):
        return (self.gx, second, self.gz)

    def announce(self):
        barrier = pltpu.get_barrier_semaphore()

        def signal(step, carry):
            for target in (
                self.by_wave((self.wave + step) % 16),
                self.by_second((self.gy + step) % 16),
            ):
                pl.semaphore_signal(barrier, inc=1, device_id=target, device_id_type=MESH)
            return carry

        lax.fori_loop(1, 16, signal, 0, unroll=UNROLL)

    def meet(self):
        pl.semaphore_wait(pltpu.get_barrier_semaphore(), 30)


class Exchange:
    def __init__(self, me, device, src, dst, send_sem, recv_sem, wanted=None):
        self.me, self.device, self.src, self.dst = me, device, src, dst
        self.send_sem, self.recv_sem, self.wanted = send_sem, recv_sem, wanted

    def each(self, act):
        def body(step, carry):
            peer = (self.me + step) % 16
            if self.wanted is None:
                act(peer)
            else:
                pl.when(self.wanted(peer))(lambda: act(peer))
            return carry

        lax.fori_loop(1, 16, body, 0, unroll=UNROLL)

    def copy(self, peer):
        return pltpu.make_async_remote_copy(
            src_ref=self.src(peer),
            dst_ref=self.dst,
            send_sem=self.send_sem(peer),
            recv_sem=self.recv_sem,
            device_id=self.device(peer),
            device_id_type=MESH,
        )

    def start(self, after=None):
        def act(peer):
            if after is not None:
                after.copy(peer).wait_send()
            self.copy(peer).start()

        own = pltpu.make_async_copy(self.src(self.me), self.dst, self.recv_sem)
        if self.wanted is None:
            own.start()
        else:
            pl.when(self.wanted(self.me))(lambda: own.start())
        self.each(act)

    def finish(self):
        self.each(lambda peer: self.copy(peer).wait_send())


def arrived(buffer, sem):
    pltpu.make_async_copy(buffer, buffer, sem).wait()


def region(at, bounds):
    row = lax.broadcasted_iota(jnp.int32, (512, 128), 0)
    third = lax.broadcasted_iota(jnp.int32, (512, 128), 1) + at.gz * 128
    first, second = row // 16 + at.gx * 32, row % 16 + at.gy * 16
    inside = (first >= bounds[0, 0]) & (first < bounds[1, 0])
    inside = inside & (second >= bounds[0, 1]) & (second < bounds[1, 1])
    inside = inside & (third >= bounds[0, 2]) & (third < bounds[1, 2])
    return jnp.where(inside, 1.0, 0.0)


def parts(ref):
    return ref.at[0], ref.at[1]


def lower(ref, axis):
    if axis == 0:
        return ref[0, :, :128], ref[1, :, :128]
    return ref[0, :, :, :128], ref[1, :, :, :128]


def lower_rows(ref):
    return jnp.concatenate([ref[:, 0:64], ref[:, 128:192]], axis=1)


class Halo:
    def __init__(self, at, block, second_out, second_in, third_out, third_in, sent, got):
        self.at, self.block = at, block
        self.second_out, self.second_in = second_out, second_in
        self.third_out, self.third_in = third_out, third_in
        gx, gy, gz = at.gx, at.gy, at.gz
        self.copies = []
        for number, (src, dst, there, here, target) in enumerate(
            (
                (block.at[:, 32], block.at[:, 0], gx < 7, gx > 0, ((gx + 1) % 8, gy, gz)),
                (block.at[:, 1], block.at[:, 33], gx > 0, gx < 7, ((gx + 7) % 8, gy, gz)),
                (second_out.at[1], second_in.at[0], gy < 15, gy > 0, (gx, (gy + 1) % 16, gz)),
                (second_out.at[0], second_in.at[1], gy > 0, gy < 15, (gx, (gy + 15) % 16, gz)),
                (third_out, third_in, None, None, (gx, gy, 1 - gz)),
            )
        ):
            copy = pltpu.make_async_remote_copy(
                src_ref=src,
                dst_ref=dst,
                send_sem=sent.at[number],
                recv_sem=got.at[number],
                device_id=target,
                device_id_type=MESH,
            )
            self.copies.append((copy, there, here, dst))

    def start(self):
        block = self.block
        for face, row in ((0, 0), (1, 15)):
            self.second_out[face] = block[:, 1:33, row, :]
        for f in range(block.shape[0]):
            cells = block[f, 1:33].reshape(512, 128).T
            row = jnp.where(self.at.gz == 0, cells[127:128], cells[0:1])
            self.third_out[f : f + 1] = row
        for copy, there, here, dst in self.copies:
            if there is None:
                copy.start()
            else:
                pl.when(there)(lambda copy=copy: copy.start())

    def arrive(self, wide):
        for copy, there, here, dst in self.copies:
            if here is None:
                copy.wait_recv()
            else:
                pl.when(here)(lambda copy=copy: copy.wait_recv())

                @pl.when(jnp.logical_not(here))
                def _(dst=dst):
                    dst[...] = jnp.zeros(dst.shape, f32)

        for f in range(self.block.shape[0]):
            row = jnp.broadcast_to(self.third_in[f : f + 1], (128, 512))
            wide[f] = row.T.reshape(32, 16, 128)

    def finish(self):
        for copy, there, here, dst in self.copies:
            if there is None:
                copy.wait_send()
            else:
                pl.when(there)(lambda copy=copy: copy.wait_send())


def neighbours(at, halo, wide, f, i):
    block = halo.block
    here = block[f, i + 1]
    row = lax.broadcasted_iota(jnp.int32, (16, 128), 0)
    lane = lax.broadcasted_iota(jnp.int32, (16, 128), 1)
    below = halo.second_in[0, f, pl.ds(i, 1)]
    above = halo.second_in[1, f, pl.ds(i, 1)]
    side = wide[f, i]
    second = (
        jnp.where(row == 0, below, pltpu.roll(here, 1, 0)),
        jnp.where(row == 15, above, pltpu.roll(here, 15, 0)),
    )
    third = (
        jnp.where(lane == 0, jnp.where(at.gz == 1, side, 0.0), pltpu.roll(here, 1, 1)),
        jnp.where(lane == 127, jnp.where(at.gz == 0, side, 0.0), pltpu.roll(here, 127, 1)),
    )
    return here, ((block[f, i], block[f, i + 2]), second, third)


def laplace(here, around):
    total = -6.0 * here
    for low, high in around:
        total = total + (low + high)
    return total


def slope(pair):
    return (pair[1] - pair[0]) * 0.5


def cell_rows(at, halo, wide, next_out, adjoint_out, source):
    def body(i, carry):
        cells = [neighbours(at, halo, wide, f, i) for f in range(7)]
        velocity, seed = cells[:3], cells[3:6]
        suscept = cells[6]
        total = 0.0
        for d in range(3):
            pair = [suscept[1][d][e] * seed[d][1][d][e] for e in range(2)]
            total = total + slope(pair)
        source[i] = -time_step * total
        for k in range(3):
            here, around = velocity[k]
            advect = sum(velocity[j][0] * slope(around[j]) for j in range(3))
            next_out[k, i] = here + time_step * (viscosity * laplace(here, around) - advect)
            here, around = seed[k]
            shear = sum(seed[j][0] * slope(velocity[j][1][k]) for j in range(3))
            carried = sum(
                slope([velocity[j][1][j][e] * around[j][e] for e in range(2)]) for j in range(3)
            )
            adjoint_out[k, i] = here + time_step * (
                viscosity * laplace(here, around) - shear + carried
            )
        return carry

    lax.fori_loop(0, 32, body, 0)


def energy_rows(at, halo, wide, cells, next_out):
    def body(i, carry):
        _, around = neighbours(at, halo, wide, 0, i)
        scaled = time_step * cells[6, i + 1]
        for k in range(3):
            next_out[k, i] = next_out[k, i] + scaled * slope(around[k])
        return carry

    lax.fori_loop(0, 32, body, 0)


ORDER = (0, 2, 1)


def kernel(
    velocity, adjoint_seed, suscept, remanence_in,
    forward_z_in, inverse_z_in, forward_x_in, lower_x_in, inverse_x_in, twiddle_in, kron_in,
    second_in, bounds, step,
    next_out, adjoint_out, gradient_out,
    z_out, z_in, k_out, k_in, y_out, y_in, x_out, x_in,
    zb_out, zb_in, kb_out, kb_in, yb_out, yb_in, xb_out, xb_in,
    cells, cells_y_out, cells_y_in, cells_z_out, cells_z_in, cells_wide,
    energy, energy_y_out, energy_y_in, energy_z_out, energy_z_in, energy_wide, source,
    z_sent, z_got, k_sent, k_got, y_sent, y_got, x_sent, x_got,
    zb_sent, zb_got, kb_sent, kb_got, yb_sent, yb_got, xb_sent, xb_got,
    cells_sent, cells_got, energy_sent, energy_got,
    remanence, forward_z, inverse_z, forward_x, lower_x, inverse_x, twiddle, kron, second, loaded,
):
    at = Place()
    at.announce()
    loads = {}
    for number, (name, src, dst) in enumerate(
        (
            ("remanence", remanence_in, remanence),
            ("forward_z", forward_z_in, forward_z),
            ("velocity", velocity, cells.at[0:3, 1:33]),
            ("seed", adjoint_seed, cells.at[3:6, 1:33]),
            ("suscept", suscept, cells.at[6, 1:33]),
            ("lower_x", lower_x_in, lower_x),
            ("twiddle", twiddle_in, twiddle),
            ("kron", kron_in, kron),
            ("second", second_in, second),
            ("inverse_x", inverse_x_in, inverse_x),
            ("inverse_z", inverse_z_in, inverse_z),
            ("forward_x", forward_x_in, forward_x),
        )
    ):
        loads[name] = pltpu.make_async_copy(src, dst, loaded.at[number])
        loads[name].start()
    in_lower = (at.gx < 4) & (at.gy < 8) & (at.gz == 0)
    has_rows = at.gy < 8

    depths = Exchange(
        at.wave, at.by_wave, lambda p: z_out.at[p], z_in.at[at.gx % 4],
        lambda p: z_sent.at[p], z_got,
    )
    firsts = Exchange(
        at.gy, at.by_second, lambda p: k_out.at[p], k_in.at[at.gy % 8],
        lambda p: k_sent.at[p], k_got,
    )
    seconds = [
        Exchange(
            at.gy, at.by_second, lambda p, f=f: y_out.at[f, p], y_in.at[f, at.gy],
            lambda p, f=f: y_sent.at[f, p], y_got.at[f],
        )
        for f in range(2)
    ]
    lasts = [
        Exchange(
            at.wave, at.by_wave, lambda p, f=f: x_out.at[f, p // 2], x_in.at[f, at.wave],
            lambda p, f=f: x_sent.at[f, p], x_got.at[f],
        )
        for f in range(3)
    ]
    depths_back = [
        Exchange(
            at.wave, at.by_wave, lambda p, f=f: zb_out.at[f, p], zb_in.at[f, at.wave],
            lambda p, f=f: zb_sent.at[f, p], zb_got.at[f],
        )
        for f in range(3)
    ]
    firsts_back = [
        Exchange(
            at.gy, at.by_second, lambda p, f=f: kb_out.at[f, p], kb_in.at[f, at.gy],
            lambda p, f=f: kb_sent.at[f, p], kb_got.at[f],
        )
        for f in range(2)
    ]
    seconds_back = Exchange(
        at.gy, at.by_second, lambda p: yb_out.at[p % 8], yb_in.at[at.gy],
        lambda p: yb_sent.at[p], yb_got, lambda p: p < 8,
    )
    lasts_back = Exchange(
        at.wave, at.by_wave, lambda p: xb_out.at[p // 2 % 4], xb_in.at[at.wave],
        lambda p: xb_sent.at[p], xb_got, lambda p: (p < 8) & (p % 2 == 0),
    )
    cell_halo = Halo(
        at, cells, cells_y_out, cells_y_in, cells_z_out, cells_z_in, cells_sent, cells_got
    )
    energy_halo = Halo(
        at, energy, energy_y_out, energy_y_in, energy_z_out, energy_z_in, energy_sent, energy_got
    )

    loads["remanence"].wait()
    loads["forward_z"].wait()
    @pl.when(in_lower)
    def _():
        magnet = remanence[...].reshape(512, 128) * region(at, bounds)
        z_out[...] = depth_waves(magnet, forward_z).reshape(16, 16, 512)

    at.meet()
    pl.when(in_lower)(lambda: depths.start())

    for name in ("velocity", "seed", "suscept"):
        loads[name].wait()
    cell_halo.start()

    loads["lower_x"].wait()
    loads["twiddle"].wait()
    loads["kron"].wait()
    @pl.when(has_rows)
    def _():
        arrived(z_in, z_got)
        block = z_in[...].reshape(64, 512)
        block = jnp.concatenate([block[:, :256], block[:, 256:]], axis=0)
        real, imag = first_forward(mul(lower_x, block), twiddle, parts(kron))
        k_out[...] = jnp.concatenate([real, imag], axis=1).reshape(16, 16, 256)
        firsts.start()

    cell_halo.arrive(cells_wide)
    cell_rows(at, cell_halo, cells_wide, next_out, adjoint_out, source)

    loads["second"].wait()
    potential, second_factor = spectral_factors(at.wave, at.gy)
    arrived(k_in, k_got)
    real, imag = rotated(*lower(second, 1), k_in[...].reshape(128, 256), -1.0)
    value = jnp.concatenate([real * potential, imag * potential], axis=1)
    for f in range(2):
        if f == 1:
            value = value * twice(second_factor)
        real, imag = rotated(*parts(second), value, 1.0)
        y_out[f] = jnp.concatenate([real, imag], axis=1).reshape(16, 16, 256)
        seconds[f].start(seconds[0] if f == 1 else None)

    loads["inverse_x"].wait()
    first_factor, third_factor = mixing_factors(at.wave)

    def send_first(f, value, after=None):
        value = first_inverse(value, twiddle, parts(kron), inverse_x)
        x_out[f, :, :, :256] = value[:128].reshape(8, 16, 256)
        x_out[f, :, :, 256:] = value[128:].reshape(8, 16, 256)
        lasts[f].start(after)

    arrived(y_in.at[0], y_got.at[0])
    value = y_in[0].reshape(256, 256)
    send_first(0, value * twice(first_factor))
    send_first(2, value * twice(third_factor), lasts[0])
    arrived(y_in.at[1], y_got.at[1])
    send_first(1, y_in[1].reshape(256, 256), lasts[2])

    loads["inverse_z"].wait()
    turned = jnp.full((8, 128), step[0] % field_period, jnp.int32).astype(f32)
    turned = full_turn * turned / field_period
    applied = (jnp.cos(turned)[:1], jnp.sin(turned)[:1], None)
    square = jnp.zeros((512, 128), f32)
    weight = source[...].reshape(512, 128)
    before = None
    for f in ORDER:
        arrived(x_in.at[f], x_got.at[f])
        field = mul(inverse_z.at[at.gz], x_in[f].reshape(256, 512)).T
        if applied[f] is not None:
            field = field + applied[f]
        square = square + field * field
        zb_out[f] = depth_waves(weight * field, forward_z).reshape(16, 16, 512)
        depths_back[f].start(before)
        before = depths_back[f]
    energy[0, 1:33] = (0.5 * square).reshape(32, 16, 128)
    energy_halo.start()

    loads["forward_x"].wait()
    def first_of(f):
        arrived(zb_in.at[f], zb_got.at[f])
        block = zb_in[f].reshape(256, 512)
        mixed = mul(forward_x.at[0], block[:, :256]) + mul(forward_x.at[1], block[:, 256:])
        real, imag = first_forward(mixed, twiddle, parts(kron))
        return jnp.concatenate([real, imag], axis=1)

    value = first_of(0) * twice(first_factor)
    value = value + first_of(2) * twice(third_factor)
    kb_out[0] = value.reshape(16, 16, 256)
    firsts_back[0].start()
    kb_out[1] = first_of(1).reshape(16, 16, 256)
    firsts_back[1].start(firsts_back[0])

    energy_halo.arrive(energy_wide)
    energy_rows(at, energy_halo, energy_wide, cells, next_out)
    pl.when(in_lower)(lambda: depths.finish())
    pl.when(has_rows)(lambda: firsts.finish())
    for each in (seconds[1], lasts[1], depths_back[1], cell_halo, energy_halo):
        each.finish()

    def second_of(f):
        arrived(kb_in.at[f], kb_got.at[f])
        real, imag = rotated(*parts(second), kb_in[f].reshape(256, 256), -1.0)
        return jnp.concatenate([real, imag], axis=1)

    value = second_of(0)
    value = (value + second_of(1) * twice(second_factor)) * twice(potential)
    real, imag = rotated(*lower(second, 0), value, 1.0)
    yb_out[...] = jnp.concatenate([real, imag], axis=1).reshape(8, 16, 256)
    seconds_back.start()
    firsts_back[1].finish()
    gradient_out[...] = jnp.zeros((32, 16, 128), f32)

    @pl.when(has_rows)
    def _():
        arrived(yb_in, yb_got)
        value = yb_in[...].reshape(256, 256)
        value = first_inverse(value, twiddle, parts(kron), lower_rows(inverse_x))
        xb_out[:, :, :256] = value[:64].reshape(4, 16, 256)
        xb_out[:, :, 256:] = value[64:].reshape(4, 16, 256)
        lasts_back.start()

    @pl.when(in_lower)
    def _():
        arrived(xb_in, xb_got)
        value = mul(inverse_z.at[0], xb_in[...].reshape(256, 512)).T
        gradient_out[...] = (value * region(at, bounds)).reshape(32, 16, 128)

    seconds_back.finish()
    pl.when(has_rows)(lambda: lasts_back.finish())


VMEM_GRANT = 24 << 20
TABLES = (
    "forward_z", "inverse_z", "forward_x", "lower_x", "inverse_x", "twiddle",
    "kron", "second",
)


def on_device(velocity, adjoint_seed, susceptibility, remanence, region_bounds, step_id):
    tables = make_tables()
    shapes = [(16, 16, 512), (4, 16, 512), (16, 16, 256), (8, 16, 256)]
    shapes += [(2, 16, 16, 256), (2, 16, 16, 256), (3, 8, 16, 512), (3, 16, 16, 512)]
    shapes += [(3, 16, 16, 512), (3, 16, 16, 512), (2, 16, 16, 256), (2, 16, 16, 256)]
    shapes += [(8, 16, 256), (16, 16, 256), (4, 16, 512), (16, 16, 512)]
    for n in (7, 1):
        shapes += [(n, 34, 16, 128), (2, n, 32, 128), (2, n, 32, 128), (8, 512), (8, 512)]
        shapes += [(n, 32, 16, 128)]
    shapes += [(32, 16, 128)]
    sems = [(16,), (), (16,), (), (2, 16), (2,), (3, 16), (3,)]
    sems += [(3, 16), (3,), (2, 16), (2,), (16,), (), (16,), ()]
    sems += [(5,)] * 4
    vmem = pl.BlockSpec(memory_space=pltpu.VMEM)
    smem = pl.BlockSpec(memory_space=pltpu.SMEM)
    hbm = pl.BlockSpec(memory_space=pltpu.HBM)
    held = [pltpu.VMEM((32, 16, 128), f32)]
    held += [pltpu.VMEM(tables[n].shape, tables[n].dtype) for n in TABLES]
    operands = [velocity, adjoint_seed, susceptibility, remanence]
    operands += [jnp.asarray(tables[n]) for n in TABLES]
    operands = [pltpu.with_memory_space_constraint(x, pltpu.HBM) for x in operands]
    return pl.pallas_call(
        kernel,
        out_shape=(
            jax.ShapeDtypeStruct((3, 32, 16, 128), f32),
            jax.ShapeDtypeStruct((3, 32, 16, 128), f32),
            jax.ShapeDtypeStruct((32, 16, 128), f32),
        ),
        in_specs=[hbm] * (4 + len(TABLES)) + [smem] * 2,
        out_specs=(vmem, vmem, vmem),
        scratch_shapes=[pltpu.VMEM(s, f32) for s in shapes]
        + [pltpu.SemaphoreType.DMA(s) for s in sems]
        + held
        + [pltpu.SemaphoreType.DMA((12,))],
        compiler_params=pltpu.CompilerParams(
            collective_id=0, has_side_effects=True, vmem_limit_bytes=VMEM_GRANT
        ),
    )(*operands, region_bounds, step_id)


def solution(mesh):
    return jax.shard_map(
        on_device,
        mesh=mesh,
        in_specs=(
            P(None, "gx", "gy", "gz"),
            P(None, "gx", "gy", "gz"),
            P("gx", "gy", "gz"),
            P("gx", "gy", "gz"),
            P(),
            P(),
        ),
        out_specs=(P(None, "gx", "gy", "gz"), P(None, "gx", "gy", "gz"), P("gx", "gy", "gz")),
        check_vma=False,
    )
```

```python
import jax
import jax.numpy as jnp
import numpy as np
from jax import lax
from jax.experimental import pallas as pl
from jax.experimental.pallas import tpu as pltpu
from jax.sharding import PartitionSpec as P

time_step = 0.5
viscosity = 0.2
field_period = 24
full_turn = 6.283185307179586

bf16 = jnp.bfloat16
f32 = jnp.float32
MESH = pl.DeviceIdType.MESH


def pieces(matrix):
    matrix = np.asarray(matrix, np.float32)
    high = matrix.astype(jnp.bfloat16)
    low = (matrix - high.astype(np.float32)).astype(jnp.bfloat16)
    return np.stack([high, low])


def cut(value):
    high = value.astype(bf16)
    return high, (value - high.astype(f32)).astype(bf16)


def product(matrix, value, dims=(((1,), (0,)), ((), ()))):
    dot = lambda a, b: lax.dot_general(a, b, dims, preferred_element_type=f32)
    return dot(matrix[0], value[0]) + dot(matrix[0], value[1]) + dot(matrix[1], value[0])


def mul(matrix, value):
    return product(matrix, cut(value))


def make_tables():
    turn = 2.0 * np.pi / 256
    eye4, eye16 = np.eye(4), np.eye(16)
    c, s, j = np.arange(2)[:, None, None], np.arange(16)[:, None], np.arange(4)
    k3 = 1 + 8 * s + 4 * c + j
    z = np.arange(128)
    phase = turn * k3[..., None] * z
    forward_z = np.stack([np.cos(phase), -np.sin(phase)], 2).reshape(256, 128)
    weight = np.where(k3 == 128, 1.0, 2.0)[..., None] / 256.0**3
    inverse_z = []
    for part in range(2):
        phase = turn * k3[..., None] * (z + 128 * part)
        both = np.stack([np.cos(phase) * weight, -np.sin(phase) * weight], 2)
        inverse_z.append(both.reshape(256, 128).T)
    q, t, ka = np.arange(8), np.arange(2), np.arange(16)
    theta = turn * 16 * (2 * q[:, None, None] + t[None, :, None]) * ka
    c, s = np.cos(theta), np.sin(theta)
    turned = np.stack([np.stack([c, s]), np.stack([-s, c])])
    sign = np.stack([np.ones(4), (-1.0) ** (1 + j)])
    forward_x = np.einsum("abqtk,gj,ji->akitqgbj", turned, sign, eye4).reshape(128, 256)
    lower_x = np.einsum("abqtk,ji->akitqbj", turned[:, :, :4], eye4).reshape(128, 64)
    back = np.stack([np.stack([c, -s]), np.stack([s, c])])
    inverse_x = np.einsum("abqtk,ij->tqaibkj", back, eye4).reshape(128, 128)
    b = np.arange(16)
    phi = turn * ka[:, None] * b
    twiddle = np.stack([np.cos(phi), np.sin(phi)])[:, :, None, :, None]
    twiddle = np.broadcast_to(twiddle, (2, 16, 4, 16, 16)).reshape(2, 64, 256)
    angle = turn * 16 * b[:, None] * b
    kron = np.concatenate([np.kron(np.cos(angle), eye16), np.kron(np.sin(angle), eye16)], 1)
    k = np.arange(256)
    angle = turn * (k[:, None] * k % 256)
    return dict(
        forward_z=pieces(forward_z),
        inverse_z=np.stack([pieces(m) for m in inverse_z]),
        forward_x=pieces(forward_x),
        lower_x=pieces(lower_x),
        inverse_x=pieces(inverse_x),
        twiddle=twiddle.astype(np.float32),
        kron=pieces(kron),
        second=np.stack([pieces(np.cos(angle)), pieces(np.sin(angle))]),
    )


def half_turned(value):
    return pltpu.roll(value, 64, 1)


def rotated(cosine, sine, value, direction):
    value = cut(value)
    first, second = product(cosine, value), product(sine, value)
    lane = lax.broadcasted_iota(jnp.int32, (first.shape[0], 128), 1)
    sign = jnp.where(lane < 64, -direction, direction)
    blocks = [
        first[:, at : at + 128] + sign * half_turned(second[:, at : at + 128])
        for at in range(0, first.shape[1], 128)
    ]
    return blocks[0] if len(blocks) == 1 else jnp.concatenate(blocks, axis=1)


def depth_waves(block, forward_z):
    return product(forward_z, cut(block), (((1,), (1,)), ((), ())))


def sixteenths(value, kron, direction):
    both = product(cut(value), kron)
    first, second = both[:, :256], both[:, 256:]
    return jnp.concatenate(
        [first[:64] - direction * second[64:], first[64:] + direction * second[:64]], axis=0
    )


def first_forward(mixed, twiddle, kron):
    real, imag = mixed[:64], mixed[64:]
    c, s = twiddle[0], twiddle[1]
    turned = jnp.concatenate([real * c + imag * s, imag * c - real * s], axis=0)
    return sixteenths(turned, kron, -1.0).T


def first_inverse(value, twiddle, kron, inverse_x):
    turned = sixteenths(value.T, kron, 1.0)
    real, imag = turned[:64], turned[64:]
    c, s = twiddle[0], twiddle[1]
    turned = jnp.concatenate([real * c - imag * s, imag * c + real * s], axis=0)
    return mul(inverse_x, turned)


def halves_on_rows(block):
    return jnp.concatenate([block[:, :256], block[:, 256:]], axis=0)


def signed_wave(index):
    folded = jnp.where(index < 128, index, index - 256)
    return jnp.where(index == 128, 0, folded).astype(f32) * (full_turn / 256)


def factor_of(index, third):
    half = full_turn / 2
    return jnp.where(third == 128, jnp.where(index == 128, half, 0.0), signed_wave(index))


def wave_numbers(place, chunk):
    row = lax.broadcasted_iota(jnp.int32, (256, 128), 0)
    lane = lax.broadcasted_iota(jnp.int32, (256, 128), 1)
    return row, lane % 64 // 4, 1 + 8 * place + 4 * chunk + lane % 4


def spectral_factors(place, gy, chunk):
    row, low, third = wave_numbers(place, chunk)
    first = low + 16 * gy
    third_wave = third.astype(f32) * (full_turn / 256)
    fold = lambda i: jnp.where(i < 128, i, i - 256).astype(f32) * (full_turn / 256)
    first_wave, second_wave = fold(first), fold(row)
    square = first_wave * first_wave + second_wave * second_wave + third_wave * third_wave
    return -third_wave / square, factor_of(row, third)


def mixing_factors(place, chunk):
    row, low, third = wave_numbers(place, chunk)
    return factor_of(low + 16 * (row // 16), third), third.astype(f32) * (full_turn / 256)


UNROLL = 5
DEPTH = 2


class Place:
    def __init__(self):
        self.gx, self.gy, self.gz = (lax.axis_index(a) for a in ("gx", "gy", "gz"))
        self.wave = self.gx * 2 + self.gz

    def by_wave(self, wave):
        return (lax.div(wave, 2), self.gy, lax.rem(wave, 2))

    def by_second(self, second):
        return (self.gx, second, self.gz)

    def announce(self):
        barrier = pltpu.get_barrier_semaphore()

        def signal(step, carry):
            for target in (
                self.by_wave(lax.rem(self.wave + step, 16)),
                self.by_second(lax.rem(self.gy + step, 16)),
            ):
                pl.semaphore_signal(barrier, inc=1, device_id=target, device_id_type=MESH)
            return carry

        lax.fori_loop(1, 16, signal, 0, unroll=UNROLL)

    def meet(self):
        pl.semaphore_wait(pltpu.get_barrier_semaphore(), 30)


class Exchange:
    def __init__(self, me, device, src, dst, send_sem, recv_sem, wanted=None):
        self.me, self.device, self.src, self.dst = me, device, src, dst
        self.send_sem, self.recv_sem, self.wanted = send_sem, recv_sem, wanted

    def each(self, act):
        def body(step, carry):
            peer = lax.rem(self.me + step, 16)
            if self.wanted is None:
                act(peer)
            else:
                pl.when(self.wanted(peer))(lambda: act(peer))
            return carry

        lax.fori_loop(1, 16, body, 0, unroll=UNROLL)

    def copy(self, peer):
        return pltpu.make_async_remote_copy(
            src_ref=self.src(peer),
            dst_ref=self.dst,
            send_sem=self.send_sem(peer),
            recv_sem=self.recv_sem,
            device_id=self.device(peer),
            device_id_type=MESH,
        )

    def start(self, after=None):
        def act(peer):
            if after is not None:
                after.copy(peer).wait_send()
            self.copy(peer).start()

        own = pltpu.make_async_copy(self.src(self.me), self.dst, self.recv_sem)
        if self.wanted is None:
            own.start()
        else:
            pl.when(self.wanted(self.me))(lambda: own.start())
        self.each(act)

    def finish(self):
        self.each(lambda peer: self.copy(peer).wait_send())


class Chain:
    def __init__(self, exchanges):
        self.exchanges, self.count = exchanges, 0

    def start(self, number):
        before = self.exchanges[number - DEPTH] if number >= DEPTH else None
        assert number == self.count
        self.exchanges[number].start(before)
        self.count += 1

    def finish(self):
        for exchange in self.exchanges[-DEPTH:]:
            exchange.finish()


def arrived(buffer, sem):
    pltpu.make_async_copy(buffer, buffer, sem).wait()


def region(at, bounds):
    row = lax.broadcasted_iota(jnp.int32, (512, 128), 0)
    third = lax.broadcasted_iota(jnp.int32, (512, 128), 1) + at.gz * 128
    first, second = row // 16 + at.gx * 32, row % 16 + at.gy * 16
    inside = (first >= bounds[0, 0]) & (first < bounds[1, 0])
    inside = inside & (second >= bounds[0, 1]) & (second < bounds[1, 1])
    inside = inside & (third >= bounds[0, 2]) & (third < bounds[1, 2])
    return jnp.where(inside, 1.0, 0.0)


def lower_rows(ref):
    return jnp.concatenate([ref[:, 0:32], ref[:, 64:96]], axis=1)


class Halo:
    def __init__(self, at, block, second_out, second_in, third_out, third_in, sent, got):
        self.at, self.block = at, block
        self.second_out, self.second_in = second_out, second_in
        self.third_out, self.third_in = third_out, third_in
        gx, gy, gz = at.gx, at.gy, at.gz
        self.copies = []
        for number, (src, dst, there, here, target) in enumerate(
            (
                (block.at[:, 32], block.at[:, 0], gx < 7, gx > 0, ((gx + 1) % 8, gy, gz)),
                (block.at[:, 1], block.at[:, 33], gx > 0, gx < 7, ((gx + 7) % 8, gy, gz)),
                (second_out.at[1], second_in.at[0], gy < 15, gy > 0, (gx, (gy + 1) % 16, gz)),
                (second_out.at[0], second_in.at[1], gy > 0, gy < 15, (gx, (gy + 15) % 16, gz)),
                (third_out, third_in, None, None, (gx, gy, 1 - gz)),
            )
        ):
            copy = pltpu.make_async_remote_copy(
                src_ref=src,
                dst_ref=dst,
                send_sem=sent.at[number],
                recv_sem=got.at[number],
                device_id=target,
                device_id_type=MESH,
            )
            self.copies.append((copy, there, here, dst))

    def start(self):
        block = self.block
        for face, row in ((0, 0), (1, 15)):
            self.second_out[face] = block[:, 1:33, row, :]
        for f in range(block.shape[0]):
            cells = block[f, 1:33].reshape(512, 128).T
            row = jnp.where(self.at.gz == 0, cells[127:128], cells[0:1])
            self.third_out[f : f + 1] = row
        for copy, there, here, dst in self.copies:
            if there is None:
                copy.start()
            else:
                pl.when(there)(lambda copy=copy: copy.start())

    def arrive(self, wide):
        for copy, there, here, dst in self.copies:
            if here is None:
                copy.wait_recv()
            else:
                pl.when(here)(lambda copy=copy: copy.wait_recv())

                @pl.when(jnp.logical_not(here))
                def _(dst=dst):
                    dst[...] = jnp.zeros(dst.shape, f32)

        for f in range(self.block.shape[0]):
            row = jnp.broadcast_to(self.third_in[f : f + 1], (128, 512))
            wide[f] = row.T.reshape(32, 16, 128)

    def finish(self):
        for copy, there, here, dst in self.copies:
            if there is None:
                copy.wait_send()
            else:
                pl.when(there)(lambda copy=copy: copy.wait_send())


def neighbours(at, halo, wide, f, i):
    block = halo.block
    here = block[f, i + 1]
    row = lax.broadcasted_iota(jnp.int32, (16, 128), 0)
    lane = lax.broadcasted_iota(jnp.int32, (16, 128), 1)
    below = halo.second_in[0, f, pl.ds(i, 1)]
    above = halo.second_in[1, f, pl.ds(i, 1)]
    side = wide[f, i]
    second = (
        jnp.where(row == 0, below, pltpu.roll(here, 1, 0)),
        jnp.where(row == 15, above, pltpu.roll(here, 15, 0)),
    )
    third = (
        jnp.where(lane == 0, jnp.where(at.gz == 1, side, 0.0), pltpu.roll(here, 1, 1)),
        jnp.where(lane == 127, jnp.where(at.gz == 0, side, 0.0), pltpu.roll(here, 127, 1)),
    )
    return here, ((block[f, i], block[f, i + 2]), second, third)


def laplace(here, around):
    total = -6.0 * here
    for low, high in around:
        total = total + (low + high)
    return total


def slope(pair):
    return (pair[1] - pair[0]) * 0.5


def cell_rows(at, halo, wide, next_out, adjoint_out, source):
    def body(i, carry):
        cells = [neighbours(at, halo, wide, f, i) for f in range(7)]
        velocity, seed = cells[:3], cells[3:6]
        suscept = cells[6]
        total = 0.0
        for d in range(3):
            pair = [suscept[1][d][e] * seed[d][1][d][e] for e in range(2)]
            total = total + slope(pair)
        source[i] = -time_step * total
        for k in range(3):
            here, around = velocity[k]
            advect = sum(velocity[j][0] * slope(around[j]) for j in range(3))
            next_out[k, i] = here + time_step * (viscosity * laplace(here, around) - advect)
            here, around = seed[k]
            shear = sum(seed[j][0] * slope(velocity[j][1][k]) for j in range(3))
            carried = sum(
                slope([velocity[j][1][j][e] * around[j][e] for e in range(2)]) for j in range(3)
            )
            adjoint_out[k, i] = here + time_step * (
                viscosity * laplace(here, around) - shear + carried
            )
        return carry

    lax.fori_loop(0, 32, body, 0)


def energy_rows(at, halo, wide, cells, next_out):
    def body(i, carry):
        _, around = neighbours(at, halo, wide, 0, i)
        scaled = time_step * cells[6, i + 1]
        for k in range(3):
            next_out[k, i] = next_out[k, i] + scaled * slope(around[k])
        return carry

    lax.fori_loop(0, 32, body, 0)


ORDER = (0, 2, 1)
CHUNKS = ((0,), (1,))
SECONDS = ((0, 0), (0, 1), (1, 0), (1, 1))
LASTS = ((0, 0), (2, 0), (0, 1), (2, 1), (1, 0), (1, 1))
BACK = ((0, 0), (0, 1), (2, 0), (2, 1), (1, 0), (1, 1))


def kernel(
    velocity, adjoint_seed, suscept, remanence_in,
    forward_z_in, inverse_z_in, forward_x_in, lower_x_in, inverse_x_in, twiddle_in, kron_in,
    second_in, bounds, step,
    next_out, adjoint_out, gradient_out,
    z_out, z_in, k_out, k_in, y_out, y_in, x_out, x_in,
    zb_out, zb_in, kb_out, kb_in, yb_out, yb_in, xb_out, xb_in,
    cells, cells_y_out, cells_y_in, cells_z_out, cells_z_in, cells_wide,
    energy, energy_y_out, energy_y_in, energy_z_out, energy_z_in, energy_wide, source,
    z_sent, z_got, k_sent, k_got, y_sent, y_got, x_sent, x_got,
    zb_sent, zb_got, kb_sent, kb_got, yb_sent, yb_got, xb_sent, xb_got,
    cells_sent, cells_got, energy_sent, energy_got,
    remanence, forward_z, inverse_z, forward_x, lower_x, inverse_x, twiddle, kron, second, loaded,
):
    at = Place()
    at.announce()
    loads = {}
    for number, (name, src, dst) in enumerate(
        (
            ("remanence", remanence_in, remanence),
            ("forward_z", forward_z_in, forward_z),
            ("velocity", velocity, cells.at[0:3, 1:33]),
            ("seed", adjoint_seed, cells.at[3:6, 1:33]),
            ("suscept", suscept, cells.at[6, 1:33]),
            ("lower_x", lower_x_in, lower_x),
            ("twiddle", twiddle_in, twiddle),
            ("kron", kron_in, kron),
            ("second", second_in, second),
            ("inverse_x", inverse_x_in, inverse_x),
            ("inverse_z", inverse_z_in, inverse_z),
            ("forward_x", forward_x_in, forward_x),
        )
    ):
        loads[name] = pltpu.make_async_copy(src, dst, loaded.at[number])
        loads[name].start()
    in_lower = (at.gx < 4) & (at.gy < 8) & (at.gz == 0)
    has_rows = at.gy < 8

    def over_waves(order, out, into, sent, got, block=lambda p: p, slot=None, wanted=None):
        slot = at.wave if slot is None else slot
        return Chain(
            [
                Exchange(
                    at.wave, at.by_wave, lambda p, k=k: out.at[*k, block(p)], into.at[*k, slot],
                    lambda p, n=n: sent.at[n, p], got.at[n], wanted,
                )
                for n, k in enumerate(order)
            ]
        )

    def over_seconds(order, out, into, sent, got, block=lambda p: p, slot=None, wanted=None):
        slot = at.gy if slot is None else slot
        return Chain(
            [
                Exchange(
                    at.gy, at.by_second, lambda p, k=k: out.at[*k, block(p)], into.at[*k, slot],
                    lambda p, n=n: sent.at[n, p], got.at[n], wanted,
                )
                for n, k in enumerate(order)
            ]
        )

    depths = over_waves(CHUNKS, z_out, z_in, z_sent, z_got, slot=lax.rem(at.gx, 4))
    firsts = over_seconds(CHUNKS, k_out, k_in, k_sent, k_got, slot=lax.rem(at.gy, 8))
    seconds = over_seconds(SECONDS, y_out, y_in, y_sent, y_got)
    lasts = over_waves(LASTS, x_out, x_in, x_sent, x_got, lambda p: lax.div(p, 2))
    depths_back = over_waves(BACK, zb_out, zb_in, zb_sent, zb_got)
    firsts_back = over_seconds(SECONDS, kb_out, kb_in, kb_sent, kb_got)
    seconds_back = over_seconds(
        CHUNKS, yb_out, yb_in, yb_sent, yb_got, lambda p: lax.rem(p, 8), None, lambda p: p < 8
    )
    lasts_back = over_waves(
        CHUNKS, xb_out, xb_in, xb_sent, xb_got, lambda p: lax.rem(lax.div(p, 2), 4), None,
        lambda p: (p < 8) & (lax.rem(p, 2) == 0),
    )
    cell_halo = Halo(
        at, cells, cells_y_out, cells_y_in, cells_z_out, cells_z_in, cells_sent, cells_got
    )
    energy_halo = Halo(
        at, energy, energy_y_out, energy_y_in, energy_z_out, energy_z_in, energy_sent, energy_got
    )

    loads["remanence"].wait()
    loads["forward_z"].wait()

    @pl.when(in_lower)
    def _():
        magnet = remanence[...].reshape(512, 128) * region(at, bounds)
        z_out[...] = depth_waves(magnet, forward_z).reshape(2, 16, 8, 512)

    at.meet()

    @pl.when(in_lower)
    def _():
        depths.start(0)
        depths.start(1)

    for name in ("velocity", "seed", "suscept"):
        loads[name].wait()
    cell_halo.start()
    for name in ("lower_x", "twiddle", "kron"):
        loads[name].wait()

    @pl.when(has_rows)
    def _():
        for c in range(2):
            arrived(z_in.at[c], z_got.at[c])
            block = mul(lower_x, halves_on_rows(z_in[c].reshape(32, 512)))
            k_out[c] = first_forward(block, twiddle, kron).reshape(16, 16, 128)
            firsts.start(c)

    cell_halo.arrive(cells_wide)
    cell_rows(at, cell_halo, cells_wide, next_out, adjoint_out, source)

    loads["second"].wait()
    factors = [spectral_factors(at.wave, at.gy, c) for c in range(2)]
    cosine, sine = second.at[0], second.at[1]
    for c in range(2):
        potential, second_factor = factors[c]
        arrived(k_in.at[c], k_got.at[c])
        value = k_in[c].reshape(128, 128)
        value = rotated(cosine[:, :, :128], sine[:, :, :128], value, -1.0) * potential
        value = jnp.concatenate([value, value * second_factor], axis=1)
        value = rotated(cosine, sine, value, 1.0)
        y_out[0, c] = value[:, :128].reshape(16, 16, 128)
        y_out[1, c] = value[:, 128:].reshape(16, 16, 128)
        seconds.start(c)
    seconds.start(2)
    seconds.start(3)

    loads["inverse_x"].wait()
    mixing = [mixing_factors(at.wave, c) for c in range(2)]

    def send_first(f, c, value):
        value = first_inverse(value, twiddle, kron, inverse_x)
        x_out[f, c, :, :, :256] = value[:64].reshape(8, 8, 256)
        x_out[f, c, :, :, 256:] = value[64:].reshape(8, 8, 256)
        lasts.start(LASTS.index((f, c)))

    for c in range(2):
        arrived(y_in.at[0, c], y_got.at[c])
        value = y_in[0, c].reshape(256, 128)
        send_first(0, c, value * mixing[c][0])
        send_first(2, c, value * mixing[c][1])
    for c in range(2):
        arrived(y_in.at[1, c], y_got.at[2 + c])
        send_first(1, c, y_in[1, c].reshape(256, 128))

    loads["inverse_z"].wait()
    turned = jnp.full((8, 128), step[0] % field_period, jnp.int32).astype(f32)
    turned = full_turn * turned / field_period
    applied = (jnp.cos(turned)[:1], jnp.sin(turned)[:1], None)
    square = jnp.zeros((512, 128), f32)
    weight = source[...].reshape(512, 128)
    for f in ORDER:
        for c in range(2):
            arrived(x_in.at[f, c], x_got.at[LASTS.index((f, c))])
        field = mul(inverse_z.at[at.gz], x_in[f].reshape(256, 512)).T
        if applied[f] is not None:
            field = field + applied[f]
        square = square + field * field
        zb_out[f] = depth_waves(weight * field, forward_z).reshape(2, 16, 8, 512)
        for c in range(2):
            depths_back.start(BACK.index((f, c)))
    energy[0, 1:33] = (0.5 * square).reshape(32, 16, 128)
    energy_halo.start()

    loads["forward_x"].wait()

    def first_of(f, c):
        arrived(zb_in.at[f, c], zb_got.at[BACK.index((f, c))])
        block = mul(forward_x, halves_on_rows(zb_in[f, c].reshape(128, 512)))
        return first_forward(block, twiddle, kron)

    for c in range(2):
        value = first_of(0, c) * mixing[c][0] + first_of(2, c) * mixing[c][1]
        kb_out[0, c] = value.reshape(16, 16, 128)
        firsts_back.start(c)
    for c in range(2):
        kb_out[1, c] = first_of(1, c).reshape(16, 16, 128)
        firsts_back.start(2 + c)

    energy_halo.arrive(energy_wide)
    energy_rows(at, energy_halo, energy_wide, cells, next_out)
    pl.when(in_lower)(lambda: depths.finish())
    pl.when(has_rows)(lambda: firsts.finish())
    for each in (seconds, lasts, depths_back, cell_halo, energy_halo):
        each.finish()

    for c in range(2):
        potential, second_factor = factors[c]
        for f in range(2):
            arrived(kb_in.at[f, c], kb_got.at[2 * f + c])
        value = [kb_in[f, c].reshape(256, 128) for f in range(2)]
        value = rotated(cosine, sine, jnp.concatenate(value, axis=1), -1.0)
        value = (value[:, :128] + value[:, 128:] * second_factor) * potential
        value = rotated(cosine[:, :128], sine[:, :128], value, 1.0)
        yb_out[c] = value.reshape(8, 16, 128)
        seconds_back.start(c)
    firsts_back.finish()
    gradient_out[...] = jnp.zeros((32, 16, 128), f32)

    @pl.when(has_rows)
    def _():
        for c in range(2):
            arrived(yb_in.at[c], yb_got.at[c])
            value = yb_in[c].reshape(256, 128)
            value = first_inverse(value, twiddle, kron, lower_rows(inverse_x))
            xb_out[c, :, :, :256] = value[:32].reshape(4, 8, 256)
            xb_out[c, :, :, 256:] = value[32:].reshape(4, 8, 256)
            lasts_back.start(c)

    @pl.when(in_lower)
    def _():
        for c in range(2):
            arrived(xb_in.at[c], xb_got.at[c])
        value = mul(inverse_z.at[0], xb_in[...].reshape(256, 512)).T
        gradient_out[...] = (value * region(at, bounds)).reshape(32, 16, 128)

    seconds_back.finish()
    pl.when(has_rows)(lambda: lasts_back.finish())


VMEM_GRANT = 24 << 20
TABLES = (
    "forward_z", "inverse_z", "forward_x", "lower_x", "inverse_x", "twiddle",
    "kron", "second",
)


def on_device(velocity, adjoint_seed, susceptibility, remanence, region_bounds, step_id):
    tables = make_tables()
    shapes = [(2, 16, 8, 512), (2, 4, 8, 512), (2, 16, 16, 128), (2, 8, 16, 128)]
    shapes += [(2, 2, 16, 16, 128)] * 2 + [(3, 2, 8, 8, 512), (3, 2, 16, 8, 512)]
    shapes += [(3, 2, 16, 8, 512)] * 2 + [(2, 2, 16, 16, 128)] * 2
    shapes += [(2, 8, 16, 128), (2, 16, 16, 128), (2, 4, 8, 512), (2, 16, 8, 512)]
    for n in (7, 1):
        shapes += [(n, 34, 16, 128), (2, n, 32, 128), (2, n, 32, 128), (8, 512), (8, 512)]
        shapes += [(n, 32, 16, 128)]
    shapes += [(32, 16, 128)]
    sems = []
    for n in (2, 2, 4, 6, 6, 4, 2, 2):
        sems += [(n, 16), (n,)]
    sems += [(5,)] * 4
    vmem = pl.BlockSpec(memory_space=pltpu.VMEM)
    smem = pl.BlockSpec(memory_space=pltpu.SMEM)
    hbm = pl.BlockSpec(memory_space=pltpu.HBM)
    held = [pltpu.VMEM((32, 16, 128), f32)]
    held += [pltpu.VMEM(tables[n].shape, tables[n].dtype) for n in TABLES]
    operands = [velocity, adjoint_seed, susceptibility, remanence]
    operands += [jnp.asarray(tables[n]) for n in TABLES]
    operands = [pltpu.with_memory_space_constraint(x, pltpu.HBM) for x in operands]
    return pl.pallas_call(
        kernel,
        out_shape=(
            jax.ShapeDtypeStruct((3, 32, 16, 128), f32),
            jax.ShapeDtypeStruct((3, 32, 16, 128), f32),
            jax.ShapeDtypeStruct((32, 16, 128), f32),
        ),
        in_specs=[hbm] * (4 + len(TABLES)) + [smem] * 2,
        out_specs=(vmem, vmem, vmem),
        scratch_shapes=[pltpu.VMEM(s, f32) for s in shapes]
        + [pltpu.SemaphoreType.DMA(s) for s in sems]
        + held
        + [pltpu.SemaphoreType.DMA((12,))],
        compiler_params=pltpu.CompilerParams(
            collective_id=0, has_side_effects=True, vmem_limit_bytes=VMEM_GRANT
        ),
    )(*operands, region_bounds, step_id)


def solution(mesh):
    return jax.shard_map(
        on_device,
        mesh=mesh,
        in_specs=(
            P(None, "gx", "gy", "gz"),
            P(None, "gx", "gy", "gz"),
            P("gx", "gy", "gz"),
            P("gx", "gy", "gz"),
            P(),
            P(),
        ),
        out_specs=(P(None, "gx", "gy", "gz"), P(None, "gx", "gy", "gz"), P("gx", "gy", "gz")),
        check_vma=False,
    )
```

```python
import jax
import jax.numpy as jnp
import numpy as np
from jax import lax
from jax.experimental import pallas as pl
from jax.experimental.pallas import tpu as pltpu
from jax.sharding import PartitionSpec as P

time_step = 0.5
viscosity = 0.2
field_period = 24
full_turn = 6.283185307179586

bf16 = jnp.bfloat16
f32 = jnp.float32
MESH = pl.DeviceIdType.MESH


def pieces(matrix):
    matrix = np.asarray(matrix, np.float32)
    high = matrix.astype(jnp.bfloat16)
    low = (matrix - high.astype(np.float32)).astype(jnp.bfloat16)
    return np.stack([high, low])


def cut(value):
    high = value.astype(bf16)
    return high, (value - high.astype(f32)).astype(bf16)


def product(matrix, value, dims=(((1,), (0,)), ((), ()))):
    dot = lambda a, b: lax.dot_general(a, b, dims, preferred_element_type=f32)
    return dot(matrix[0], value[0]) + dot(matrix[0], value[1]) + dot(matrix[1], value[0])


def mul(matrix, value):
    return product(matrix, cut(value))


def make_tables():
    turn = 2.0 * np.pi / 256
    eye4, eye16 = np.eye(4), np.eye(16)
    c, s, j = np.arange(2)[:, None, None], np.arange(16)[:, None], np.arange(4)
    k3 = 1 + 8 * s + 4 * c + j
    z = np.arange(256)
    phase = turn * k3[..., None] * z
    forward_z = np.stack([np.cos(phase), -np.sin(phase)], 2).reshape(256, 256)
    weight = np.where(k3 == 128, 1.0, 2.0)[..., None] / 256.0**3
    both = np.stack([np.cos(phase) * weight, -np.sin(phase) * weight], 2)
    inverse_z = both.reshape(256, 256).T
    q, t, ka = np.arange(8), np.arange(2), np.arange(16)
    theta = turn * 16 * (2 * q[:, None, None] + t[None, :, None]) * ka
    c, s = np.cos(theta), np.sin(theta)
    turned = np.stack([np.stack([c, s]), np.stack([-s, c])])
    forward_x = np.einsum("abqtk,ji->akiqtbj", turned, eye4).reshape(128, 128)
    lower_x = np.einsum("abqtk,ji->akitqbj", turned[:, :, :4], eye4).reshape(128, 64)
    back = np.stack([np.stack([c, -s]), np.stack([s, c])])
    inverse_x = np.einsum("abqtk,ij->qtaibkj", back, eye4).reshape(128, 128)
    b = np.arange(16)
    phi = turn * ka[:, None] * b
    twiddle = np.stack([np.cos(phi), np.sin(phi)])[:, :, None, :, None]
    twiddle = np.broadcast_to(twiddle, (2, 16, 4, 16, 16)).reshape(2, 64, 256)
    angle = turn * 16 * b[:, None] * b
    kron = np.concatenate([np.kron(np.cos(angle), eye16), np.kron(np.sin(angle), eye16)], 1)
    k = np.arange(256)
    angle = turn * (k[:, None] * k % 256)
    return dict(
        forward_z=pieces(forward_z),
        inverse_z=pieces(inverse_z),
        forward_x=pieces(forward_x),
        lower_x=pieces(lower_x),
        inverse_x=pieces(inverse_x),
        twiddle=twiddle.astype(np.float32),
        kron=pieces(kron),
        second=np.stack([pieces(np.cos(angle)), pieces(np.sin(angle))]),
    )


def half_turned(value):
    return pltpu.roll(value, 64, 1)


def rotated(cosine, sine, value, direction):
    value = cut(value)
    first, second = product(cosine, value), product(sine, value)
    lane = lax.broadcasted_iota(jnp.int32, (first.shape[0], 128), 1)
    sign = jnp.where(lane < 64, -direction, direction)
    blocks = [
        first[:, at : at + 128] + sign * half_turned(second[:, at : at + 128])
        for at in range(0, first.shape[1], 128)
    ]
    return blocks[0] if len(blocks) == 1 else jnp.concatenate(blocks, axis=1)


def depth_waves(block, forward_z):
    return product(forward_z, cut(block), (((1,), (1,)), ((), ())))


def sixteenths(value, kron, direction):
    both = product(cut(value), kron)
    first, second = both[:, :256], both[:, 256:]
    return jnp.concatenate(
        [first[:64] - direction * second[64:], first[64:] + direction * second[:64]], axis=0
    )


def first_forward(mixed, twiddle, kron):
    real, imag = mixed[:64], mixed[64:]
    c, s = twiddle[0], twiddle[1]
    turned = jnp.concatenate([real * c + imag * s, imag * c - real * s], axis=0)
    return sixteenths(turned, kron, -1.0).T


def first_inverse(value, twiddle, kron, inverse_x):
    turned = sixteenths(value.T, kron, 1.0)
    real, imag = turned[:64], turned[64:]
    c, s = twiddle[0], twiddle[1]
    turned = jnp.concatenate([real * c - imag * s, imag * c + real * s], axis=0)
    return mul(inverse_x, turned)


def halves_on_rows(block):
    return jnp.concatenate([block[:, :256], block[:, 256:]], axis=0)


def signed_wave(index):
    folded = jnp.where(index < 128, index, index - 256)
    return jnp.where(index == 128, 0, folded).astype(f32) * (full_turn / 256)


def factor_of(index, third):
    half = full_turn / 2
    return jnp.where(third == 128, jnp.where(index == 128, half, 0.0), signed_wave(index))


def wave_numbers(place, chunk):
    row = lax.broadcasted_iota(jnp.int32, (256, 128), 0)
    lane = lax.broadcasted_iota(jnp.int32, (256, 128), 1)
    return row, lane % 64 // 4, 1 + 8 * place + 4 * chunk + lane % 4


def spectral_factors(place, gy, chunk):
    row, low, third = wave_numbers(place, chunk)
    first = low + 16 * gy
    third_wave = third.astype(f32) * (full_turn / 256)
    fold = lambda i: jnp.where(i < 128, i, i - 256).astype(f32) * (full_turn / 256)
    first_wave, second_wave = fold(first), fold(row)
    square = first_wave * first_wave + second_wave * second_wave + third_wave * third_wave
    return -third_wave / square, factor_of(row, third)


def mixing_factors(place, chunk):
    row, low, third = wave_numbers(place, chunk)
    return factor_of(low + 16 * (row // 16), third), third.astype(f32) * (full_turn / 256)


UNROLL = 5
DEPTH = 2


class Place:
    def __init__(self):
        self.gx, self.gy, self.gz = (lax.axis_index(a) for a in ("gx", "gy", "gz"))
        self.wave = self.gx * 2 + self.gz

    def by_wave(self, wave):
        return (lax.div(wave, 2), self.gy, lax.rem(wave, 2))

    def by_second(self, second):
        return (self.gx, second, self.gz)

    def announce(self):
        barrier = pltpu.get_barrier_semaphore()

        def signal(step, carry):
            for target in (
                self.by_wave(lax.rem(self.wave + step, 16)),
                self.by_second(lax.rem(self.gy + step, 16)),
            ):
                pl.semaphore_signal(barrier, inc=1, device_id=target, device_id_type=MESH)
            return carry

        lax.fori_loop(1, 16, signal, 0, unroll=UNROLL)

    def meet(self):
        pl.semaphore_wait(pltpu.get_barrier_semaphore(), 30)


class Exchange:
    def __init__(self, me, device, src, dst, send_sem, recv_sem, wanted=None):
        self.me, self.device, self.src, self.dst = me, device, src, dst
        self.send_sem, self.recv_sem, self.wanted = send_sem, recv_sem, wanted

    def each(self, act):
        def body(step, carry):
            peer = lax.rem(self.me + step, 16)
            if self.wanted is None:
                act(peer)
            else:
                pl.when(self.wanted(peer))(lambda: act(peer))
            return carry

        lax.fori_loop(1, 16, body, 0, unroll=UNROLL)

    def copy(self, peer):
        return pltpu.make_async_remote_copy(
            src_ref=self.src(peer),
            dst_ref=self.dst,
            send_sem=self.send_sem(peer),
            recv_sem=self.recv_sem,
            device_id=self.device(peer),
            device_id_type=MESH,
        )

    def start(self, after=None):
        def act(peer):
            if after is not None:
                after.copy(peer).wait_send()
            self.copy(peer).start()

        own = pltpu.make_async_copy(self.src(self.me), self.dst, self.recv_sem)
        if self.wanted is None:
            own.start()
        else:
            pl.when(self.wanted(self.me))(lambda: own.start())
        self.each(act)

    def finish(self):
        self.each(lambda peer: self.copy(peer).wait_send())


class Chain:
    def __init__(self, exchanges):
        self.exchanges, self.count = exchanges, 0

    def start(self, number):
        before = self.exchanges[number - DEPTH] if number >= DEPTH else None
        assert number == self.count
        self.exchanges[number].start(before)
        self.count += 1

    def finish(self):
        for exchange in self.exchanges[-DEPTH:]:
            exchange.finish()


def arrived(buffer, sem):
    pltpu.make_async_copy(buffer, buffer, sem).wait()


def region(at, bounds):
    row = lax.broadcasted_iota(jnp.int32, (512, 128), 0)
    third = lax.broadcasted_iota(jnp.int32, (512, 128), 1) + at.gz * 128
    first, second = row // 16 + at.gx * 32, row % 16 + at.gy * 16
    inside = (first >= bounds[0, 0]) & (first < bounds[1, 0])
    inside = inside & (second >= bounds[0, 1]) & (second < bounds[1, 1])
    inside = inside & (third >= bounds[0, 2]) & (third < bounds[1, 2])
    return jnp.where(inside, 1.0, 0.0)


class Halo:
    def __init__(self, at, block, second_out, second_in, third_out, third_in, sent, got):
        self.at, self.block = at, block
        self.second_out, self.second_in = second_out, second_in
        self.third_out, self.third_in = third_out, third_in
        gx, gy, gz = at.gx, at.gy, at.gz
        self.copies = []
        for number, (src, dst, there, here, target) in enumerate(
            (
                (block.at[:, 32], block.at[:, 0], gx < 7, gx > 0, ((gx + 1) % 8, gy, gz)),
                (block.at[:, 1], block.at[:, 33], gx > 0, gx < 7, ((gx + 7) % 8, gy, gz)),
                (second_out.at[1], second_in.at[0], gy < 15, gy > 0, (gx, (gy + 1) % 16, gz)),
                (second_out.at[0], second_in.at[1], gy > 0, gy < 15, (gx, (gy + 15) % 16, gz)),
                (third_out, third_in, None, None, (gx, gy, 1 - gz)),
            )
        ):
            copy = pltpu.make_async_remote_copy(
                src_ref=src,
                dst_ref=dst,
                send_sem=sent.at[number],
                recv_sem=got.at[number],
                device_id=target,
                device_id_type=MESH,
            )
            self.copies.append((copy, there, here, dst))

    def start(self):
        block = self.block
        for face, row in ((0, 0), (1, 15)):
            self.second_out[face] = block[:, 1:33, row, :]
        for f in range(block.shape[0]):
            cells = block[f, 1:33].reshape(512, 128).T
            row = jnp.where(self.at.gz == 0, cells[127:128], cells[0:1])
            self.third_out[f : f + 1] = row
        for copy, there, here, dst in self.copies:
            if there is None:
                copy.start()
            else:
                pl.when(there)(lambda copy=copy: copy.start())

    def arrive(self, wide):
        for copy, there, here, dst in self.copies:
            if here is None:
                copy.wait_recv()
            else:
                pl.when(here)(lambda copy=copy: copy.wait_recv())

                @pl.when(jnp.logical_not(here))
                def _(dst=dst):
                    dst[...] = jnp.zeros(dst.shape, f32)

        for f in range(self.block.shape[0]):
            row = jnp.broadcast_to(self.third_in[f : f + 1], (128, 512))
            wide[f] = row.T.reshape(32, 16, 128)

    def finish(self):
        for copy, there, here, dst in self.copies:
            if there is None:
                copy.wait_send()
            else:
                pl.when(there)(lambda copy=copy: copy.wait_send())


def neighbours(at, halo, wide, f, i):
    block = halo.block
    here = block[f, i + 1]
    row = lax.broadcasted_iota(jnp.int32, (16, 128), 0)
    lane = lax.broadcasted_iota(jnp.int32, (16, 128), 1)
    below = halo.second_in[0, f, pl.ds(i, 1)]
    above = halo.second_in[1, f, pl.ds(i, 1)]
    side = wide[f, i]
    second = (
        jnp.where(row == 0, below, pltpu.roll(here, 1, 0)),
        jnp.where(row == 15, above, pltpu.roll(here, 15, 0)),
    )
    third = (
        jnp.where(lane == 0, jnp.where(at.gz == 1, side, 0.0), pltpu.roll(here, 1, 1)),
        jnp.where(lane == 127, jnp.where(at.gz == 0, side, 0.0), pltpu.roll(here, 127, 1)),
    )
    return here, ((block[f, i], block[f, i + 2]), second, third)


def laplace(here, around):
    total = -6.0 * here
    for low, high in around:
        total = total + (low + high)
    return total


def slope(pair):
    return (pair[1] - pair[0]) * 0.5


def cell_rows(at, halo, wide, next_out, adjoint_out, source):
    def body(i, carry):
        cells = [neighbours(at, halo, wide, f, i) for f in range(7)]
        velocity, seed = cells[:3], cells[3:6]
        suscept = cells[6]
        total = 0.0
        for d in range(3):
            pair = [suscept[1][d][e] * seed[d][1][d][e] for e in range(2)]
            total = total + slope(pair)
        source[i] = -time_step * total
        for k in range(3):
            here, around = velocity[k]
            advect = sum(velocity[j][0] * slope(around[j]) for j in range(3))
            next_out[k, i] = here + time_step * (viscosity * laplace(here, around) - advect)
            here, around = seed[k]
            shear = sum(seed[j][0] * slope(velocity[j][1][k]) for j in range(3))
            carried = sum(
                slope([velocity[j][1][j][e] * around[j][e] for e in range(2)]) for j in range(3)
            )
            adjoint_out[k, i] = here + time_step * (
                viscosity * laplace(here, around) - shear + carried
            )
        return carry

    lax.fori_loop(0, 32, body, 0)


def energy_rows(at, halo, wide, cells, next_out):
    def body(i, carry):
        _, around = neighbours(at, halo, wide, 0, i)
        scaled = time_step * cells[6, i + 1]
        for k in range(3):
            next_out[k, i] = next_out[k, i] + scaled * slope(around[k])
        return carry

    lax.fori_loop(0, 32, body, 0)


ORDER = (0, 2, 1)
CHUNKS = ((0,), (1,))
SECONDS = ((0, 0), (0, 1), (1, 0), (1, 1))
LASTS = ((0, 0), (2, 0), (0, 1), (2, 1), (1, 0), (1, 1))
BACK = ((0, 0), (0, 1), (2, 0), (2, 1), (1, 0), (1, 1))


def kernel(
    velocity, adjoint_seed, suscept, remanence_in,
    forward_z_in, inverse_z_in, forward_x_in, lower_x_in, inverse_x_in, twiddle_in, kron_in,
    second_in, bounds, step,
    next_out, adjoint_out, gradient_out,
    z_out, z_in, k_out, k_in, y_out, y_in, x_out, x_in,
    zb_out, zb_in, kb_out, kb_in, yb_out, yb_in, xb_out, xb_in,
    cells, cells_y_out, cells_y_in, cells_z_out, cells_z_in, cells_wide,
    energy, energy_y_out, energy_y_in, energy_z_out, energy_z_in, energy_wide, source,
    source_in, energy_out,
    z_sent, z_got, k_sent, k_got, y_sent, y_got, x_sent, x_got,
    zb_sent, zb_got, kb_sent, kb_got, yb_sent, yb_got, xb_sent, xb_got,
    cells_sent, cells_got, energy_sent, energy_got, swap_sent, swap_got,
    remanence, forward_z, inverse_z, forward_x, lower_x, inverse_x, twiddle, kron, second, loaded,
):
    at = Place()
    at.announce()
    loads = {}
    for number, (name, src, dst) in enumerate(
        (
            ("remanence", remanence_in, remanence),
            ("forward_z", forward_z_in, forward_z),
            ("velocity", velocity, cells.at[0:3, 1:33]),
            ("seed", adjoint_seed, cells.at[3:6, 1:33]),
            ("suscept", suscept, cells.at[6, 1:33]),
            ("lower_x", lower_x_in, lower_x),
            ("twiddle", twiddle_in, twiddle),
            ("kron", kron_in, kron),
            ("second", second_in, second),
            ("inverse_x", inverse_x_in, inverse_x),
            ("inverse_z", inverse_z_in, inverse_z),
            ("forward_x", forward_x_in, forward_x),
        )
    ):
        loads[name] = pltpu.make_async_copy(src, dst, loaded.at[number])
        loads[name].start()
    in_lower = (at.gx < 4) & (at.gy < 8) & (at.gz == 0)
    has_rows = at.gy < 8

    def over_waves(order, out, into, sent, got, block=lambda p: p, slot=None, wanted=None):
        slot = at.wave if slot is None else slot
        return Chain(
            [
                Exchange(
                    at.wave, at.by_wave, lambda p, k=k: out.at[*k, block(p)], into.at[*k, slot],
                    lambda p, n=n: sent.at[n, p], got.at[n], wanted,
                )
                for n, k in enumerate(order)
            ]
        )

    def over_seconds(order, out, into, sent, got, block=lambda p: p, slot=None, wanted=None):
        slot = at.gy if slot is None else slot
        return Chain(
            [
                Exchange(
                    at.gy, at.by_second, lambda p, k=k: out.at[*k, block(p)], into.at[*k, slot],
                    lambda p, n=n: sent.at[n, p], got.at[n], wanted,
                )
                for n, k in enumerate(order)
            ]
        )

    depths = over_waves(CHUNKS, z_out, z_in, z_sent, z_got, slot=lax.rem(at.gx, 4))
    firsts = over_seconds(CHUNKS, k_out, k_in, k_sent, k_got, slot=lax.rem(at.gy, 8))
    seconds = over_seconds(SECONDS, y_out, y_in, y_sent, y_got)
    lasts = over_waves(LASTS, x_out, x_in, x_sent, x_got)
    depths_back = over_waves(BACK, zb_out, zb_in, zb_sent, zb_got)
    firsts_back = over_seconds(SECONDS, kb_out, kb_in, kb_sent, kb_got)
    seconds_back = over_seconds(
        CHUNKS, yb_out, yb_in, yb_sent, yb_got, lambda p: lax.rem(p, 8), None, lambda p: p < 8
    )
    lasts_back = over_waves(
        CHUNKS, xb_out, xb_in, xb_sent, xb_got, lambda p: lax.rem(lax.div(p, 2), 4), None,
        lambda p: (p < 8) & (lax.rem(p, 2) == 0),
    )
    cell_halo = Halo(
        at, cells, cells_y_out, cells_y_in, cells_z_out, cells_z_in, cells_sent, cells_got
    )
    energy_halo = Halo(
        at, energy, energy_y_out, energy_y_in, energy_z_out, energy_z_in, energy_sent, energy_got
    )

    loads["remanence"].wait()
    loads["forward_z"].wait()

    @pl.when(in_lower)
    def _():
        magnet = remanence[...].reshape(512, 128) * region(at, bounds)
        z_out[...] = depth_waves(magnet, forward_z[:, :, :128]).reshape(2, 16, 8, 512)

    at.meet()

    @pl.when(in_lower)
    def _():
        depths.start(0)
        depths.start(1)

    for name in ("velocity", "seed", "suscept"):
        loads[name].wait()
    cell_halo.start()
    for name in ("lower_x", "twiddle", "kron"):
        loads[name].wait()

    @pl.when(has_rows)
    def _():
        for c in range(2):
            arrived(z_in.at[c], z_got.at[c])
            block = mul(lower_x, halves_on_rows(z_in[c].reshape(32, 512)))
            k_out[c] = first_forward(block, twiddle, kron).reshape(16, 16, 128)
            firsts.start(c)

    cell_halo.arrive(cells_wide)
    cell_rows(at, cell_halo, cells_wide, next_out, adjoint_out, source)
    here, there = at.gz * 16, (1 - at.gz) * 16
    source_swap = pltpu.make_async_remote_copy(
        src_ref=source.at[pl.ds(there, 16)],
        dst_ref=source_in,
        send_sem=swap_sent.at[0],
        recv_sem=swap_got.at[0],
        device_id=(at.gx, at.gy, 1 - at.gz),
        device_id_type=MESH,
    )
    energy_swap = pltpu.make_async_remote_copy(
        src_ref=energy_out,
        dst_ref=energy.at[0, pl.ds(1 + here, 16)],
        send_sem=swap_sent.at[1],
        recv_sem=swap_got.at[1],
        device_id=(at.gx, at.gy, 1 - at.gz),
        device_id_type=MESH,
    )
    source_swap.start()

    loads["second"].wait()
    factors = [spectral_factors(at.wave, at.gy, c) for c in range(2)]
    cosine, sine = second.at[0], second.at[1]
    for c in range(2):
        potential, second_factor = factors[c]
        arrived(k_in.at[c], k_got.at[c])
        value = k_in[c].reshape(128, 128)
        value = rotated(cosine[:, :, :128], sine[:, :, :128], value, -1.0) * potential
        value = jnp.concatenate([value, value * second_factor], axis=1)
        value = rotated(cosine, sine, value, 1.0)
        y_out[0, c] = value[:, :128].reshape(16, 16, 128)
        y_out[1, c] = value[:, 128:].reshape(16, 16, 128)
        seconds.start(c)
    seconds.start(2)
    seconds.start(3)

    loads["inverse_x"].wait()
    mixing = [mixing_factors(at.wave, c) for c in range(2)]

    def send_first(f, c, value):
        value = first_inverse(value, twiddle, kron, inverse_x)
        x_out[f, c] = value.reshape(16, 8, 256)
        lasts.start(LASTS.index((f, c)))

    for c in range(2):
        arrived(y_in.at[0, c], y_got.at[c])
        value = y_in[0, c].reshape(256, 128)
        send_first(0, c, value * mixing[c][0])
        send_first(2, c, value * mixing[c][1])
    for c in range(2):
        arrived(y_in.at[1, c], y_got.at[2 + c])
        send_first(1, c, y_in[1, c].reshape(256, 128))

    loads["inverse_z"].wait()
    turned = jnp.full((8, 256), step[0] % field_period, jnp.int32).astype(f32)
    turned = full_turn * turned / field_period
    applied = (jnp.cos(turned)[:1], jnp.sin(turned)[:1], None)
    square = jnp.zeros((256, 256), f32)
    source_swap.wait_recv()
    mine = source[pl.ds(here, 16)].reshape(256, 128).T
    theirs = source_in[...].reshape(256, 128).T
    weight = jnp.concatenate(
        [jnp.where(at.gz == 0, mine, theirs), jnp.where(at.gz == 0, theirs, mine)], axis=0
    )
    for f in ORDER:
        for c in range(2):
            arrived(x_in.at[f, c], x_got.at[LASTS.index((f, c))])
        field = mul(inverse_z, x_in[f].reshape(256, 256))
        if applied[f] is not None:
            field = field + applied[f]
        square = square + field * field
        zb_out[f] = mul(forward_z, weight * field).reshape(2, 16, 8, 256)
        for c in range(2):
            depths_back.start(BACK.index((f, c)))
    low, high = 0.5 * square[:128].T, 0.5 * square[128:].T
    mine, theirs = jnp.where(at.gz == 0, low, high), jnp.where(at.gz == 0, high, low)
    energy[0, pl.ds(1 + here, 16)] = mine.reshape(16, 16, 128)
    energy_out[...] = theirs.reshape(16, 16, 128)
    energy_swap.start()

    loads["forward_x"].wait()

    def first_of(f, c):
        arrived(zb_in.at[f, c], zb_got.at[BACK.index((f, c))])
        block = mul(forward_x, zb_in[f, c].reshape(128, 256))
        return first_forward(block, twiddle, kron)

    for c in range(2):
        value = first_of(0, c) * mixing[c][0] + first_of(2, c) * mixing[c][1]
        kb_out[0, c] = value.reshape(16, 16, 128)
        firsts_back.start(c)
    for c in range(2):
        kb_out[1, c] = first_of(1, c).reshape(16, 16, 128)
        firsts_back.start(2 + c)

    energy_swap.wait_recv()
    energy_halo.start()
    pl.when(in_lower)(lambda: depths.finish())
    pl.when(has_rows)(lambda: firsts.finish())
    for each in (seconds, lasts, depths_back, cell_halo):
        each.finish()
    source_swap.wait_send()
    energy_swap.wait_send()

    for c in range(2):
        potential, second_factor = factors[c]
        for f in range(2):
            arrived(kb_in.at[f, c], kb_got.at[2 * f + c])
        value = [kb_in[f, c].reshape(256, 128) for f in range(2)]
        value = rotated(cosine, sine, jnp.concatenate(value, axis=1), -1.0)
        value = (value[:, :128] + value[:, 128:] * second_factor) * potential
        value = rotated(cosine[:, :128], sine[:, :128], value, 1.0)
        yb_out[c] = value.reshape(8, 16, 128)
        seconds_back.start(c)
    firsts_back.finish()
    energy_halo.arrive(energy_wide)
    energy_rows(at, energy_halo, energy_wide, cells, next_out)
    energy_halo.finish()
    gradient_out[...] = jnp.zeros((32, 16, 128), f32)

    @pl.when(has_rows)
    def _():
        for c in range(2):
            arrived(yb_in.at[c], yb_got.at[c])
            value = yb_in[c].reshape(256, 128)
            value = first_inverse(value, twiddle, kron, inverse_x[:, :64]).reshape(4, 2, 8, 256)
            xb_out[c, :, :, :256] = value[:, 0]
            xb_out[c, :, :, 256:] = value[:, 1]
            lasts_back.start(c)

    @pl.when(in_lower)
    def _():
        for c in range(2):
            arrived(xb_in.at[c], xb_got.at[c])
        value = mul(inverse_z[:, :128], xb_in[...].reshape(256, 512)).T
        gradient_out[...] = (value * region(at, bounds)).reshape(32, 16, 128)

    seconds_back.finish()
    pl.when(has_rows)(lambda: lasts_back.finish())


VMEM_GRANT = 24 << 20
TABLES = (
    "forward_z", "inverse_z", "forward_x", "lower_x", "inverse_x", "twiddle",
    "kron", "second",
)


def on_device(velocity, adjoint_seed, susceptibility, remanence, region_bounds, step_id):
    tables = make_tables()
    shapes = [(2, 16, 8, 512), (2, 4, 8, 512), (2, 16, 16, 128), (2, 8, 16, 128)]
    shapes += [(2, 2, 16, 16, 128)] * 2 + [(3, 2, 16, 8, 256)] * 2
    shapes += [(3, 2, 16, 8, 256)] * 2 + [(2, 2, 16, 16, 128)] * 2
    shapes += [(2, 8, 16, 128), (2, 16, 16, 128), (2, 4, 8, 512), (2, 16, 8, 512)]
    for n in (7, 1):
        shapes += [(n, 34, 16, 128), (2, n, 32, 128), (2, n, 32, 128), (8, 512), (8, 512)]
        shapes += [(n, 32, 16, 128)]
    shapes += [(32, 16, 128)] + [(16, 16, 128)] * 2
    sems = []
    for n in (2, 2, 4, 6, 6, 4, 2, 2):
        sems += [(n, 16), (n,)]
    sems += [(5,)] * 4 + [(2,)] * 2
    vmem = pl.BlockSpec(memory_space=pltpu.VMEM)
    smem = pl.BlockSpec(memory_space=pltpu.SMEM)
    hbm = pl.BlockSpec(memory_space=pltpu.HBM)
    held = [pltpu.VMEM((32, 16, 128), f32)]
    held += [pltpu.VMEM(tables[n].shape, tables[n].dtype) for n in TABLES]
    operands = [velocity, adjoint_seed, susceptibility, remanence]
    operands += [jnp.asarray(tables[n]) for n in TABLES]
    operands = [pltpu.with_memory_space_constraint(x, pltpu.HBM) for x in operands]
    return pl.pallas_call(
        kernel,
        out_shape=(
            jax.ShapeDtypeStruct((3, 32, 16, 128), f32),
            jax.ShapeDtypeStruct((3, 32, 16, 128), f32),
            jax.ShapeDtypeStruct((32, 16, 128), f32),
        ),
        in_specs=[hbm] * (4 + len(TABLES)) + [smem] * 2,
        out_specs=(vmem, vmem, vmem),
        scratch_shapes=[pltpu.VMEM(s, f32) for s in shapes]
        + [pltpu.SemaphoreType.DMA(s) for s in sems]
        + held
        + [pltpu.SemaphoreType.DMA((12,))],
        compiler_params=pltpu.CompilerParams(
            collective_id=0, has_side_effects=True, vmem_limit_bytes=VMEM_GRANT
        ),
    )(*operands, region_bounds, step_id)


def solution(mesh):
    return jax.shard_map(
        on_device,
        mesh=mesh,
        in_specs=(
            P(None, "gx", "gy", "gz"),
            P(None, "gx", "gy", "gz"),
            P("gx", "gy", "gz"),
            P("gx", "gy", "gz"),
            P(),
            P(),
        ),
        out_specs=(P(None, "gx", "gy", "gz"), P(None, "gx", "gy", "gz"), P("gx", "gy", "gz")),
        check_vma=False,
    )
```

```python
import jax
import jax.numpy as jnp
import numpy as np
from jax import lax
from jax.experimental import pallas as pl
from jax.experimental.pallas import tpu as pltpu
from jax.sharding import PartitionSpec as P

time_step = 0.5
viscosity = 0.2
field_period = 24
full_turn = 6.283185307179586

bf16 = jnp.bfloat16
f32 = jnp.float32
MESH = pl.DeviceIdType.MESH


def pieces(matrix):
    matrix = np.asarray(matrix, np.float32)
    high = matrix.astype(jnp.bfloat16)
    low = (matrix - high.astype(np.float32)).astype(jnp.bfloat16)
    return np.stack([high, low])


def cut(value):
    high = value.astype(bf16)
    return high, (value - high.astype(f32)).astype(bf16)


def dot(left, right, dims=(((1,), (0,)), ((), ()))):
    return lax.dot_general(left, right, dims, preferred_element_type=f32)


def mul(matrix, value):
    high, low = cut(value)
    rows = matrix.shape[1]
    both = dot(matrix[...].reshape(2 * rows, matrix.shape[2]), high)
    return both[:rows] + both[rows:] + dot(matrix[0], low)


def make_tables():
    turn = 2.0 * np.pi / 256
    eye4, eye16 = np.eye(4), np.eye(16)
    c, s, j = np.arange(2)[:, None, None], np.arange(16)[:, None], np.arange(4)
    k3 = 1 + 8 * s + 4 * c + j
    z = np.arange(256)
    phase = turn * k3[..., None] * z
    forward_z = np.stack([np.cos(phase), -np.sin(phase)], 2).reshape(256, 256)
    weight = np.where(k3 == 128, 1.0, 2.0)[..., None] / 256.0**3
    both = np.stack([np.cos(phase) * weight, -np.sin(phase) * weight], 2)
    inverse_z = both.reshape(256, 256).T
    q, t, ka = np.arange(8), np.arange(2), np.arange(16)
    theta = turn * 16 * (2 * q[:, None, None] + t[None, :, None]) * ka
    c, s = np.cos(theta), np.sin(theta)
    turned = np.stack([np.stack([c, s]), np.stack([-s, c])])
    forward_x = np.einsum("abqtk,ji->akiqtbj", turned, eye4).reshape(128, 128)
    lower_x = np.einsum("abqtk,ji->akitqbj", turned[:, :, :4], eye4).reshape(128, 64)
    back = np.stack([np.stack([c, -s]), np.stack([s, c])])
    inverse_x = np.einsum("abqtk,ij->qtaibkj", back, eye4).reshape(128, 128)
    b = np.arange(16)
    phi = turn * ka[:, None] * b
    twiddle = np.stack([np.cos(phi), np.sin(phi)])[:, :, None, :, None]
    twiddle = np.broadcast_to(twiddle, (2, 16, 4, 16, 16)).reshape(2, 64, 256)
    angle = turn * 16 * b[:, None] * b
    kron = np.concatenate([np.kron(np.cos(angle), eye16), np.kron(np.sin(angle), eye16)], 1)
    k = np.arange(256)
    angle = turn * (k[:, None] * k % 256)
    return dict(
        forward_z=pieces(forward_z),
        inverse_z=pieces(inverse_z),
        forward_x=pieces(forward_x),
        lower_x=pieces(lower_x),
        inverse_x=pieces(inverse_x),
        twiddle=twiddle.astype(np.float32),
        kron=pieces(kron),
        second=np.stack([pieces(np.cos(angle)), pieces(np.sin(angle))]),
    )


def half_turned(value):
    return pltpu.roll(value, 64, 1)


def rotated(tables, value, direction):
    high, low = cut(value)
    rows, depth = tables.shape[2], tables.shape[3]
    both = dot(tables.reshape(4 * rows, depth), high)
    rest = dot(tables[:, 0].reshape(2 * rows, depth), low)
    first = both[:rows] + both[rows : 2 * rows] + rest[:rows]
    second = both[2 * rows : 3 * rows] + both[3 * rows :] + rest[rows:]
    lane = lax.broadcasted_iota(jnp.int32, (rows, 128), 1)
    sign = jnp.where(lane < 64, -direction, direction)
    blocks = [
        first[:, at : at + 128] + sign * half_turned(second[:, at : at + 128])
        for at in range(0, first.shape[1], 128)
    ]
    return blocks[0] if len(blocks) == 1 else jnp.concatenate(blocks, axis=1)


def depth_waves(block, forward_z):
    high, low = cut(block)
    dims = (((1,), (1,)), ((), ()))
    both = dot(forward_z.reshape(512, 128), high, dims)
    return both[:256] + both[256:] + dot(forward_z[0], low, dims)


def sixteenths(value, kron, direction):
    high, low = cut(value)
    both = dot(jnp.concatenate([high, low], axis=0), kron[0])
    both = both[:128] + both[128:] + dot(high, kron[1])
    first, second = both[:, :256], both[:, 256:]
    return jnp.concatenate(
        [first[:64] - direction * second[64:], first[64:] + direction * second[:64]], axis=0
    )


def first_forward(mixed, twiddle, kron):
    real, imag = mixed[:64], mixed[64:]
    c, s = twiddle[0], twiddle[1]
    turned = jnp.concatenate([real * c + imag * s, imag * c - real * s], axis=0)
    return sixteenths(turned, kron, -1.0).T


def first_inverse(value, twiddle, kron, inverse_x):
    turned = sixteenths(value.T, kron, 1.0)
    real, imag = turned[:64], turned[64:]
    c, s = twiddle[0], twiddle[1]
    turned = jnp.concatenate([real * c - imag * s, imag * c + real * s], axis=0)
    return mul(inverse_x, turned)


def halves_on_rows(block):
    return jnp.concatenate([block[:, :256], block[:, 256:]], axis=0)


def signed_wave(index):
    folded = jnp.where(index < 128, index, index - 256)
    return jnp.where(index == 128, 0, folded).astype(f32) * (full_turn / 256)


def factor_of(index, third):
    half = full_turn / 2
    return jnp.where(third == 128, jnp.where(index == 128, half, 0.0), signed_wave(index))


def wave_numbers(place, chunk):
    row = lax.broadcasted_iota(jnp.int32, (256, 128), 0)
    lane = lax.broadcasted_iota(jnp.int32, (256, 128), 1)
    return row, lane % 64 // 4, 1 + 8 * place + 4 * chunk + lane % 4


def spectral_factors(place, gy, chunk):
    row, low, third = wave_numbers(place, chunk)
    first = low + 16 * gy
    third_wave = third.astype(f32) * (full_turn / 256)
    fold = lambda i: jnp.where(i < 128, i, i - 256).astype(f32) * (full_turn / 256)
    first_wave, second_wave = fold(first), fold(row)
    square = first_wave * first_wave + second_wave * second_wave + third_wave * third_wave
    return -third_wave / square, factor_of(row, third)


def mixing_factors(place, chunk):
    row, low, third = wave_numbers(place, chunk)
    return factor_of(low + 16 * (row // 16), third), third.astype(f32) * (full_turn / 256)


UNROLL = 5
DEPTH = 2


class Place:
    def __init__(self):
        self.gx, self.gy, self.gz = (lax.axis_index(a) for a in ("gx", "gy", "gz"))
        self.wave = self.gx * 2 + self.gz

    def by_wave(self, wave):
        return (lax.div(wave, 2), self.gy, lax.rem(wave, 2))

    def by_second(self, second):
        return (self.gx, second, self.gz)

    def announce(self):
        barrier = pltpu.get_barrier_semaphore()

        def signal(step, carry):
            for target in (
                self.by_wave(lax.rem(self.wave + step, 16)),
                self.by_second(lax.rem(self.gy + step, 16)),
            ):
                pl.semaphore_signal(barrier, inc=1, device_id=target, device_id_type=MESH)
            return carry

        lax.fori_loop(1, 16, signal, 0, unroll=UNROLL)

    def meet(self):
        pl.semaphore_wait(pltpu.get_barrier_semaphore(), 30)


class Exchange:
    def __init__(self, me, device, src, dst, send_sem, recv_sem, wanted=None):
        self.me, self.device, self.src, self.dst = me, device, src, dst
        self.send_sem, self.recv_sem, self.wanted = send_sem, recv_sem, wanted

    def each(self, act):
        def body(step, carry):
            peer = lax.rem(self.me + step, 16)
            if self.wanted is None:
                act(peer)
            else:
                pl.when(self.wanted(peer))(lambda: act(peer))
            return carry

        lax.fori_loop(1, 16, body, 0, unroll=UNROLL)

    def copy(self, peer):
        return pltpu.make_async_remote_copy(
            src_ref=self.src(peer),
            dst_ref=self.dst,
            send_sem=self.send_sem(peer),
            recv_sem=self.recv_sem,
            device_id=self.device(peer),
            device_id_type=MESH,
        )

    def start(self, after=None):
        def act(peer):
            if after is not None:
                after.copy(peer).wait_send()
            self.copy(peer).start()

        own = pltpu.make_async_copy(self.src(self.me), self.dst, self.recv_sem)
        if self.wanted is None:
            own.start()
        else:
            pl.when(self.wanted(self.me))(lambda: own.start())
        self.each(act)

    def finish(self):
        self.each(lambda peer: self.copy(peer).wait_send())


class Chain:
    def __init__(self, exchanges):
        self.exchanges, self.count = exchanges, 0

    def start(self, number):
        before = self.exchanges[number - DEPTH] if number >= DEPTH else None
        assert number == self.count
        self.exchanges[number].start(before)
        self.count += 1

    def finish(self):
        for exchange in self.exchanges[-DEPTH:]:
            exchange.finish()


def arrived(buffer, sem):
    pltpu.make_async_copy(buffer, buffer, sem).wait()


def region(at, bounds):
    row = lax.broadcasted_iota(jnp.int32, (512, 128), 0)
    third = lax.broadcasted_iota(jnp.int32, (512, 128), 1) + at.gz * 128
    first, second = row // 16 + at.gx * 32, row % 16 + at.gy * 16
    inside = (first >= bounds[0, 0]) & (first < bounds[1, 0])
    inside = inside & (second >= bounds[0, 1]) & (second < bounds[1, 1])
    inside = inside & (third >= bounds[0, 2]) & (third < bounds[1, 2])
    return jnp.where(inside, 1.0, 0.0)


class Halo:
    def __init__(self, at, block, second_out, second_in, third_out, third_in, sent, got):
        self.at, self.block = at, block
        self.second_out, self.second_in = second_out, second_in
        self.third_out, self.third_in = third_out, third_in
        gx, gy, gz = at.gx, at.gy, at.gz
        self.copies = []
        for number, (src, dst, there, here, target) in enumerate(
            (
                (block.at[:, 32], block.at[:, 0], gx < 7, gx > 0, ((gx + 1) % 8, gy, gz)),
                (block.at[:, 1], block.at[:, 33], gx > 0, gx < 7, ((gx + 7) % 8, gy, gz)),
                (second_out.at[1], second_in.at[0], gy < 15, gy > 0, (gx, (gy + 1) % 16, gz)),
                (second_out.at[0], second_in.at[1], gy > 0, gy < 15, (gx, (gy + 15) % 16, gz)),
                (third_out, third_in, None, None, (gx, gy, 1 - gz)),
            )
        ):
            copy = pltpu.make_async_remote_copy(
                src_ref=src,
                dst_ref=dst,
                send_sem=sent.at[number],
                recv_sem=got.at[number],
                device_id=target,
                device_id_type=MESH,
            )
            self.copies.append((copy, there, here, dst))

    def start(self):
        block = self.block
        for face, row in ((0, 0), (1, 15)):
            self.second_out[face] = block[:, 1:33, row, :]
        for f in range(block.shape[0]):
            cells = block[f, 1:33].reshape(512, 128).T
            row = jnp.where(self.at.gz == 0, cells[127:128], cells[0:1])
            self.third_out[f : f + 1] = row
        for copy, there, here, dst in self.copies:
            if there is None:
                copy.start()
            else:
                pl.when(there)(lambda copy=copy: copy.start())

    def arrive(self, wide):
        for copy, there, here, dst in self.copies:
            if here is None:
                copy.wait_recv()
            else:
                pl.when(here)(lambda copy=copy: copy.wait_recv())

                @pl.when(jnp.logical_not(here))
                def _(dst=dst):
                    dst[...] = jnp.zeros(dst.shape, f32)

        for f in range(self.block.shape[0]):
            row = jnp.broadcast_to(self.third_in[f : f + 1], (128, 512))
            wide[f] = row.T.reshape(32, 16, 128)

    def finish(self):
        for copy, there, here, dst in self.copies:
            if there is None:
                copy.wait_send()
            else:
                pl.when(there)(lambda copy=copy: copy.wait_send())


def neighbours(at, halo, wide, f, i):
    block = halo.block
    here = block[f, i + 1]
    row = lax.broadcasted_iota(jnp.int32, (16, 128), 0)
    lane = lax.broadcasted_iota(jnp.int32, (16, 128), 1)
    below = halo.second_in[0, f, pl.ds(i, 1)]
    above = halo.second_in[1, f, pl.ds(i, 1)]
    side = wide[f, i]
    second = (
        jnp.where(row == 0, below, pltpu.roll(here, 1, 0)),
        jnp.where(row == 15, above, pltpu.roll(here, 15, 0)),
    )
    third = (
        jnp.where(lane == 0, jnp.where(at.gz == 1, side, 0.0), pltpu.roll(here, 1, 1)),
        jnp.where(lane == 127, jnp.where(at.gz == 0, side, 0.0), pltpu.roll(here, 127, 1)),
    )
    return here, ((block[f, i], block[f, i + 2]), second, third)


def laplace(here, around):
    total = -6.0 * here
    for low, high in around:
        total = total + (low + high)
    return total


def slope(pair):
    return (pair[1] - pair[0]) * 0.5


def cell_rows(at, halo, wide, next_out, adjoint_out, source):
    def body(i, carry):
        cells = [neighbours(at, halo, wide, f, i) for f in range(7)]
        velocity, seed = cells[:3], cells[3:6]
        suscept = cells[6]
        total = 0.0
        for d in range(3):
            pair = [suscept[1][d][e] * seed[d][1][d][e] for e in range(2)]
            total = total + slope(pair)
        source[i] = -time_step * total
        for k in range(3):
            here, around = velocity[k]
            advect = sum(velocity[j][0] * slope(around[j]) for j in range(3))
            next_out[k, i] = here + time_step * (viscosity * laplace(here, around) - advect)
            here, around = seed[k]
            shear = sum(seed[j][0] * slope(velocity[j][1][k]) for j in range(3))
            carried = sum(
                slope([velocity[j][1][j][e] * around[j][e] for e in range(2)]) for j in range(3)
            )
            adjoint_out[k, i] = here + time_step * (
                viscosity * laplace(here, around) - shear + carried
            )
        return carry

    lax.fori_loop(0, 32, body, 0)


def energy_rows(at, halo, wide, cells, next_out):
    def body(i, carry):
        _, around = neighbours(at, halo, wide, 0, i)
        scaled = time_step * cells[6, i + 1]
        for k in range(3):
            next_out[k, i] = next_out[k, i] + scaled * slope(around[k])
        return carry

    lax.fori_loop(0, 32, body, 0)


ORDER = (0, 2, 1)
CHUNKS = ((0,), (1,))
SECONDS = ((0, 0), (0, 1), (1, 0), (1, 1))
LASTS = ((0, 0), (2, 0), (0, 1), (2, 1), (1, 0), (1, 1))
BACK = ((0, 0), (0, 1), (2, 0), (2, 1), (1, 0), (1, 1))


def kernel(
    velocity, adjoint_seed, suscept, remanence_in,
    forward_z_in, inverse_z_in, forward_x_in, lower_x_in, inverse_x_in, twiddle_in, kron_in,
    second_in, bounds, step,
    next_out, adjoint_out, gradient_out,
    z_out, z_in, k_out, k_in, y_out, y_in, x_out, x_in,
    zb_out, zb_in, kb_out, kb_in, yb_out, yb_in, xb_out, xb_in,
    cells, cells_y_out, cells_y_in, cells_z_out, cells_z_in, cells_wide,
    energy, energy_y_out, energy_y_in, energy_z_out, energy_z_in, energy_wide, source,
    source_in, energy_out,
    z_sent, z_got, k_sent, k_got, y_sent, y_got, x_sent, x_got,
    zb_sent, zb_got, kb_sent, kb_got, yb_sent, yb_got, xb_sent, xb_got,
    cells_sent, cells_got, energy_sent, energy_got, swap_sent, swap_got,
    remanence, forward_z, inverse_z, forward_x, lower_x, inverse_x, twiddle, kron, second, loaded,
):
    at = Place()
    at.announce()
    loads = {}
    for number, (name, src, dst) in enumerate(
        (
            ("remanence", remanence_in, remanence),
            ("forward_z", forward_z_in, forward_z),
            ("velocity", velocity, cells.at[0:3, 1:33]),
            ("seed", adjoint_seed, cells.at[3:6, 1:33]),
            ("suscept", suscept, cells.at[6, 1:33]),
            ("lower_x", lower_x_in, lower_x),
            ("twiddle", twiddle_in, twiddle),
            ("kron", kron_in, kron),
            ("second", second_in, second),
            ("inverse_x", inverse_x_in, inverse_x),
            ("inverse_z", inverse_z_in, inverse_z),
            ("forward_x", forward_x_in, forward_x),
        )
    ):
        loads[name] = pltpu.make_async_copy(src, dst, loaded.at[number])
        loads[name].start()
    in_lower = (at.gx < 4) & (at.gy < 8) & (at.gz == 0)
    has_rows = at.gy < 8

    def over_waves(order, out, into, sent, got, block=lambda p: p, slot=None, wanted=None):
        slot = at.wave if slot is None else slot
        return Chain(
            [
                Exchange(
                    at.wave, at.by_wave, lambda p, k=k: out.at[*k, block(p)], into.at[*k, slot],
                    lambda p, n=n: sent.at[n, p], got.at[n], wanted,
                )
                for n, k in enumerate(order)
            ]
        )

    def over_seconds(order, out, into, sent, got, block=lambda p: p, slot=None, wanted=None):
        slot = at.gy if slot is None else slot
        return Chain(
            [
                Exchange(
                    at.gy, at.by_second, lambda p, k=k: out.at[*k, block(p)], into.at[*k, slot],
                    lambda p, n=n: sent.at[n, p], got.at[n], wanted,
                )
                for n, k in enumerate(order)
            ]
        )

    depths = over_waves(CHUNKS, z_out, z_in, z_sent, z_got, slot=lax.rem(at.gx, 4))
    firsts = over_seconds(CHUNKS, k_out, k_in, k_sent, k_got, slot=lax.rem(at.gy, 8))
    seconds = over_seconds(SECONDS, y_out, y_in, y_sent, y_got)
    lasts = over_waves(LASTS, x_out, x_in, x_sent, x_got)
    depths_back = over_waves(BACK, zb_out, zb_in, zb_sent, zb_got)
    firsts_back = over_seconds(SECONDS, kb_out, kb_in, kb_sent, kb_got)
    seconds_back = over_seconds(
        CHUNKS, yb_out, yb_in, yb_sent, yb_got, lambda p: lax.rem(p, 8), None, lambda p: p < 8
    )
    lasts_back = over_waves(
        CHUNKS, xb_out, xb_in, xb_sent, xb_got, lambda p: lax.rem(lax.div(p, 2), 4), None,
        lambda p: (p < 8) & (lax.rem(p, 2) == 0),
    )
    cell_halo = Halo(
        at, cells, cells_y_out, cells_y_in, cells_z_out, cells_z_in, cells_sent, cells_got
    )
    energy_halo = Halo(
        at, energy, energy_y_out, energy_y_in, energy_z_out, energy_z_in, energy_sent, energy_got
    )

    loads["remanence"].wait()
    loads["forward_z"].wait()

    @pl.when(in_lower)
    def _():
        magnet = remanence[...].reshape(512, 128) * region(at, bounds)
        z_out[...] = depth_waves(magnet, forward_z[:, :, :128]).reshape(2, 16, 8, 512)

    at.meet()

    @pl.when(in_lower)
    def _():
        depths.start(0)
        depths.start(1)

    for name in ("velocity", "seed", "suscept"):
        loads[name].wait()
    cell_halo.start()
    for name in ("lower_x", "twiddle", "kron"):
        loads[name].wait()

    @pl.when(has_rows)
    def _():
        for c in range(2):
            arrived(z_in.at[c], z_got.at[c])
            block = mul(lower_x, halves_on_rows(z_in[c].reshape(32, 512)))
            k_out[c] = first_forward(block, twiddle, kron).reshape(16, 16, 128)
            firsts.start(c)

    cell_halo.arrive(cells_wide)
    cell_rows(at, cell_halo, cells_wide, next_out, adjoint_out, source)
    here, there = at.gz * 16, (1 - at.gz) * 16
    source_swap = pltpu.make_async_remote_copy(
        src_ref=source.at[pl.ds(there, 16)],
        dst_ref=source_in,
        send_sem=swap_sent.at[0],
        recv_sem=swap_got.at[0],
        device_id=(at.gx, at.gy, 1 - at.gz),
        device_id_type=MESH,
    )
    energy_swap = pltpu.make_async_remote_copy(
        src_ref=energy_out,
        dst_ref=energy.at[0, pl.ds(1 + here, 16)],
        send_sem=swap_sent.at[1],
        recv_sem=swap_got.at[1],
        device_id=(at.gx, at.gy, 1 - at.gz),
        device_id_type=MESH,
    )
    source_swap.start()

    loads["second"].wait()
    factors = [spectral_factors(at.wave, at.gy, c) for c in range(2)]
    for c in range(2):
        potential, second_factor = factors[c]
        arrived(k_in.at[c], k_got.at[c])
        value = k_in[c].reshape(128, 128)
        value = rotated(second[:, :, :, :128], value, -1.0) * potential
        value = jnp.concatenate([value, value * second_factor], axis=1)
        value = rotated(second[...], value, 1.0)
        y_out[0, c] = value[:, :128].reshape(16, 16, 128)
        y_out[1, c] = value[:, 128:].reshape(16, 16, 128)
        seconds.start(c)
    seconds.start(2)
    seconds.start(3)

    loads["inverse_x"].wait()
    mixing = [mixing_factors(at.wave, c) for c in range(2)]

    def send_first(f, c, value):
        value = first_inverse(value, twiddle, kron, inverse_x)
        x_out[f, c] = value.reshape(16, 8, 256)
        lasts.start(LASTS.index((f, c)))

    for c in range(2):
        arrived(y_in.at[0, c], y_got.at[c])
        value = y_in[0, c].reshape(256, 128)
        send_first(0, c, value * mixing[c][0])
        send_first(2, c, value * mixing[c][1])
    for c in range(2):
        arrived(y_in.at[1, c], y_got.at[2 + c])
        send_first(1, c, y_in[1, c].reshape(256, 128))

    loads["inverse_z"].wait()
    turned = jnp.full((8, 256), step[0] % field_period, jnp.int32).astype(f32)
    turned = full_turn * turned / field_period
    applied = (jnp.cos(turned)[:1], jnp.sin(turned)[:1], None)
    square = jnp.zeros((256, 256), f32)
    source_swap.wait_recv()
    mine = source[pl.ds(here, 16)].reshape(256, 128).T
    theirs = source_in[...].reshape(256, 128).T
    weight = jnp.concatenate(
        [jnp.where(at.gz == 0, mine, theirs), jnp.where(at.gz == 0, theirs, mine)], axis=0
    )
    for f in ORDER:
        for c in range(2):
            arrived(x_in.at[f, c], x_got.at[LASTS.index((f, c))])
        field = mul(inverse_z, x_in[f].reshape(256, 256))
        if applied[f] is not None:
            field = field + applied[f]
        square = square + field * field
        zb_out[f] = mul(forward_z, weight * field).reshape(2, 16, 8, 256)
        for c in range(2):
            depths_back.start(BACK.index((f, c)))
    low, high = 0.5 * square[:128].T, 0.5 * square[128:].T
    mine, theirs = jnp.where(at.gz == 0, low, high), jnp.where(at.gz == 0, high, low)
    energy[0, pl.ds(1 + here, 16)] = mine.reshape(16, 16, 128)
    energy_out[...] = theirs.reshape(16, 16, 128)
    energy_swap.start()

    loads["forward_x"].wait()

    def first_of(f, c):
        arrived(zb_in.at[f, c], zb_got.at[BACK.index((f, c))])
        block = mul(forward_x, zb_in[f, c].reshape(128, 256))
        return first_forward(block, twiddle, kron)

    for c in range(2):
        value = first_of(0, c) * mixing[c][0] + first_of(2, c) * mixing[c][1]
        kb_out[0, c] = value.reshape(16, 16, 128)
        firsts_back.start(c)
    for c in range(2):
        kb_out[1, c] = first_of(1, c).reshape(16, 16, 128)
        firsts_back.start(2 + c)

    energy_swap.wait_recv()
    energy_halo.start()
    pl.when(in_lower)(lambda: depths.finish())
    pl.when(has_rows)(lambda: firsts.finish())
    for each in (seconds, lasts, depths_back, cell_halo):
        each.finish()
    source_swap.wait_send()
    energy_swap.wait_send()

    for c in range(2):
        potential, second_factor = factors[c]
        for f in range(2):
            arrived(kb_in.at[f, c], kb_got.at[2 * f + c])
        value = [kb_in[f, c].reshape(256, 128) for f in range(2)]
        value = rotated(second[...], jnp.concatenate(value, axis=1), -1.0)
        value = (value[:, :128] + value[:, 128:] * second_factor) * potential
        value = rotated(second[:, :, :128], value, 1.0)
        yb_out[c] = value.reshape(8, 16, 128)
        seconds_back.start(c)
    firsts_back.finish()
    energy_halo.arrive(energy_wide)
    energy_rows(at, energy_halo, energy_wide, cells, next_out)
    energy_halo.finish()
    gradient_out[...] = jnp.zeros((32, 16, 128), f32)

    @pl.when(has_rows)
    def _():
        for c in range(2):
            arrived(yb_in.at[c], yb_got.at[c])
            value = yb_in[c].reshape(256, 128)
            value = first_inverse(value, twiddle, kron, inverse_x[:, :64]).reshape(4, 2, 8, 256)
            xb_out[c, :, :, :256] = value[:, 0]
            xb_out[c, :, :, 256:] = value[:, 1]
            lasts_back.start(c)

    seconds_back.finish()
    pl.when(has_rows)(lambda: lasts_back.finish())

    @pl.when(in_lower)
    def _():
        for c in range(2):
            arrived(xb_in.at[c], xb_got.at[c])
        value = mul(inverse_z[:, :128], xb_in[...].reshape(256, 512)).T
        gradient_out[...] = (value * region(at, bounds)).reshape(32, 16, 128)


VMEM_GRANT = 24 << 20
TABLES = (
    "forward_z", "inverse_z", "forward_x", "lower_x", "inverse_x", "twiddle",
    "kron", "second",
)


def put_out(a_in, b_in, c_in, a_out, b_out, c_out, sems):
    pairs = ((a_in, a_out), (b_in, b_out), (c_in, c_out))
    copies = [pltpu.make_async_copy(*pair, sems.at[n]) for n, pair in enumerate(pairs)]
    for copy in copies:
        copy.start()
    for copy in copies:
        copy.wait()


def on_device(velocity, adjoint_seed, susceptibility, remanence, region_bounds, step_id):
    tables = make_tables()
    shapes = [(2, 16, 8, 512), (2, 4, 8, 512), (2, 16, 16, 128), (2, 8, 16, 128)]
    shapes += [(2, 2, 16, 16, 128)] * 2 + [(3, 2, 16, 8, 256)] * 2
    shapes += [(3, 2, 16, 8, 256)] * 2 + [(2, 2, 16, 16, 128)] * 2
    shapes += [(2, 8, 16, 128), (2, 16, 16, 128), (2, 4, 8, 512), (2, 16, 8, 512)]
    for n in (7, 1):
        shapes += [(n, 34, 16, 128), (2, n, 32, 128), (2, n, 32, 128), (8, 512), (8, 512)]
        shapes += [(n, 32, 16, 128)]
    shapes += [(32, 16, 128)] + [(16, 16, 128)] * 2
    sems = []
    for n in (2, 2, 4, 6, 6, 4, 2, 2):
        sems += [(n, 16), (n,)]
    sems += [(5,)] * 4 + [(2,)] * 2
    vmem = pl.BlockSpec(memory_space=pltpu.VMEM)
    smem = pl.BlockSpec(memory_space=pltpu.SMEM)
    hbm = pl.BlockSpec(memory_space=pltpu.HBM)
    held = [pltpu.VMEM((32, 16, 128), f32)]
    held += [pltpu.VMEM(tables[n].shape, tables[n].dtype) for n in TABLES]
    operands = [velocity, adjoint_seed, susceptibility, remanence]
    operands += [jnp.asarray(tables[n]) for n in TABLES]
    operands = [pltpu.with_memory_space_constraint(x, pltpu.HBM) for x in operands]
    results = pl.pallas_call(
        kernel,
        out_shape=(
            jax.ShapeDtypeStruct((3, 32, 16, 128), f32),
            jax.ShapeDtypeStruct((3, 32, 16, 128), f32),
            jax.ShapeDtypeStruct((32, 16, 128), f32),
        ),
        in_specs=[hbm] * (4 + len(TABLES)) + [smem] * 2,
        out_specs=(vmem, vmem, vmem),
        scratch_shapes=[pltpu.VMEM(s, f32) for s in shapes]
        + [pltpu.SemaphoreType.DMA(s) for s in sems]
        + held
        + [pltpu.SemaphoreType.DMA((12,))],
        compiler_params=pltpu.CompilerParams(
            collective_id=0, has_side_effects=True, vmem_limit_bytes=VMEM_GRANT
        ),
    )(*operands, region_bounds, step_id)
    anywhere = pl.BlockSpec(memory_space=pl.ANY)
    return pl.pallas_call(
        put_out,
        out_shape=[jax.ShapeDtypeStruct(r.shape, f32) for r in results],
        in_specs=[anywhere] * 3,
        out_specs=[hbm] * 3,
        scratch_shapes=[pltpu.SemaphoreType.DMA((3,))],
        compiler_params=pltpu.CompilerParams(vmem_limit_bytes=1 << 20),
    )(*results)


def solution(mesh):
    return jax.shard_map(
        on_device,
        mesh=mesh,
        in_specs=(
            P(None, "gx", "gy", "gz"),
            P(None, "gx", "gy", "gz"),
            P("gx", "gy", "gz"),
            P("gx", "gy", "gz"),
            P(),
            P(),
        ),
        out_specs=(P(None, "gx", "gy", "gz"), P(None, "gx", "gy", "gz"), P("gx", "gy", "gz")),
        check_vma=False,
    )
```

```python
import jax
import jax.numpy as jnp
import numpy as np
from jax import lax
from jax.experimental import pallas as pl
from jax.experimental.pallas import tpu as pltpu
from jax.sharding import PartitionSpec as P

time_step = 0.5
viscosity = 0.2
field_period = 24
full_turn = 6.283185307179586

bf16 = jnp.bfloat16
f32 = jnp.float32
MESH = pl.DeviceIdType.MESH


def pieces(matrix):
    matrix = np.asarray(matrix, np.float32)
    high = matrix.astype(jnp.bfloat16)
    low = (matrix - high.astype(np.float32)).astype(jnp.bfloat16)
    return np.stack([high, low])


def cut(value):
    high = value.astype(bf16)
    return high, (value - high.astype(f32)).astype(bf16)


def dot(left, right, dims=(((1,), (0,)), ((), ()))):
    return lax.dot_general(left, right, dims, preferred_element_type=f32)


def mul(matrix, value):
    high, low = cut(value)
    rows = matrix.shape[1]
    both = dot(matrix[...].reshape(2 * rows, matrix.shape[2]), high)
    return both[:rows] + both[rows:] + dot(matrix[0], low)


def make_tables():
    turn = 2.0 * np.pi / 256
    eye4, eye16 = np.eye(4), np.eye(16)
    c, s, j = np.arange(2)[:, None, None], np.arange(16)[:, None], np.arange(4)
    k3 = 1 + 8 * s + 4 * c + j
    z = np.arange(256)
    phase = turn * k3[..., None] * z
    forward_z = np.stack([np.cos(phase), -np.sin(phase)], 2).reshape(256, 256)
    weight = np.where(k3 == 128, 1.0, 2.0)[..., None] / 256.0**3
    both = np.stack([np.cos(phase) * weight, -np.sin(phase) * weight], 2)
    inverse_z = both.reshape(256, 256).T
    q, t, ka = np.arange(8), np.arange(2), np.arange(16)
    theta = turn * 16 * (2 * q[:, None, None] + t[None, :, None]) * ka
    c, s = np.cos(theta), np.sin(theta)
    turned = np.stack([np.stack([c, s]), np.stack([-s, c])])
    forward_x = np.einsum("abqtk,ji->akiqtbj", turned, eye4).reshape(128, 128)
    lower_x = np.einsum("abqtk,ji->akitqbj", turned[:, :, :4], eye4).reshape(128, 64)
    back = np.stack([np.stack([c, -s]), np.stack([s, c])])
    inverse_x = np.einsum("abqtk,ij->qtaibkj", back, eye4).reshape(128, 128)
    b = np.arange(16)
    phi = turn * ka[:, None] * b
    twiddle = np.stack([np.cos(phi), np.sin(phi)])[:, :, None, :, None]
    twiddle = np.broadcast_to(twiddle, (2, 16, 4, 16, 16)).reshape(2, 64, 256)
    angle = turn * 16 * b[:, None] * b
    kron = np.concatenate([np.kron(np.cos(angle), eye16), np.kron(np.sin(angle), eye16)], 1)
    k = np.arange(256)
    angle = turn * (k[:, None] * k % 256)
    return dict(
        forward_z=pieces(forward_z),
        inverse_z=pieces(inverse_z),
        forward_x=pieces(forward_x),
        lower_x=pieces(lower_x),
        inverse_x=pieces(inverse_x),
        twiddle=twiddle.astype(np.float32),
        kron=pieces(kron),
        second=np.stack([pieces(np.cos(angle)), pieces(np.sin(angle))]),
    )


def half_turned(value):
    return pltpu.roll(value, 64, 1)


def rotated(tables, value, direction):
    high, low = cut(value)
    rows, depth = tables.shape[2], tables.shape[3]
    both = dot(tables.reshape(4 * rows, depth), high)
    rest = dot(tables[:, 0].reshape(2 * rows, depth), low)
    first = both[:rows] + both[rows : 2 * rows] + rest[:rows]
    second = both[2 * rows : 3 * rows] + both[3 * rows :] + rest[rows:]
    lane = lax.broadcasted_iota(jnp.int32, (rows, 128), 1)
    sign = jnp.where(lane < 64, -direction, direction)
    blocks = [
        first[:, at : at + 128] + sign * half_turned(second[:, at : at + 128])
        for at in range(0, first.shape[1], 128)
    ]
    return blocks[0] if len(blocks) == 1 else jnp.concatenate(blocks, axis=1)


def depth_waves(block, forward_z):
    high, low = cut(block)
    dims = (((1,), (1,)), ((), ()))
    both = dot(forward_z.reshape(256, 128), high, dims)
    return both[:128] + both[128:] + dot(forward_z[0], low, dims)


def sixteenths(value, kron, direction):
    high, low = cut(value)
    both = dot(jnp.concatenate([high, low], axis=0), kron[0])
    both = both[:128] + both[128:] + dot(high, kron[1])
    first, second = both[:, :256], both[:, 256:]
    return jnp.concatenate(
        [first[:64] - direction * second[64:], first[64:] + direction * second[:64]], axis=0
    )


def first_forward(mixed, twiddle, kron):
    real, imag = mixed[:64], mixed[64:]
    c, s = twiddle[0], twiddle[1]
    turned = jnp.concatenate([real * c + imag * s, imag * c - real * s], axis=0)
    return sixteenths(turned, kron, -1.0).T


def first_inverse(value, twiddle, kron, inverse_x):
    turned = sixteenths(value.T, kron, 1.0)
    real, imag = turned[:64], turned[64:]
    c, s = twiddle[0], twiddle[1]
    turned = jnp.concatenate([real * c - imag * s, imag * c + real * s], axis=0)
    return mul(inverse_x, turned)


def halves_on_rows(block):
    return jnp.concatenate([block[:, :256], block[:, 256:]], axis=0)


def signed_wave(index):
    folded = jnp.where(index < 128, index, index - 256)
    return jnp.where(index == 128, 0, folded).astype(f32) * (full_turn / 256)


def factor_of(index, third):
    half = full_turn / 2
    return jnp.where(third == 128, jnp.where(index == 128, half, 0.0), signed_wave(index))


def wave_numbers(place, chunk):
    row = lax.broadcasted_iota(jnp.int32, (256, 128), 0)
    lane = lax.broadcasted_iota(jnp.int32, (256, 128), 1)
    return row, lane % 64 // 4, 1 + 8 * place + 4 * chunk + lane % 4


def spectral_factors(place, gy, chunk):
    row, low, third = wave_numbers(place, chunk)
    first = low + 16 * gy
    third_wave = third.astype(f32) * (full_turn / 256)
    fold = lambda i: jnp.where(i < 128, i, i - 256).astype(f32) * (full_turn / 256)
    first_wave, second_wave = fold(first), fold(row)
    square = first_wave * first_wave + second_wave * second_wave + third_wave * third_wave
    return -third_wave / square, factor_of(row, third)


def mixing_factors(place, chunk):
    row, low, third = wave_numbers(place, chunk)
    return factor_of(low + 16 * (row // 16), third), third.astype(f32) * (full_turn / 256)


UNROLL = 5
DEPTH = 3


class Place:
    def __init__(self):
        self.gx, self.gy, self.gz = (lax.axis_index(a) for a in ("gx", "gy", "gz"))
        self.wave = self.gx * 2 + self.gz

    def by_wave(self, wave):
        return (lax.div(wave, 2), self.gy, lax.rem(wave, 2))

    def by_second(self, second):
        return (self.gx, second, self.gz)

    def announce(self):
        barrier = pltpu.get_barrier_semaphore()

        def signal(step, carry):
            for target in (
                self.by_wave(lax.rem(self.wave + step, 16)),
                self.by_second(lax.rem(self.gy + step, 16)),
            ):
                pl.semaphore_signal(barrier, inc=1, device_id=target, device_id_type=MESH)
            return carry

        lax.fori_loop(1, 16, signal, 0, unroll=UNROLL)

    def meet(self):
        pl.semaphore_wait(pltpu.get_barrier_semaphore(), 30)


class Exchange:
    def __init__(self, me, device, src, dst, send_sem, recv_sem, wanted=None):
        self.me, self.device, self.src, self.dst = me, device, src, dst
        self.send_sem, self.recv_sem, self.wanted = send_sem, recv_sem, wanted

    def each(self, act):
        def body(step, carry):
            peer = lax.rem(self.me + step, 16)
            if self.wanted is None:
                act(peer)
            else:
                pl.when(self.wanted(peer))(lambda: act(peer))
            return carry

        lax.fori_loop(1, 16, body, 0, unroll=UNROLL)

    def copy(self, peer):
        return pltpu.make_async_remote_copy(
            src_ref=self.src(peer),
            dst_ref=self.dst,
            send_sem=self.send_sem(peer),
            recv_sem=self.recv_sem,
            device_id=self.device(peer),
            device_id_type=MESH,
        )

    def start(self, after=None):
        def act(peer):
            if after is not None:
                after.copy(peer).wait_send()
            self.copy(peer).start()

        own = pltpu.make_async_copy(self.src(self.me), self.dst, self.recv_sem)
        if self.wanted is None:
            own.start()
        else:
            pl.when(self.wanted(self.me))(lambda: own.start())
        self.each(act)

    def finish(self):
        self.each(lambda peer: self.copy(peer).wait_send())


class Chain:
    def __init__(self, exchanges):
        self.exchanges, self.count = exchanges, 0

    def start(self, number):
        before = self.exchanges[number - DEPTH] if number >= DEPTH else None
        assert number == self.count
        self.exchanges[number].start(before)
        self.count += 1

    def finish(self):
        for exchange in self.exchanges[-DEPTH:]:
            exchange.finish()


def arrived(buffer, sem):
    pltpu.make_async_copy(buffer, buffer, sem).wait()


def region(at, bounds):
    row = lax.broadcasted_iota(jnp.int32, (512, 128), 0)
    third = lax.broadcasted_iota(jnp.int32, (512, 128), 1) + at.gz * 128
    first, second = row // 16 + at.gx * 32, row % 16 + at.gy * 16
    inside = (first >= bounds[0, 0]) & (first < bounds[1, 0])
    inside = inside & (second >= bounds[0, 1]) & (second < bounds[1, 1])
    inside = inside & (third >= bounds[0, 2]) & (third < bounds[1, 2])
    return jnp.where(inside, 1.0, 0.0)


class Halo:
    def __init__(self, at, block, second_out, second_in, third_out, third_in, sent, got):
        self.at, self.block = at, block
        self.second_out, self.second_in = second_out, second_in
        self.third_out, self.third_in = third_out, third_in
        gx, gy, gz = at.gx, at.gy, at.gz
        self.copies = []
        for number, (src, dst, there, here, target) in enumerate(
            (
                (block.at[:, 32], block.at[:, 0], gx < 7, gx > 0, ((gx + 1) % 8, gy, gz)),
                (block.at[:, 1], block.at[:, 33], gx > 0, gx < 7, ((gx + 7) % 8, gy, gz)),
                (second_out.at[1], second_in.at[0], gy < 15, gy > 0, (gx, (gy + 1) % 16, gz)),
                (second_out.at[0], second_in.at[1], gy > 0, gy < 15, (gx, (gy + 15) % 16, gz)),
                (third_out, third_in, None, None, (gx, gy, 1 - gz)),
            )
        ):
            copy = pltpu.make_async_remote_copy(
                src_ref=src,
                dst_ref=dst,
                send_sem=sent.at[number],
                recv_sem=got.at[number],
                device_id=target,
                device_id_type=MESH,
            )
            self.copies.append((copy, there, here, dst))

    def start(self):
        block = self.block
        for face, row in ((0, 0), (1, 15)):
            self.second_out[face] = block[:, 1:33, row, :]
        for f in range(block.shape[0]):
            cells = block[f, 1:33].reshape(512, 128).T
            row = jnp.where(self.at.gz == 0, cells[127:128], cells[0:1])
            self.third_out[f : f + 1] = row
        for copy, there, here, dst in self.copies:
            if there is None:
                copy.start()
            else:
                pl.when(there)(lambda copy=copy: copy.start())

    def arrive(self, wide):
        for copy, there, here, dst in self.copies:
            if here is None:
                copy.wait_recv()
            else:
                pl.when(here)(lambda copy=copy: copy.wait_recv())

                @pl.when(jnp.logical_not(here))
                def _(dst=dst):
                    dst[...] = jnp.zeros(dst.shape, f32)

        for f in range(self.block.shape[0]):
            row = jnp.broadcast_to(self.third_in[f : f + 1], (128, 512))
            wide[f] = row.T.reshape(32, 16, 128)

    def finish(self):
        for copy, there, here, dst in self.copies:
            if there is None:
                copy.wait_send()
            else:
                pl.when(there)(lambda copy=copy: copy.wait_send())


def neighbours(at, halo, wide, f, i):
    block = halo.block
    here = block[f, i + 1]
    row = lax.broadcasted_iota(jnp.int32, (16, 128), 0)
    lane = lax.broadcasted_iota(jnp.int32, (16, 128), 1)
    below = halo.second_in[0, f, pl.ds(i, 1)]
    above = halo.second_in[1, f, pl.ds(i, 1)]
    side = wide[f, i]
    second = (
        jnp.where(row == 0, below, pltpu.roll(here, 1, 0)),
        jnp.where(row == 15, above, pltpu.roll(here, 15, 0)),
    )
    third = (
        jnp.where(lane == 0, jnp.where(at.gz == 1, side, 0.0), pltpu.roll(here, 1, 1)),
        jnp.where(lane == 127, jnp.where(at.gz == 0, side, 0.0), pltpu.roll(here, 127, 1)),
    )
    return here, ((block[f, i], block[f, i + 2]), second, third)


def laplace(here, around):
    total = -6.0 * here
    for low, high in around:
        total = total + (low + high)
    return total


def slope(pair):
    return (pair[1] - pair[0]) * 0.5


def cell_rows(at, halo, wide, next_out, adjoint_out, source):
    def body(i, carry):
        cells = [neighbours(at, halo, wide, f, i) for f in range(7)]
        velocity, seed = cells[:3], cells[3:6]
        suscept = cells[6]
        total = 0.0
        for d in range(3):
            pair = [suscept[1][d][e] * seed[d][1][d][e] for e in range(2)]
            total = total + slope(pair)
        source[i] = -time_step * total
        for k in range(3):
            here, around = velocity[k]
            advect = sum(velocity[j][0] * slope(around[j]) for j in range(3))
            next_out[k, i] = here + time_step * (viscosity * laplace(here, around) - advect)
            here, around = seed[k]
            shear = sum(seed[j][0] * slope(velocity[j][1][k]) for j in range(3))
            carried = sum(
                slope([velocity[j][1][j][e] * around[j][e] for e in range(2)]) for j in range(3)
            )
            adjoint_out[k, i] = here + time_step * (
                viscosity * laplace(here, around) - shear + carried
            )
        return carry

    lax.fori_loop(0, 32, body, 0)


def energy_rows(at, halo, wide, cells, next_out):
    def body(i, carry):
        _, around = neighbours(at, halo, wide, 0, i)
        scaled = time_step * cells[6, i + 1]
        for k in range(3):
            next_out[k, i] = next_out[k, i] + scaled * slope(around[k])
        return carry

    lax.fori_loop(0, 32, body, 0)


ORDER = (0, 2, 1)
CHUNKS = ((0,), (1,))
SECONDS = ((0, 0), (0, 1), (1, 0), (1, 1))
LASTS = ((0, 0), (2, 0), (0, 1), (2, 1), (1, 0), (1, 1))
BACK = ((0, 0), (0, 1), (2, 0), (2, 1), (1, 0), (1, 1))


def kernel(
    velocity, adjoint_seed, suscept, remanence_in,
    forward_z_in, inverse_z_in, forward_x_in, lower_x_in, inverse_x_in, twiddle_in, kron_in,
    second_in, bounds, step,
    next_out, adjoint_out, gradient_out,
    z_out, z_in, k_out, k_in, y_out, y_in, x_out, x_in,
    zb_out, zb_in, kb_out, kb_in, yb_out, yb_in, xb_out, xb_in,
    cells, cells_y_out, cells_y_in, cells_z_out, cells_z_in, cells_wide,
    energy, energy_y_out, energy_y_in, energy_z_out, energy_z_in, energy_wide, source,
    source_in, energy_out,
    z_sent, z_got, k_sent, k_got, y_sent, y_got, x_sent, x_got,
    zb_sent, zb_got, kb_sent, kb_got, yb_sent, yb_got, xb_sent, xb_got,
    cells_sent, cells_got, energy_sent, energy_got, swap_sent, swap_got,
    remanence, forward_z, inverse_z, forward_x, lower_x, inverse_x, twiddle, kron, second, loaded,
):
    at = Place()
    at.announce()
    loads = {}
    for number, (name, src, dst) in enumerate(
        (
            ("remanence", remanence_in, remanence),
            ("forward_z", forward_z_in, forward_z),
            ("velocity", velocity, cells.at[0:3, 1:33]),
            ("seed", adjoint_seed, cells.at[3:6, 1:33]),
            ("suscept", suscept, cells.at[6, 1:33]),
            ("lower_x", lower_x_in, lower_x),
            ("twiddle", twiddle_in, twiddle),
            ("kron", kron_in, kron),
            ("second", second_in, second),
            ("inverse_x", inverse_x_in, inverse_x),
            ("inverse_z", inverse_z_in, inverse_z),
            ("forward_x", forward_x_in, forward_x),
        )
    ):
        loads[name] = pltpu.make_async_copy(src, dst, loaded.at[number])
        loads[name].start()
    in_lower = (at.gx < 4) & (at.gy < 8) & (at.gz == 0)
    has_rows = at.gy < 8

    def over_waves(order, out, into, sent, got, block=lambda p: p, slot=None, wanted=None):
        slot = at.wave if slot is None else slot
        return Chain(
            [
                Exchange(
                    at.wave, at.by_wave, lambda p, k=k: out.at[*k, block(p)], into.at[*k, slot],
                    lambda p, n=n: sent.at[n, p], got.at[n], wanted,
                )
                for n, k in enumerate(order)
            ]
        )

    def over_seconds(order, out, into, sent, got, block=lambda p: p, slot=None, wanted=None):
        slot = at.gy if slot is None else slot
        return Chain(
            [
                Exchange(
                    at.gy, at.by_second, lambda p, k=k: out.at[*k, block(p)], into.at[*k, slot],
                    lambda p, n=n: sent.at[n, p], got.at[n], wanted,
                )
                for n, k in enumerate(order)
            ]
        )

    depths = over_waves(CHUNKS, z_out, z_in, z_sent, z_got, slot=lax.rem(at.gx, 4))
    firsts = over_seconds(CHUNKS, k_out, k_in, k_sent, k_got, slot=lax.rem(at.gy, 8))
    seconds = over_seconds(SECONDS, y_out, y_in, y_sent, y_got)
    lasts = over_waves(LASTS, x_out, x_in, x_sent, x_got)
    depths_back = over_waves(BACK, zb_out, zb_in, zb_sent, zb_got)
    firsts_back = over_seconds(SECONDS, kb_out, kb_in, kb_sent, kb_got)
    seconds_back = over_seconds(
        CHUNKS, yb_out, yb_in, yb_sent, yb_got, lambda p: lax.rem(p, 8), None, lambda p: p < 8
    )
    lasts_back = over_waves(
        CHUNKS, xb_out, xb_in, xb_sent, xb_got, lambda p: lax.rem(lax.div(p, 2), 4), None,
        lambda p: (p < 8) & (lax.rem(p, 2) == 0),
    )
    cell_halo = Halo(
        at, cells, cells_y_out, cells_y_in, cells_z_out, cells_z_in, cells_sent, cells_got
    )
    energy_halo = Halo(
        at, energy, energy_y_out, energy_y_in, energy_z_out, energy_z_in, energy_sent, energy_got
    )

    loads["remanence"].wait()
    loads["forward_z"].wait()

    @pl.when(in_lower)
    def _():
        magnet = remanence[...].reshape(512, 128) * region(at, bounds)
        remanence[...] = magnet.reshape(32, 16, 128)
        z_out[0] = depth_waves(magnet, forward_z[:, :128, :128]).reshape(16, 8, 512)

    at.meet()

    @pl.when(in_lower)
    def _():
        depths.start(0)
        magnet = remanence[...].reshape(512, 128)
        z_out[1] = depth_waves(magnet, forward_z[:, 128:, :128]).reshape(16, 8, 512)
        depths.start(1)

    for name in ("velocity", "seed", "suscept"):
        loads[name].wait()
    cell_halo.start()
    for name in ("lower_x", "twiddle", "kron"):
        loads[name].wait()

    @pl.when(has_rows)
    def _():
        for c in range(2):
            arrived(z_in.at[c], z_got.at[c])
            block = mul(lower_x, halves_on_rows(z_in[c].reshape(32, 512)))
            k_out[c] = first_forward(block, twiddle, kron).reshape(16, 16, 128)
            firsts.start(c)

    cell_halo.arrive(cells_wide)
    cell_rows(at, cell_halo, cells_wide, next_out, adjoint_out, source)
    here, there = at.gz * 16, (1 - at.gz) * 16
    source_swap = pltpu.make_async_remote_copy(
        src_ref=source.at[pl.ds(there, 16)],
        dst_ref=source_in,
        send_sem=swap_sent.at[0],
        recv_sem=swap_got.at[0],
        device_id=(at.gx, at.gy, 1 - at.gz),
        device_id_type=MESH,
    )
    energy_swap = pltpu.make_async_remote_copy(
        src_ref=energy_out,
        dst_ref=energy.at[0, pl.ds(1 + here, 16)],
        send_sem=swap_sent.at[1],
        recv_sem=swap_got.at[1],
        device_id=(at.gx, at.gy, 1 - at.gz),
        device_id_type=MESH,
    )
    source_swap.start()

    loads["second"].wait()
    factors = [spectral_factors(at.wave, at.gy, c) for c in range(2)]
    for c in range(2):
        potential, second_factor = factors[c]
        arrived(k_in.at[c], k_got.at[c])
        value = k_in[c].reshape(128, 128)
        value = rotated(second[:, :, :, :128], value, -1.0) * potential
        value = jnp.concatenate([value, value * second_factor], axis=1)
        value = rotated(second[...], value, 1.0)
        y_out[0, c] = value[:, :128].reshape(16, 16, 128)
        y_out[1, c] = value[:, 128:].reshape(16, 16, 128)
        seconds.start(c)
    seconds.start(2)
    seconds.start(3)

    loads["inverse_x"].wait()
    mixing = [mixing_factors(at.wave, c) for c in range(2)]

    def send_first(f, c, value):
        value = first_inverse(value, twiddle, kron, inverse_x)
        x_out[f, c] = value.reshape(16, 8, 256)
        lasts.start(LASTS.index((f, c)))

    for c in range(2):
        arrived(y_in.at[0, c], y_got.at[c])
        value = y_in[0, c].reshape(256, 128)
        send_first(0, c, value * mixing[c][0])
        send_first(2, c, value * mixing[c][1])
    for c in range(2):
        arrived(y_in.at[1, c], y_got.at[2 + c])
        send_first(1, c, y_in[1, c].reshape(256, 128))

    loads["inverse_z"].wait()
    turned = jnp.full((8, 256), step[0] % field_period, jnp.int32).astype(f32)
    turned = full_turn * turned / field_period
    applied = (jnp.cos(turned)[:1], jnp.sin(turned)[:1], None)
    square = jnp.zeros((256, 256), f32)
    source_swap.wait_recv()
    mine = source[pl.ds(here, 16)].reshape(256, 128).T
    theirs = source_in[...].reshape(256, 128).T
    weight = jnp.concatenate(
        [jnp.where(at.gz == 0, mine, theirs), jnp.where(at.gz == 0, theirs, mine)], axis=0
    )
    for f in ORDER:
        for c in range(2):
            arrived(x_in.at[f, c], x_got.at[LASTS.index((f, c))])
        field = mul(inverse_z, x_in[f].reshape(256, 256))
        if applied[f] is not None:
            field = field + applied[f]
        square = square + field * field
        zb_out[f] = mul(forward_z, weight * field).reshape(2, 16, 8, 256)
        for c in range(2):
            depths_back.start(BACK.index((f, c)))
    low, high = 0.5 * square[:128].T, 0.5 * square[128:].T
    mine, theirs = jnp.where(at.gz == 0, low, high), jnp.where(at.gz == 0, high, low)
    energy[0, pl.ds(1 + here, 16)] = mine.reshape(16, 16, 128)
    energy_out[...] = theirs.reshape(16, 16, 128)
    energy_swap.start()

    loads["forward_x"].wait()

    def first_of(f, c):
        arrived(zb_in.at[f, c], zb_got.at[BACK.index((f, c))])
        block = mul(forward_x, zb_in[f, c].reshape(128, 256))
        return first_forward(block, twiddle, kron)

    for c in range(2):
        value = first_of(0, c) * mixing[c][0] + first_of(2, c) * mixing[c][1]
        kb_out[0, c] = value.reshape(16, 16, 128)
        firsts_back.start(c)
    for c in range(2):
        kb_out[1, c] = first_of(1, c).reshape(16, 16, 128)
        firsts_back.start(2 + c)

    energy_swap.wait_recv()
    energy_halo.start()
    pl.when(in_lower)(lambda: depths.finish())
    pl.when(has_rows)(lambda: firsts.finish())
    for each in (seconds, lasts, depths_back, cell_halo):
        each.finish()
    source_swap.wait_send()
    energy_swap.wait_send()

    for c in range(2):
        potential, second_factor = factors[c]
        for f in range(2):
            arrived(kb_in.at[f, c], kb_got.at[2 * f + c])
        value = [kb_in[f, c].reshape(256, 128) for f in range(2)]
        value = rotated(second[...], jnp.concatenate(value, axis=1), -1.0)
        value = (value[:, :128] + value[:, 128:] * second_factor) * potential
        value = rotated(second[:, :, :128], value, 1.0)
        yb_out[c] = value.reshape(8, 16, 128)
        seconds_back.start(c)
    firsts_back.finish()
    energy_halo.arrive(energy_wide)
    energy_rows(at, energy_halo, energy_wide, cells, next_out)
    energy_halo.finish()
    gradient_out[...] = jnp.zeros((32, 16, 128), f32)

    @pl.when(has_rows)
    def _():
        for c in range(2):
            arrived(yb_in.at[c], yb_got.at[c])
            value = yb_in[c].reshape(256, 128)
            value = first_inverse(value, twiddle, kron, inverse_x[:, :64]).reshape(4, 2, 8, 256)
            xb_out[c, :, :, :256] = value[:, 0]
            xb_out[c, :, :, 256:] = value[:, 1]
            lasts_back.start(c)

    seconds_back.finish()
    pl.when(has_rows)(lambda: lasts_back.finish())

    @pl.when(in_lower)
    def _():
        inside = region(at, bounds)
        value = 0.0
        for c in range(2):
            arrived(xb_in.at[c], xb_got.at[c])
            table = inverse_z[:, :128, 128 * c : 128 * (c + 1)]
            value = value + mul(table, xb_in[c].reshape(128, 512))
        gradient_out[...] = (value.T * inside).reshape(32, 16, 128)


VMEM_GRANT = 24 << 20
TABLES = (
    "forward_z", "inverse_z", "forward_x", "lower_x", "inverse_x", "twiddle",
    "kron", "second",
)


def put_out(a_in, b_in, c_in, a_out, b_out, c_out, sems):
    pairs = ((a_in, a_out), (b_in, b_out), (c_in, c_out))
    copies = [pltpu.make_async_copy(*pair, sems.at[n]) for n, pair in enumerate(pairs)]
    for copy in copies:
        copy.start()
    for copy in copies:
        copy.wait()


def on_device(velocity, adjoint_seed, susceptibility, remanence, region_bounds, step_id):
    tables = make_tables()
    shapes = [(2, 16, 8, 512), (2, 4, 8, 512), (2, 16, 16, 128), (2, 8, 16, 128)]
    shapes += [(2, 2, 16, 16, 128)] * 2 + [(3, 2, 16, 8, 256)] * 2
    shapes += [(3, 2, 16, 8, 256)] * 2 + [(2, 2, 16, 16, 128)] * 2
    shapes += [(2, 8, 16, 128), (2, 16, 16, 128), (2, 4, 8, 512), (2, 16, 8, 512)]
    for n in (7, 1):
        shapes += [(n, 34, 16, 128), (2, n, 32, 128), (2, n, 32, 128), (8, 512), (8, 512)]
        shapes += [(n, 32, 16, 128)]
    shapes += [(32, 16, 128)] + [(16, 16, 128)] * 2
    sems = []
    for n in (2, 2, 4, 6, 6, 4, 2, 2):
        sems += [(n, 16), (n,)]
    sems += [(5,)] * 4 + [(2,)] * 2
    vmem = pl.BlockSpec(memory_space=pltpu.VMEM)
    smem = pl.BlockSpec(memory_space=pltpu.SMEM)
    hbm = pl.BlockSpec(memory_space=pltpu.HBM)
    held = [pltpu.VMEM((32, 16, 128), f32)]
    held += [pltpu.VMEM(tables[n].shape, tables[n].dtype) for n in TABLES]
    operands = [velocity, adjoint_seed, susceptibility, remanence]
    operands += [jnp.asarray(tables[n]) for n in TABLES]
    operands = [pltpu.with_memory_space_constraint(x, pltpu.HBM) for x in operands]
    results = pl.pallas_call(
        kernel,
        out_shape=(
            jax.ShapeDtypeStruct((3, 32, 16, 128), f32),
            jax.ShapeDtypeStruct((3, 32, 16, 128), f32),
            jax.ShapeDtypeStruct((32, 16, 128), f32),
        ),
        in_specs=[hbm] * (4 + len(TABLES)) + [smem] * 2,
        out_specs=(vmem, vmem, vmem),
        scratch_shapes=[pltpu.VMEM(s, f32) for s in shapes]
        + [pltpu.SemaphoreType.DMA(s) for s in sems]
        + held
        + [pltpu.SemaphoreType.DMA((12,))],
        compiler_params=pltpu.CompilerParams(
            collective_id=0, has_side_effects=True, vmem_limit_bytes=VMEM_GRANT
        ),
    )(*operands, region_bounds, step_id)
    anywhere = pl.BlockSpec(memory_space=pl.ANY)
    return pl.pallas_call(
        put_out,
        out_shape=[jax.ShapeDtypeStruct(r.shape, f32) for r in results],
        in_specs=[anywhere] * 3,
        out_specs=[hbm] * 3,
        scratch_shapes=[pltpu.SemaphoreType.DMA((3,))],
        compiler_params=pltpu.CompilerParams(vmem_limit_bytes=1 << 20),
    )(*results)


def solution(mesh):
    return jax.shard_map(
        on_device,
        mesh=mesh,
        in_specs=(
            P(None, "gx", "gy", "gz"),
            P(None, "gx", "gy", "gz"),
            P("gx", "gy", "gz"),
            P("gx", "gy", "gz"),
            P(),
            P(),
        ),
        out_specs=(P(None, "gx", "gy", "gz"), P(None, "gx", "gy", "gz"), P("gx", "gy", "gz")),
        check_vma=False,
    )
```

```python
import jax
import jax.numpy as jnp
import numpy as np
from jax import lax
from jax.experimental import pallas as pl
from jax.experimental.pallas import tpu as pltpu
from jax.sharding import PartitionSpec as P

time_step = 0.5
viscosity = 0.2
field_period = 24
full_turn = 6.283185307179586

bf16 = jnp.bfloat16
f32 = jnp.float32
MESH = pl.DeviceIdType.MESH


def pieces(matrix):
    matrix = np.asarray(matrix, np.float32)
    high = matrix.astype(jnp.bfloat16)
    low = (matrix - high.astype(np.float32)).astype(jnp.bfloat16)
    return np.stack([high, low])


def cut(value):
    high = value.astype(bf16)
    return high, (value - high.astype(f32)).astype(bf16)


def dot(left, right, dims=(((1,), (0,)), ((), ()))):
    return lax.dot_general(left, right, dims, preferred_element_type=f32)


def mul(matrix, value):
    high, low = cut(value)
    rows = matrix.shape[1]
    both = dot(matrix[...].reshape(2 * rows, matrix.shape[2]), high)
    return both[:rows] + both[rows:] + dot(matrix[0], low)


def make_tables():
    turn = 2.0 * np.pi / 256
    eye4, eye16 = np.eye(4), np.eye(16)
    c, s, j = np.arange(2)[:, None, None], np.arange(16)[:, None], np.arange(4)
    k3 = 1 + 8 * s + 4 * c + j
    z = np.arange(256)
    phase = turn * k3[..., None] * z
    forward_z = np.stack([np.cos(phase), -np.sin(phase)], 2).reshape(256, 256)
    weight = np.where(k3 == 128, 1.0, 2.0)[..., None] / 256.0**3
    both = np.stack([np.cos(phase) * weight, -np.sin(phase) * weight], 2)
    inverse_z = both.reshape(256, 256).T
    q, t, ka = np.arange(8), np.arange(2), np.arange(16)
    theta = turn * 16 * (2 * q[:, None, None] + t[None, :, None]) * ka
    c, s = np.cos(theta), np.sin(theta)
    turned = np.stack([np.stack([c, s]), np.stack([-s, c])])
    forward_x = np.einsum("abqtk,ji->akiqtbj", turned, eye4).reshape(128, 128)
    lower_x = np.einsum("abqtk,ji->akitqbj", turned[:, :, :4], eye4).reshape(128, 64)
    back = np.stack([np.stack([c, -s]), np.stack([s, c])])
    inverse_x = np.einsum("abqtk,ij->qtaibkj", back, eye4).reshape(128, 128)
    b = np.arange(16)
    phi = turn * ka[:, None] * b
    twiddle = np.stack([np.cos(phi), np.sin(phi)])[:, :, None, :, None]
    twiddle = np.broadcast_to(twiddle, (2, 16, 4, 16, 16)).reshape(2, 64, 256)
    angle = turn * 16 * b[:, None] * b
    kron = np.concatenate([np.kron(np.cos(angle), eye16), np.kron(np.sin(angle), eye16)], 1)
    k = np.arange(256)
    angle = turn * (k[:, None] * k % 256)
    return dict(
        forward_z=pieces(forward_z),
        inverse_z=pieces(inverse_z),
        forward_x=pieces(forward_x),
        lower_x=pieces(lower_x),
        inverse_x=pieces(inverse_x),
        twiddle=twiddle.astype(np.float32),
        kron=pieces(kron),
        second=np.stack([pieces(np.cos(angle)), pieces(np.sin(angle))]),
    )


def half_turned(value):
    return pltpu.roll(value, 64, 1)


def rotated(tables, value, direction):
    high, low = cut(value)
    rows, depth = tables.shape[2], tables.shape[3]
    both = dot(tables.reshape(4 * rows, depth), high)
    rest = dot(tables[:, 0].reshape(2 * rows, depth), low)
    first = both[:rows] + both[rows : 2 * rows] + rest[:rows]
    second = both[2 * rows : 3 * rows] + both[3 * rows :] + rest[rows:]
    lane = lax.broadcasted_iota(jnp.int32, (rows, 128), 1)
    sign = jnp.where(lane < 64, -direction, direction)
    blocks = [
        first[:, at : at + 128] + sign * half_turned(second[:, at : at + 128])
        for at in range(0, first.shape[1], 128)
    ]
    return blocks[0] if len(blocks) == 1 else jnp.concatenate(blocks, axis=1)


def depth_waves(block, forward_z):
    high, low = cut(block)
    dims = (((1,), (1,)), ((), ()))
    both = dot(forward_z.reshape(256, 128), high, dims)
    return both[:128] + both[128:] + dot(forward_z[0], low, dims)


def sixteenths(value, kron, direction):
    high, low = cut(value)
    both = dot(jnp.concatenate([high, low], axis=0), kron[0])
    both = both[:128] + both[128:] + dot(high, kron[1])
    first, second = both[:, :256], both[:, 256:]
    return jnp.concatenate(
        [first[:64] - direction * second[64:], first[64:] + direction * second[:64]], axis=0
    )


def first_forward(mixed, twiddle, kron):
    real, imag = mixed[:64], mixed[64:]
    c, s = twiddle[0], twiddle[1]
    turned = jnp.concatenate([real * c + imag * s, imag * c - real * s], axis=0)
    return sixteenths(turned, kron, -1.0).T


def first_inverse(value, twiddle, kron, inverse_x):
    turned = sixteenths(value.T, kron, 1.0)
    real, imag = turned[:64], turned[64:]
    c, s = twiddle[0], twiddle[1]
    turned = jnp.concatenate([real * c - imag * s, imag * c + real * s], axis=0)
    return mul(inverse_x, turned)


def halves_on_rows(block):
    return jnp.concatenate([block[:, :256], block[:, 256:]], axis=0)


def signed_wave(index):
    folded = jnp.where(index < 128, index, index - 256)
    return jnp.where(index == 128, 0, folded).astype(f32) * (full_turn / 256)


def factor_of(index, third):
    half = full_turn / 2
    return jnp.where(third == 128, jnp.where(index == 128, half, 0.0), signed_wave(index))


def wave_numbers(place, chunk):
    row = lax.broadcasted_iota(jnp.int32, (256, 128), 0)
    lane = lax.broadcasted_iota(jnp.int32, (256, 128), 1)
    return row, lane % 64 // 4, 1 + 8 * place + 4 * chunk + lane % 4


def spectral_factors(place, gy, chunk):
    row, low, third = wave_numbers(place, chunk)
    first = low + 16 * gy
    third_wave = third.astype(f32) * (full_turn / 256)
    fold = lambda i: jnp.where(i < 128, i, i - 256).astype(f32) * (full_turn / 256)
    first_wave, second_wave = fold(first), fold(row)
    square = first_wave * first_wave + second_wave * second_wave + third_wave * third_wave
    return -third_wave / square, factor_of(row, third)


def mixing_factors(place, chunk):
    row, low, third = wave_numbers(place, chunk)
    return factor_of(low + 16 * (row // 16), third), third.astype(f32) * (full_turn / 256)


UNROLL = 5
DEPTH = 3


class Place:
    def __init__(self):
        self.gx, self.gy, self.gz = (lax.axis_index(a) for a in ("gx", "gy", "gz"))
        self.wave = self.gx * 2 + self.gz

    def by_wave(self, wave):
        return (lax.div(wave, 2), self.gy, lax.rem(wave, 2))

    def by_second(self, second):
        return (self.gx, second, self.gz)

    def announce(self):
        barrier = pltpu.get_barrier_semaphore()

        def signal(step, carry):
            for target in (
                self.by_wave(lax.rem(self.wave + step, 16)),
                self.by_second(lax.rem(self.gy + step, 16)),
            ):
                pl.semaphore_signal(barrier, inc=1, device_id=target, device_id_type=MESH)
            return carry

        lax.fori_loop(1, 16, signal, 0, unroll=UNROLL)

    def meet(self):
        pl.semaphore_wait(pltpu.get_barrier_semaphore(), 30)


class Exchange:
    def __init__(self, me, device, src, dst, send_sem, recv_sem, wanted=None):
        self.me, self.device, self.src, self.dst = me, device, src, dst
        self.send_sem, self.recv_sem, self.wanted = send_sem, recv_sem, wanted

    def each(self, act):
        def body(step, carry):
            peer = lax.rem(self.me + step, 16)
            if self.wanted is None:
                act(peer)
            else:
                pl.when(self.wanted(peer))(lambda: act(peer))
            return carry

        lax.fori_loop(1, 16, body, 0, unroll=UNROLL)

    def copy(self, peer):
        return pltpu.make_async_remote_copy(
            src_ref=self.src(peer),
            dst_ref=self.dst,
            send_sem=self.send_sem(peer),
            recv_sem=self.recv_sem,
            device_id=self.device(peer),
            device_id_type=MESH,
        )

    def start(self, after=None):
        def act(peer):
            if after is not None:
                after.copy(peer).wait_send()
            self.copy(peer).start()

        own = pltpu.make_async_copy(self.src(self.me), self.dst, self.recv_sem)
        if self.wanted is None:
            own.start()
        else:
            pl.when(self.wanted(self.me))(lambda: own.start())
        self.each(act)

    def finish(self):
        self.each(lambda peer: self.copy(peer).wait_send())


class Chain:
    def __init__(self, exchanges):
        self.exchanges, self.count = exchanges, 0

    def start(self, number):
        before = self.exchanges[number - DEPTH] if number >= DEPTH else None
        assert number == self.count
        self.exchanges[number].start(before)
        self.count += 1

    def finish(self):
        for exchange in self.exchanges[-DEPTH:]:
            exchange.finish()


def arrived(buffer, sem):
    pltpu.make_async_copy(buffer, buffer, sem).wait()


def region(at, bounds):
    row = lax.broadcasted_iota(jnp.int32, (512, 128), 0)
    third = lax.broadcasted_iota(jnp.int32, (512, 128), 1) + at.gz * 128
    first, second = row // 16 + at.gx * 32, row % 16 + at.gy * 16
    inside = (first >= bounds[0, 0]) & (first < bounds[1, 0])
    inside = inside & (second >= bounds[0, 1]) & (second < bounds[1, 1])
    inside = inside & (third >= bounds[0, 2]) & (third < bounds[1, 2])
    return jnp.where(inside, 1.0, 0.0)


class Halo:
    def __init__(self, at, block, second_out, second_in, third_out, third_in, sent, got):
        self.at, self.block = at, block
        self.second_out, self.second_in = second_out, second_in
        self.third_out, self.third_in = third_out, third_in
        gx, gy, gz = at.gx, at.gy, at.gz
        self.copies = []
        for number, (src, dst, there, here, target) in enumerate(
            (
                (block.at[:, 32], block.at[:, 0], gx < 7, gx > 0, ((gx + 1) % 8, gy, gz)),
                (block.at[:, 1], block.at[:, 33], gx > 0, gx < 7, ((gx + 7) % 8, gy, gz)),
                (second_out.at[1], second_in.at[0], gy < 15, gy > 0, (gx, (gy + 1) % 16, gz)),
                (second_out.at[0], second_in.at[1], gy > 0, gy < 15, (gx, (gy + 15) % 16, gz)),
                (third_out, third_in, None, None, (gx, gy, 1 - gz)),
            )
        ):
            copy = pltpu.make_async_remote_copy(
                src_ref=src,
                dst_ref=dst,
                send_sem=sent.at[number],
                recv_sem=got.at[number],
                device_id=target,
                device_id_type=MESH,
            )
            self.copies.append((copy, there, here, dst))

    def start(self):
        block = self.block
        for face, row in ((0, 0), (1, 15)):
            self.second_out[face] = block[:, 1:33, row, :]
        for f in range(block.shape[0]):
            cells = block[f, 1:33].reshape(512, 128).T
            row = jnp.where(self.at.gz == 0, cells[127:128], cells[0:1])
            self.third_out[f : f + 1] = row
        for copy, there, here, dst in self.copies:
            if there is None:
                copy.start()
            else:
                pl.when(there)(lambda copy=copy: copy.start())

    def arrive(self, wide):
        for copy, there, here, dst in self.copies:
            if here is None:
                copy.wait_recv()
            else:
                pl.when(here)(lambda copy=copy: copy.wait_recv())

                @pl.when(jnp.logical_not(here))
                def _(dst=dst):
                    dst[...] = jnp.zeros(dst.shape, f32)

        for f in range(self.block.shape[0]):
            row = jnp.broadcast_to(self.third_in[f : f + 1], (128, 512))
            wide[f] = row.T.reshape(32, 16, 128)

    def finish(self):
        for copy, there, here, dst in self.copies:
            if there is None:
                copy.wait_send()
            else:
                pl.when(there)(lambda copy=copy: copy.wait_send())


def neighbours(at, halo, wide, f, i):
    block = halo.block
    here = block[f, i + 1]
    row = lax.broadcasted_iota(jnp.int32, (16, 128), 0)
    lane = lax.broadcasted_iota(jnp.int32, (16, 128), 1)
    below = halo.second_in[0, f, pl.ds(i, 1)]
    above = halo.second_in[1, f, pl.ds(i, 1)]
    side = wide[f, i]
    second = (
        jnp.where(row == 0, below, pltpu.roll(here, 1, 0)),
        jnp.where(row == 15, above, pltpu.roll(here, 15, 0)),
    )
    third = (
        jnp.where(lane == 0, jnp.where(at.gz == 1, side, 0.0), pltpu.roll(here, 1, 1)),
        jnp.where(lane == 127, jnp.where(at.gz == 0, side, 0.0), pltpu.roll(here, 127, 1)),
    )
    return here, ((block[f, i], block[f, i + 2]), second, third)


def laplace(here, around):
    total = -6.0 * here
    for low, high in around:
        total = total + (low + high)
    return total


def slope(pair):
    return (pair[1] - pair[0]) * 0.5


def cell_rows(at, halo, wide, next_out, adjoint_out, source):
    def body(i, carry):
        cells = [neighbours(at, halo, wide, f, i) for f in range(7)]
        velocity, seed = cells[:3], cells[3:6]
        suscept = cells[6]
        total = 0.0
        for d in range(3):
            pair = [suscept[1][d][e] * seed[d][1][d][e] for e in range(2)]
            total = total + slope(pair)
        source[i] = -time_step * total
        for k in range(3):
            here, around = velocity[k]
            advect = sum(velocity[j][0] * slope(around[j]) for j in range(3))
            next_out[k, i] = here + time_step * (viscosity * laplace(here, around) - advect)
            here, around = seed[k]
            shear = sum(seed[j][0] * slope(velocity[j][1][k]) for j in range(3))
            carried = sum(
                slope([velocity[j][1][j][e] * around[j][e] for e in range(2)]) for j in range(3)
            )
            adjoint_out[k, i] = here + time_step * (
                viscosity * laplace(here, around) - shear + carried
            )
        return carry

    lax.fori_loop(0, 32, body, 0)


def energy_rows(at, halo, wide, cells, next_out):
    def body(i, carry):
        _, around = neighbours(at, halo, wide, 0, i)
        scaled = time_step * cells[6, i + 1]
        for k in range(3):
            next_out[k, i] = next_out[k, i] + scaled * slope(around[k])
        return carry

    lax.fori_loop(0, 32, body, 0)


ORDER = (0, 2, 1)
CHUNKS = ((0,), (1,))
SECONDS = ((0, 0), (0, 1), (1, 0), (1, 1))
LASTS = ((0, 0), (2, 0), (0, 1), (2, 1), (1, 0), (1, 1))
BACK = ((0, 0), (0, 1), (2, 0), (2, 1), (1, 0), (1, 1))


def kernel(
    velocity, adjoint_seed, suscept, remanence_in,
    forward_z_in, inverse_z_in, forward_x_in, lower_x_in, inverse_x_in, twiddle_in, kron_in,
    second_in, bounds, step,
    next_out, adjoint_out, gradient_out,
    z_out, z_in, k_out, k_in, y_out, y_in, x_out, x_in,
    zb_out, zb_in, kb_out, kb_in, yb_out, yb_in, xb_out, xb_in,
    cells, cells_y_out, cells_y_in, cells_z_out, cells_z_in, cells_wide,
    energy, energy_y_out, energy_y_in, energy_z_out, energy_z_in, energy_wide, source,
    source_in, energy_out,
    z_sent, z_got, k_sent, k_got, y_sent, y_got, x_sent, x_got,
    zb_sent, zb_got, kb_sent, kb_got, yb_sent, yb_got, xb_sent, xb_got,
    cells_sent, cells_got, energy_sent, energy_got, swap_sent, swap_got,
    remanence, forward_z, inverse_z, forward_x, lower_x, inverse_x, twiddle, kron, second, loaded,
):
    at = Place()
    at.announce()
    loads = {}
    for number, (name, src, dst) in enumerate(
        (
            ("remanence", remanence_in, remanence),
            ("forward_z", forward_z_in, forward_z),
            ("velocity", velocity, cells.at[0:3, 1:33]),
            ("seed", adjoint_seed, cells.at[3:6, 1:33]),
            ("suscept", suscept, cells.at[6, 1:33]),
            ("lower_x", lower_x_in, lower_x),
            ("twiddle", twiddle_in, twiddle),
            ("kron", kron_in, kron),
            ("second", second_in, second),
            ("inverse_x", inverse_x_in, inverse_x),
            ("inverse_z", inverse_z_in, inverse_z),
            ("forward_x", forward_x_in, forward_x),
        )
    ):
        loads[name] = pltpu.make_async_copy(src, dst, loaded.at[number])
        loads[name].start()
    in_lower = (at.gx < 4) & (at.gy < 8) & (at.gz == 0)
    has_rows = at.gy < 8

    def over_waves(order, out, into, sent, got, block=lambda p: p, slot=None, wanted=None):
        slot = at.wave if slot is None else slot
        return Chain(
            [
                Exchange(
                    at.wave, at.by_wave, lambda p, k=k: out.at[*k, block(p)], into.at[*k, slot],
                    lambda p, n=n: sent.at[n, p], got.at[n], wanted,
                )
                for n, k in enumerate(order)
            ]
        )

    def over_seconds(order, out, into, sent, got, block=lambda p: p, slot=None, wanted=None):
        slot = at.gy if slot is None else slot
        return Chain(
            [
                Exchange(
                    at.gy, at.by_second, lambda p, k=k: out.at[*k, block(p)], into.at[*k, slot],
                    lambda p, n=n: sent.at[n, p], got.at[n], wanted,
                )
                for n, k in enumerate(order)
            ]
        )

    depths = over_waves(CHUNKS, z_out, z_in, z_sent, z_got, slot=lax.rem(at.gx, 4))
    firsts = over_seconds(CHUNKS, k_out, k_in, k_sent, k_got, slot=lax.rem(at.gy, 8))
    seconds = over_seconds(SECONDS, y_out, y_in, y_sent, y_got)
    lasts = over_waves(LASTS, x_out, x_in, x_sent, x_got)
    depths_back = over_waves(BACK, zb_out, zb_in, zb_sent, zb_got)
    firsts_back = over_seconds(SECONDS, kb_out, kb_in, kb_sent, kb_got)
    seconds_back = over_seconds(
        CHUNKS, yb_out, yb_in, yb_sent, yb_got, lambda p: lax.rem(p, 8), None, lambda p: p < 8
    )
    lasts_back = over_waves(
        CHUNKS, xb_out, xb_in, xb_sent, xb_got, lambda p: lax.rem(lax.div(p, 2), 4), None,
        lambda p: (p < 8) & (lax.rem(p, 2) == 0),
    )
    cell_halo = Halo(
        at, cells, cells_y_out, cells_y_in, cells_z_out, cells_z_in, cells_sent, cells_got
    )
    energy_halo = Halo(
        at, energy, energy_y_out, energy_y_in, energy_z_out, energy_z_in, energy_sent, energy_got
    )

    loads["remanence"].wait()
    loads["forward_z"].wait()

    @pl.when(in_lower)
    def _():
        magnet = remanence[...].reshape(512, 128) * region(at, bounds)
        remanence[...] = magnet.reshape(32, 16, 128)
        z_out[0] = depth_waves(magnet, forward_z[:, :128, :128]).reshape(16, 8, 512)

    at.meet()

    @pl.when(in_lower)
    def _():
        depths.start(0)
        magnet = remanence[...].reshape(512, 128)
        z_out[1] = depth_waves(magnet, forward_z[:, 128:, :128]).reshape(16, 8, 512)
        depths.start(1)

    for name in ("velocity", "seed", "suscept"):
        loads[name].wait()
    cell_halo.start()
    for name in ("lower_x", "twiddle", "kron"):
        loads[name].wait()

    @pl.when(has_rows)
    def _():
        for c in range(2):
            arrived(z_in.at[c], z_got.at[c])
            block = mul(lower_x, halves_on_rows(z_in[c].reshape(32, 512)))
            k_out[c] = first_forward(block, twiddle, kron).reshape(16, 16, 128)
            firsts.start(c)

    cell_halo.arrive(cells_wide)
    cell_rows(at, cell_halo, cells_wide, next_out, adjoint_out, source)
    here, there = at.gz * 16, (1 - at.gz) * 16
    source_swap = pltpu.make_async_remote_copy(
        src_ref=source.at[pl.ds(there, 16)],
        dst_ref=source_in,
        send_sem=swap_sent.at[0],
        recv_sem=swap_got.at[0],
        device_id=(at.gx, at.gy, 1 - at.gz),
        device_id_type=MESH,
    )
    energy_swap = pltpu.make_async_remote_copy(
        src_ref=energy_out,
        dst_ref=energy.at[0, pl.ds(1 + here, 16)],
        send_sem=swap_sent.at[1],
        recv_sem=swap_got.at[1],
        device_id=(at.gx, at.gy, 1 - at.gz),
        device_id_type=MESH,
    )
    source_swap.start()

    loads["second"].wait()
    factors = [spectral_factors(at.wave, at.gy, c) for c in range(2)]
    for c in range(2):
        potential, second_factor = factors[c]
        arrived(k_in.at[c], k_got.at[c])
        value = k_in[c].reshape(128, 128)
        value = rotated(second[:, :, :, :128], value, -1.0) * potential
        value = jnp.concatenate([value, value * second_factor], axis=1)
        value = rotated(second[...], value, 1.0)
        y_out[0, c] = value[:, :128].reshape(16, 16, 128)
        y_out[1, c] = value[:, 128:].reshape(16, 16, 128)
        seconds.start(c)
    seconds.start(2)
    seconds.start(3)

    loads["inverse_x"].wait()
    mixing = [mixing_factors(at.wave, c) for c in range(2)]

    def send_first(f, c, value):
        value = first_inverse(value, twiddle, kron, inverse_x)
        x_out[f, c] = value.reshape(16, 8, 256)
        lasts.start(LASTS.index((f, c)))

    for c in range(2):
        arrived(y_in.at[0, c], y_got.at[c])
        value = y_in[0, c].reshape(256, 128)
        send_first(0, c, value * mixing[c][0])
        send_first(2, c, value * mixing[c][1])
    for c in range(2):
        arrived(y_in.at[1, c], y_got.at[2 + c])
        send_first(1, c, y_in[1, c].reshape(256, 128))

    loads["inverse_z"].wait()
    turned = jnp.full((8, 256), step[0] % field_period, jnp.int32).astype(f32)
    turned = full_turn * turned / field_period
    applied = (jnp.cos(turned)[:1], jnp.sin(turned)[:1], None)
    square = jnp.zeros((256, 256), f32)
    source_swap.wait_recv()
    mine = source[pl.ds(here, 16)].reshape(256, 128).T
    theirs = source_in[...].reshape(256, 128).T
    weight = jnp.concatenate(
        [jnp.where(at.gz == 0, mine, theirs), jnp.where(at.gz == 0, theirs, mine)], axis=0
    )
    for f in ORDER:
        for c in range(2):
            arrived(x_in.at[f, c], x_got.at[LASTS.index((f, c))])
        field = mul(inverse_z, x_in[f].reshape(256, 256))
        if applied[f] is not None:
            field = field + applied[f]
        square = square + field * field
        zb_out[f] = mul(forward_z, weight * field).reshape(2, 16, 8, 256)
        for c in range(2):
            depths_back.start(BACK.index((f, c)))
    low, high = 0.5 * square[:128].T, 0.5 * square[128:].T
    mine, theirs = jnp.where(at.gz == 0, low, high), jnp.where(at.gz == 0, high, low)
    energy[0, pl.ds(1 + here, 16)] = mine.reshape(16, 16, 128)
    energy_out[...] = theirs.reshape(16, 16, 128)
    energy_swap.start()

    loads["forward_x"].wait()

    def first_of(f, c):
        arrived(zb_in.at[f, c], zb_got.at[BACK.index((f, c))])
        block = mul(forward_x, zb_in[f, c].reshape(128, 256))
        return first_forward(block, twiddle, kron)

    for c in range(2):
        value = first_of(0, c) * mixing[c][0] + first_of(2, c) * mixing[c][1]
        kb_out[0, c] = value.reshape(16, 16, 128)
        firsts_back.start(c)
    for c in range(2):
        kb_out[1, c] = first_of(1, c).reshape(16, 16, 128)
        firsts_back.start(2 + c)

    energy_swap.wait_recv()
    energy_halo.start()
    pl.when(in_lower)(lambda: depths.finish())
    pl.when(has_rows)(lambda: firsts.finish())
    for each in (seconds, lasts, depths_back, cell_halo):
        each.finish()
    source_swap.wait_send()
    energy_swap.wait_send()

    for c in range(2):
        potential, second_factor = factors[c]
        for f in range(2):
            arrived(kb_in.at[f, c], kb_got.at[2 * f + c])
        value = [kb_in[f, c].reshape(256, 128) for f in range(2)]
        value = rotated(second[...], jnp.concatenate(value, axis=1), -1.0)
        value = (value[:, :128] + value[:, 128:] * second_factor) * potential
        value = rotated(second[:, :, :128], value, 1.0)
        yb_out[c] = value.reshape(8, 16, 128)
        seconds_back.start(c)
    firsts_back.finish()
    gradient_out[...] = jnp.zeros((32, 16, 128), f32)

    @pl.when(has_rows)
    def _():
        for c in range(2):
            arrived(yb_in.at[c], yb_got.at[c])
            value = yb_in[c].reshape(256, 128)
            value = first_inverse(value, twiddle, kron, inverse_x[:, :64]).reshape(4, 2, 8, 256)
            xb_out[c, :, :, :256] = value[:, 0]
            xb_out[c, :, :, 256:] = value[:, 1]
            lasts_back.start(c)

    energy_halo.arrive(energy_wide)
    energy_rows(at, energy_halo, energy_wide, cells, next_out)
    energy_halo.finish()
    seconds_back.finish()
    pl.when(has_rows)(lambda: lasts_back.finish())

    @pl.when(in_lower)
    def _():
        inside = region(at, bounds)
        value = 0.0
        for c in range(2):
            arrived(xb_in.at[c], xb_got.at[c])
            table = inverse_z[:, :128, 128 * c : 128 * (c + 1)]
            value = value + mul(table, xb_in[c].reshape(128, 512))
        gradient_out[...] = (value.T * inside).reshape(32, 16, 128)


VMEM_GRANT = 24 << 20
TABLES = (
    "forward_z", "inverse_z", "forward_x", "lower_x", "inverse_x", "twiddle",
    "kron", "second",
)


def put_out(a_in, b_in, c_in, a_out, b_out, c_out, sems):
    pairs = ((a_in, a_out), (b_in, b_out), (c_in, c_out))
    copies = [pltpu.make_async_copy(*pair, sems.at[n]) for n, pair in enumerate(pairs)]
    for copy in copies:
        copy.start()
    for copy in copies:
        copy.wait()


def on_device(velocity, adjoint_seed, susceptibility, remanence, region_bounds, step_id):
    tables = make_tables()
    shapes = [(2, 16, 8, 512), (2, 4, 8, 512), (2, 16, 16, 128), (2, 8, 16, 128)]
    shapes += [(2, 2, 16, 16, 128)] * 2 + [(3, 2, 16, 8, 256)] * 2
    shapes += [(3, 2, 16, 8, 256)] * 2 + [(2, 2, 16, 16, 128)] * 2
    shapes += [(2, 8, 16, 128), (2, 16, 16, 128), (2, 4, 8, 512), (2, 16, 8, 512)]
    for n in (7, 1):
        shapes += [(n, 34, 16, 128), (2, n, 32, 128), (2, n, 32, 128), (8, 512), (8, 512)]
        shapes += [(n, 32, 16, 128)]
    shapes += [(32, 16, 128)] + [(16, 16, 128)] * 2
    sems = []
    for n in (2, 2, 4, 6, 6, 4, 2, 2):
        sems += [(n, 16), (n,)]
    sems += [(5,)] * 4 + [(2,)] * 2
    vmem = pl.BlockSpec(memory_space=pltpu.VMEM)
    smem = pl.BlockSpec(memory_space=pltpu.SMEM)
    hbm = pl.BlockSpec(memory_space=pltpu.HBM)
    held = [pltpu.VMEM((32, 16, 128), f32)]
    held += [pltpu.VMEM(tables[n].shape, tables[n].dtype) for n in TABLES]
    operands = [velocity, adjoint_seed, susceptibility, remanence]
    operands += [jnp.asarray(tables[n]) for n in TABLES]
    operands = [pltpu.with_memory_space_constraint(x, pltpu.HBM) for x in operands]
    results = pl.pallas_call(
        kernel,
        out_shape=(
            jax.ShapeDtypeStruct((3, 32, 16, 128), f32),
            jax.ShapeDtypeStruct((3, 32, 16, 128), f32),
            jax.ShapeDtypeStruct((32, 16, 128), f32),
        ),
        in_specs=[hbm] * (4 + len(TABLES)) + [smem] * 2,
        out_specs=(vmem, vmem, vmem),
        scratch_shapes=[pltpu.VMEM(s, f32) for s in shapes]
        + [pltpu.SemaphoreType.DMA(s) for s in sems]
        + held
        + [pltpu.SemaphoreType.DMA((12,))],
        compiler_params=pltpu.CompilerParams(
            collective_id=0, has_side_effects=True, vmem_limit_bytes=VMEM_GRANT
        ),
    )(*operands, region_bounds, step_id)
    anywhere = pl.BlockSpec(memory_space=pl.ANY)
    return pl.pallas_call(
        put_out,
        out_shape=[jax.ShapeDtypeStruct(r.shape, f32) for r in results],
        in_specs=[anywhere] * 3,
        out_specs=[hbm] * 3,
        scratch_shapes=[pltpu.SemaphoreType.DMA((3,))],
        compiler_params=pltpu.CompilerParams(vmem_limit_bytes=1 << 20),
    )(*results)


def solution(mesh):
    return jax.shard_map(
        on_device,
        mesh=mesh,
        in_specs=(
            P(None, "gx", "gy", "gz"),
            P(None, "gx", "gy", "gz"),
            P("gx", "gy", "gz"),
            P("gx", "gy", "gz"),
            P(),
            P(),
        ),
        out_specs=(P(None, "gx", "gy", "gz"), P(None, "gx", "gy", "gz"), P("gx", "gy", "gz")),
        check_vma=False,
    )
```
